32 devices in a mesh: seq: 8 (over z, x), tp: 4 (over y, core).
Axes of the slice: x: 2, y: 2, z: 4, core: 2. Of those that a mesh axis runs over, the one named last changes fastest.
Arguments:
- inputs: bfloat16 [1024, 4, 2048], P(('seq', 'tp')), may hold values from -6 to 6
- documents: int32 [4, 1024], replicated, may hold values from 0 to 3, as said below
- query_weight: bfloat16 [2048, 2048], P(None, 'tp'), may hold values from -0.125 to 0.125
- key_weight: bfloat16 [2048, 2048], P(None, 'tp'), may hold values from -0.125 to 0.125
- value_weight: bfloat16 [2048, 2048], P(None, 'tp'), may hold values from -0.125 to 0.125
- output_weight: bfloat16 [2048, 2048], P('tp'), may hold values from -0.125 to 0.125
- query_gain: float32 [2048], P('tp'), may hold values from 0.25 to 1.75
- key_gain: float32 [2048], P('tp'), may hold values from 0.25 to 1.75
- attention_gain: float32 [2048], replicated, may hold values from 0.5 to 1.5
- gate_weight: bfloat16 [2048, 8192], P(None, 'tp'), may hold values from -0.125 to 0.125
- up_weight: bfloat16 [2048, 8192], P(None, 'tp'), may hold values from -0.125 to 0.125
- down_weight: bfloat16 [8192, 2048], P('tp'), may hold values from -0.0625 to 0.0625
- feed_gain: float32 [2048], replicated, may hold values from 0.5 to 1.5
- cotangent: bfloat16 [1024, 4, 2048], P(('seq', 'tp')), may hold values from -6 to 6
Outputs:
- layer_out: float32 [1024, 4, 2048], P(('seq', 'tp'))
- input_grad: float32 [1024, 4, 2048], P(('seq', 'tp'))
- grad_query: float32 [2048, 2048], P('seq', 'tp')
- grad_key: float32 [2048, 2048], P('seq', 'tp')
- grad_value: float32 [2048, 2048], P('seq', 'tp')
- grad_output: float32 [2048, 2048], P('tp', 'seq')
- grad_gate: float32 [2048, 8192], P('seq', 'tp')
- grad_up: float32 [2048, 8192], P('seq', 'tp')
- grad_down: float32 [8192, 2048], P('tp', 'seq')
- grad_query_gain: float32 [2048], P('seq')
- grad_key_gain: float32 [2048], P('seq')
- grad_attention_gain: float32 [2048], P('seq')
- grad_feed_gain: float32 [2048], P('seq')
The draws below stay inside these ranges and needn't reach their ends.
Inputs may be any that keep to these rules, and one draw needn't show every extreme that they name: In each sequence the ids never fall and each of its documents covers consecutive tokens; one sequence, which one drawn from the seed, is a single document of all 1024 tokens.
All inputs are finite; a program needn't handle non-finite values.
Results may differ from the reference program's by a relative error of at most 0.025.
Values may be sent and summed in bfloat16 or wider, within the bound.
No kernel may reach another device: no remote copies, remote signals or barrier semaphores. Data moves between devices by JAX's collectives and lax.ppermute only.
A program may use at most 320 MiB of HBM per device.

```python
import jax
import jax.numpy as jnp
from jax import lax

D = 2048
HEADS = 16
HEAD = 128
FF = 8192
SEQS = 4
DOCS = 4
LENGTH = 1024


def draw_documents(key, part):
    chosen = jax.random.randint(jax.random.fold_in(key, 1), (), 0, SEQS)
    row_keys = jax.random.split(jax.random.fold_in(key, 2), SEQS)

    def cuts_of(row_key):
        return jax.random.permutation(row_key, LENGTH - 1)[:DOCS - 1] + 1
    cuts = jax.vmap(cuts_of)(row_keys).astype(jnp.int32)
    places = jnp.arange(LENGTH, dtype=jnp.int32)
    ids = jnp.sum((places[None, :, None] >= cuts[:, None, :]).astype(jnp.int32), axis=-1)
    rows = jnp.arange(SEQS, dtype=jnp.int32)[:, None]
    return jnp.where(rows == chosen, 0, ids).astype(jnp.int32)


def block_levels(rng, extent, cuts, smallest, largest):
    level = 1.0
    for position, parts in cuts:
        steps = jax.random.uniform(jax.random.fold_in(jax.random.fold_in(rng, 6), position), (parts,), jnp.float32, smallest / len(cuts), largest / len(cuts))
        level = level * jnp.repeat(jnp.exp(steps), extent[position] // parts).reshape((-1,) + (1,) * (len(extent) - 1 - position))
    return level


def gaussian(own_key, shape, spread, bound, cuts=(), kind=jnp.bfloat16):
    values = spread * jax.random.normal(own_key, shape, jnp.float32)
    if cuts:
        values = values * block_levels(own_key, shape, cuts, -0.22, 0.18)
    return jnp.clip(values, -bound, bound).astype(kind)


def setup_inputs(seed: int = 0) -> dict:
    keys = jax.random.split(jax.random.key(seed), 15)
    inputs = gaussian(keys[0], (LENGTH, SEQS, D), 1.0, 6.0, ((0, 32),))
    documents = draw_documents(jax.random.fold_in(keys[14], 71), 0)
    query_weight = gaussian(keys[2], (D, D), D ** -0.5, 0.125, ((1, 4),))
    key_weight = gaussian(keys[3], (D, D), D ** -0.5, 0.125, ((1, 4),))
    value_weight = gaussian(keys[4], (D, D), D ** -0.5, 0.125, ((1, 4),))
    output_weight = gaussian(keys[5], (D, D), D ** -0.5, 0.125, ((0, 4),))
    query_gain = jnp.clip(1.0 + 0.15 * jax.random.normal(keys[6], (D,), jnp.float32), 0.25, 1.75)
    key_gain = jnp.clip(1.0 + 0.15 * jax.random.normal(keys[7], (D,), jnp.float32), 0.25, 1.75)
    attention_gain = jnp.clip(1.0 + 0.1 * jax.random.normal(keys[8], (D,), jnp.float32), 0.5, 1.5)
    gate_weight = gaussian(keys[9], (D, FF), D ** -0.5, 0.125, ((1, 4),))
    up_weight = gaussian(keys[10], (D, FF), D ** -0.5, 0.125, ((1, 4),))
    down_weight = gaussian(keys[11], (FF, D), FF ** -0.5, 0.0625, ((0, 4),))
    feed_gain = jnp.clip(1.0 + 0.1 * jax.random.normal(keys[12], (D,), jnp.float32), 0.5, 1.5)
    cotangent = gaussian(keys[13], (LENGTH, SEQS, D), 1.0, 6.0, ((0, 32),))
    return dict(inputs=inputs, documents=documents, query_weight=query_weight, key_weight=key_weight, value_weight=value_weight, output_weight=output_weight, query_gain=query_gain, key_gain=key_gain, attention_gain=attention_gain, gate_weight=gate_weight, up_weight=up_weight, down_weight=down_weight, feed_gain=feed_gain, cotangent=cotangent)


EPS = 1e-06
THETA = 500000.0
NEGATIVE = -1e+30

@jax.custom_vjp
def low(v):
    return lax.optimization_barrier(v.astype(jnp.bfloat16)).astype(jnp.float32)

@jax.custom_vjp
def low_back(v):
    return v

def low_keep(v):
    return (low(v), None)

def low_pass(kept, grad):
    return (grad,)

def back_keep(v):
    return (v, None)

def back_low(kept, grad):
    return (low(grad),)
low.defvjp(low_keep, low_pass)
low_back.defvjp(back_keep, back_low)

def matmul(left_side, right_side):
    return jnp.dot(left_side, right_side, precision=lax.Precision.HIGHEST, preferred_element_type=jnp.float32)

def rms_norm(tensor, gain):
    return tensor * lax.rsqrt(lax.optimization_barrier(jnp.mean(tensor * tensor, axis=-1, keepdims=True)) + EPS) * gain

def rope_tables(positions, head_size):
    half_size = head_size // 2
    rates = jnp.exp(-jnp.log(THETA) * (2.0 * jnp.arange(half_size, dtype=jnp.float32) / head_size))
    angles = positions.astype(jnp.float32)[..., None] * rates
    cosine = jnp.cos(angles)
    sine_part = jnp.sin(angles)
    return (jnp.concatenate([cosine, cosine], axis=-1)[..., None, :], jnp.concatenate([sine_part, sine_part], axis=-1)[..., None, :])

def rotate(tensor, cosine, sine_part):
    half_size = tensor.shape[-1] // 2
    turned = jnp.concatenate([-tensor[..., half_size:], tensor[..., :half_size]], axis=-1)
    return tensor * cosine + turned * sine_part

def head_attend(pieces):
    queries, keys_in, values_in, doc_row = pieces
    scores = low_back(jnp.dot(queries, keys_in.T, precision=lax.Precision.HIGHEST)) * HEAD ** (-0.5)
    places = jnp.arange(doc_row.shape[0], dtype=jnp.int32)
    allowed = (doc_row[:, None] == doc_row[None, :]) & (places[None, :] <= places[:, None])
    scores = jnp.where(allowed, scores, NEGATIVE)
    weights = low(jax.nn.softmax(scores, axis=-1))
    return matmul(weights, values_in)

def attention(queries, keys_in, values_in, documents):
    length, seq_count = (queries.shape[0], queries.shape[1])

    def by_head(tensor):
        return jnp.transpose(tensor, (1, 2, 0, 3)).reshape(seq_count * HEADS, length, HEAD)
    doc_rows = jnp.broadcast_to(documents[:, None, :], (seq_count, HEADS, length)).reshape(seq_count * HEADS, length)
    mixed = lax.map(jax.checkpoint(head_attend), (by_head(queries), by_head(keys_in), by_head(values_in), doc_rows))
    mixed = jnp.transpose(mixed.reshape(seq_count, HEADS, length, HEAD), (2, 0, 1, 3))
    return mixed.reshape(length, seq_count, HEADS * HEAD)

def forward(inputs, query_weight, key_weight, value_weight, output_weight, query_gain, key_gain, attention_gain, gate_weight, up_weight, down_weight, feed_gain, documents, cosine, sine_part):
    length, seq_count = (inputs.shape[0], inputs.shape[1])

    def heads_of(tensor):
        return tensor.reshape(length, seq_count, HEADS, HEAD)
    queries = low_back(matmul(inputs, query_weight))
    keys_proj = low_back(matmul(inputs, key_weight))
    values_proj = low(low_back(matmul(inputs, value_weight)))
    queries = low(rotate(heads_of(rms_norm(queries, query_gain)), cosine, sine_part))
    keys_proj = low(rotate(heads_of(rms_norm(keys_proj, key_gain)), cosine, sine_part))
    mixed = attention(queries, keys_proj, heads_of(values_proj), documents)
    mixed = low(low_back(mixed))
    branch = low_back(matmul(mixed, output_weight))
    hidden = inputs + rms_norm(branch, attention_gain)
    normed = low(hidden)
    gate_value = low_back(matmul(normed, gate_weight))
    up_value = low_back(matmul(normed, up_weight))
    activated = low(jax.nn.silu(gate_value) * up_value)
    down_value = low_back(matmul(activated, down_weight))
    return hidden + rms_norm(down_value, feed_gain)

def reference(inputs, documents, query_weight, key_weight, value_weight, output_weight, query_gain, key_gain, attention_gain, gate_weight, up_weight, down_weight, feed_gain, cotangent):
    length = inputs.shape[0]
    starts = lax.optimization_barrier(jnp.sum((documents[:, None, :] < documents[:, :, None]).astype(jnp.int32), axis=-1))
    positions = (jnp.arange(length, dtype=jnp.int32)[None, :] - starts).T
    cosine, sine_part = rope_tables(positions, HEAD)
    floats = [tensor.astype(jnp.float32) for tensor in (inputs, query_weight, key_weight, value_weight, output_weight, query_gain, key_gain, attention_gain, gate_weight, up_weight, down_weight, feed_gain)]

    def layer(*params):
        return forward(*params, documents, cosine, sine_part)
    layer_out, pullback = jax.vjp(layer, *floats)
    grads = pullback(cotangent.astype(jnp.float32))
    return (layer_out, grads[0], grads[1], grads[2], grads[3], grads[4], grads[8], grads[9], grads[10], grads[5], grads[6], grads[7], grads[11])
```

```python
import jax
import jax.numpy as jnp
from jax import lax
from jax.sharding import PartitionSpec as P

HEAD = 128


EPS = 1e-06
THETA = 500000.0
NEGATIVE = -1e30


def rope_tables(positions, head_size):
    half_size = head_size // 2
    rates = jnp.exp(-jnp.log(THETA) * (2.0 * jnp.arange(half_size, dtype=jnp.float32) / head_size))
    angles = positions.astype(jnp.float32)[..., None] * rates
    cosine = jnp.cos(angles)
    sine_part = jnp.sin(angles)
    return (
        jnp.concatenate([cosine, cosine], axis=-1)[..., None, :],
        jnp.concatenate([sine_part, sine_part], axis=-1)[..., None, :],
    )


def rotate(tensor, cosine, sine_part):
    half_size = tensor.shape[-1] // 2
    turned = jnp.concatenate([-tensor[..., half_size:], tensor[..., :half_size]], axis=-1)
    return tensor * cosine + turned * sine_part


def unrotate(grad_in, cosine, sine_part):
    half_size = grad_in.shape[-1] // 2
    scaled = grad_in * sine_part
    return grad_in * cosine + jnp.concatenate(
        [scaled[..., half_size:], -scaled[..., :half_size]], axis=-1
    )


def rms_scale(tensor):
    return lax.rsqrt(jnp.mean(tensor * tensor, axis=-1, keepdims=True) + EPS)


def norm_back(tensor, inverse, gain, grad_in):
    weighted = grad_in * gain
    return inverse * weighted - tensor * inverse**3 * jnp.mean(
        weighted * tensor, axis=-1, keepdims=True
    )


def cycle_values(key_low, value_low):
    return (
        lax.all_gather(jnp.transpose(key_low, (1, 0, 2)), "seq", axis=1, tiled=True),
        lax.all_gather(jnp.transpose(value_low, (1, 0, 2)), "seq", axis=1, tiled=True),
    )


def allowed_mask(query_docs, key_docs, query_first, key_first):
    query_places = query_first + jnp.arange(query_docs.shape[0], dtype=jnp.int32)
    key_places = key_first + jnp.arange(key_docs.shape[0], dtype=jnp.int32)
    return (query_docs[:, None] == key_docs[None, :]) & (
        key_places[None, :] <= query_places[:, None]
    )


def local(
    inputs,
    documents,
    query_weight,
    key_weight,
    value_weight,
    output_weight,
    query_gain,
    key_gain,
    attention_gain,
    gate_weight,
    up_weight,
    down_weight,
    feed_gain,
    cotangent,
):
    row_count, seq_count, model_width = inputs.shape
    heads_width = query_weight.shape[1]
    local_heads = heads_width // HEAD
    score_scale = HEAD ** (-0.5)
    seq_index = lax.axis_index("seq")
    tp_index = lax.axis_index("tp")
    total_length = documents.shape[1]
    f32 = jnp.float32
    bf16 = jnp.bfloat16
    whole = lax.all_gather(inputs, "tp", axis=0, tiled=True)
    here_length = whole.shape[0]
    queries = jnp.einsum("tsd,dh->tsh", whole, query_weight, preferred_element_type=f32)
    keys_proj = jnp.einsum("tsd,dh->tsh", whole, key_weight, preferred_element_type=f32)
    values_proj = jnp.einsum("tsd,dh->tsh", whole, value_weight, preferred_element_type=f32)
    query_sq, key_sq = lax.psum(
        (jnp.sum(queries * queries, axis=-1), jnp.sum(keys_proj * keys_proj, axis=-1)), "tp"
    )
    query_inv = lax.rsqrt(query_sq / model_width + EPS)[..., None]
    key_inv = lax.rsqrt(key_sq / model_width + EPS)[..., None]
    first_row = seq_index * here_length
    own_docs = lax.dynamic_slice_in_dim(documents, first_row, here_length, 1)
    starts = jnp.sum((documents[:, None, :] < own_docs[:, :, None]).astype(jnp.int32), axis=-1)
    positions = (first_row + jnp.arange(here_length, dtype=jnp.int32))[:, None] - starts.T
    cosine, sine_part = rope_tables(positions, HEAD)

    def heads_of(tensor):
        return tensor.reshape(here_length, seq_count, local_heads, HEAD)

    query_low = rotate(heads_of(queries * query_inv * query_gain), cosine, sine_part).astype(bf16)
    key_low = rotate(heads_of(keys_proj * key_inv * key_gain), cosine, sine_part).astype(bf16)
    key_low = key_low.reshape(here_length, seq_count, heads_width)
    value_low = values_proj.astype(bf16)
    key_cycle, value_cycle = cycle_values(key_low, value_low)
    query_seq = jnp.transpose(query_low, (1, 0, 2, 3))

    def keys_in_reach(key_part, value_part):
        return (
            key_part.reshape(total_length, local_heads, HEAD),
            value_part.reshape(total_length, local_heads, HEAD),
        )

    def scores_of(query_part, key_heads, query_docs, key_docs, first_query, first_key):
        scores = (
            jnp.einsum("qhd,khd->hqk", query_part, key_heads, preferred_element_type=f32)
            * score_scale
        )
        return jnp.where(
            allowed_mask(query_docs, key_docs, first_query, first_key)[None], scores, NEGATIVE
        )

    def attend(pieces):
        query_part, key_part, value_part, own_part, doc_row = pieces
        key_heads, value_heads = keys_in_reach(key_part, value_part)
        scores = scores_of(query_part, key_heads, own_part, doc_row, first_row, 0)
        top_score = jnp.max(scores, axis=-1, keepdims=True)
        spread = jnp.exp(scores - top_score)
        total_sum = jnp.sum(spread, axis=-1, keepdims=True)
        weights = (spread / total_sum).astype(bf16)
        mixed_part = jnp.einsum("hqk,khd->qhd", weights, value_heads, preferred_element_type=f32)
        return (mixed_part, (top_score + jnp.log(total_sum))[..., 0])

    attended, log_total = lax.map(attend, (query_seq, key_cycle, value_cycle, own_docs, documents))
    mixed_low = (
        jnp.transpose(attended, (1, 0, 2, 3))
        .reshape(here_length, seq_count, heads_width)
        .astype(bf16)
    )
    part = mixed_low
    branch = lax.psum_scatter(
        jnp.einsum("tsh,hd->tsd", part, output_weight, preferred_element_type=f32).astype(
            jnp.bfloat16
        ),
        "tp",
        scatter_dimension=0,
        tiled=True,
    ).astype(jnp.float32)
    attn_inv = rms_scale(branch)
    hidden = inputs.astype(f32) + branch * attn_inv * attention_gain
    hidden_whole = lax.all_gather(hidden.astype(bf16), "tp", axis=0, tiled=True)
    gate_value = jnp.einsum("tsd,df->tsf", hidden_whole, gate_weight, preferred_element_type=f32)
    up_value = jnp.einsum("tsd,df->tsf", hidden_whole, up_weight, preferred_element_type=f32)
    sigmoid_value = jax.nn.sigmoid(gate_value)
    act_low = (gate_value * sigmoid_value * up_value).astype(bf16)
    part = act_low
    down_value = lax.psum_scatter(
        jnp.einsum("tsf,fd->tsd", part, down_weight, preferred_element_type=f32).astype(
            jnp.bfloat16
        ),
        "tp",
        scatter_dimension=0,
        tiled=True,
    ).astype(jnp.float32)
    feed_inv = rms_scale(down_value)
    layer_out = hidden + down_value * feed_inv * feed_gain
    grad_top = cotangent.astype(f32)
    feed_gain_term = jnp.sum(grad_top * down_value * feed_inv, axis=(0, 1))
    down_grad_low = norm_back(down_value, feed_inv, feed_gain, grad_top).astype(bf16)
    down_whole = lax.all_gather(down_grad_low, "tp", axis=0, tiled=True)
    act_grad = jnp.einsum("tsd,fd->tsf", down_whole, down_weight, preferred_element_type=f32)
    down_term = jnp.einsum("tsd,tsf->df", down_whole, act_low, preferred_element_type=f32)
    up_grad_low = (act_grad * gate_value * sigmoid_value).astype(bf16)
    gate_grad_low = (
        act_grad * up_value * sigmoid_value * (1.0 + gate_value * (1.0 - sigmoid_value))
    ).astype(bf16)
    gate_term = jnp.einsum("tsd,tsf->df", hidden_whole, gate_grad_low, preferred_element_type=f32)
    up_term = jnp.einsum("tsd,tsf->df", hidden_whole, up_grad_low, preferred_element_type=f32)
    hidden_grad = grad_top + lax.psum_scatter(
        (
            jnp.einsum("tsf,df->tsd", gate_grad_low, gate_weight, preferred_element_type=f32)
            + jnp.einsum("tsf,df->tsd", up_grad_low, up_weight, preferred_element_type=f32)
        ).astype(jnp.bfloat16),
        "tp",
        scatter_dimension=0,
        tiled=True,
    ).astype(jnp.float32)
    attention_gain_term = jnp.sum(hidden_grad * branch * attn_inv, axis=(0, 1))
    branch_grad_low = norm_back(branch, attn_inv, attention_gain, hidden_grad).astype(bf16)
    branch_whole = lax.all_gather(branch_grad_low, "tp", axis=0, tiled=True)
    out_term = jnp.einsum("tsd,tsh->dh", branch_whole, mixed_low, preferred_element_type=f32)
    mixed_grad_low = jnp.einsum(
        "tsd,hd->tsh", branch_whole, output_weight, preferred_element_type=f32
    ).astype(bf16)
    grad_seq = jnp.transpose(
        mixed_grad_low.reshape(here_length, seq_count, local_heads, HEAD), (1, 0, 2, 3)
    )
    delta_own = jnp.transpose(jnp.sum(grad_seq.astype(f32) * attended, axis=-1), (0, 2, 1))
    key_cycle, value_cycle = cycle_values(key_low, value_low)

    def query_back(pieces):
        query_part, key_part, value_part, own_part, doc_row, grad_part, log_part, delta_part = (
            pieces
        )
        key_heads, value_heads = keys_in_reach(key_part, value_part)
        scores = scores_of(query_part, key_heads, own_part, doc_row, first_row, 0)
        weights = jnp.exp(scores - log_part[..., None])
        weight_grad = jnp.einsum("qhd,khd->hqk", grad_part, value_heads, preferred_element_type=f32)
        score_grad = (weights * (weight_grad - delta_part[:, :, None]) * score_scale).astype(bf16)
        query_grad = jnp.einsum("hqk,khd->qhd", score_grad, key_heads, preferred_element_type=f32)
        key_grad = jnp.einsum("hqk,qhd->khd", score_grad, query_part, preferred_element_type=f32)
        value_grad = jnp.einsum(
            "hqk,qhd->khd", weights.astype(bf16), grad_part, preferred_element_type=f32
        )
        return (
            query_grad,
            key_grad.reshape(total_length, heads_width),
            value_grad.reshape(total_length, heads_width),
        )

    query_grads, key_full, value_full = lax.map(
        query_back,
        (query_seq, key_cycle, value_cycle, own_docs, documents, grad_seq, log_total, delta_own),
    )
    key_own, value_own = (
        lax.psum_scatter(
            key_full.astype(jnp.bfloat16), "seq", scatter_dimension=1, tiled=True
        ).astype(jnp.float32),
        lax.psum_scatter(
            value_full.astype(jnp.bfloat16), "seq", scatter_dimension=1, tiled=True
        ).astype(jnp.float32),
    )
    value_grad_low = jnp.transpose(value_own, (1, 0, 2)).astype(bf16)
    query_rot = unrotate(jnp.transpose(query_grads, (1, 0, 2, 3)), cosine, sine_part)
    query_rot = query_rot.reshape(here_length, seq_count, heads_width)
    key_rot = unrotate(heads_of(jnp.transpose(key_own, (1, 0, 2))), cosine, sine_part)
    key_rot = key_rot.reshape(here_length, seq_count, heads_width)
    query_gain_term = jnp.sum(query_rot * queries * query_inv, axis=(0, 1))
    key_gain_term = jnp.sum(key_rot * keys_proj * key_inv, axis=(0, 1))

    def placed(term):
        return lax.dynamic_update_slice(
            jnp.zeros((model_width,), f32), term, (tp_index * heads_width,)
        )

    query_dot, key_dot, query_gain_sum, key_gain_sum, attention_gain_sum, feed_gain_sum = (
        lax.psum(
            jnp.sum(query_rot * query_gain * queries, axis=-1).astype(jnp.bfloat16), "tp"
        ).astype(jnp.float32),
        lax.psum(
            jnp.sum(key_rot * key_gain * keys_proj, axis=-1).astype(jnp.bfloat16), "tp"
        ).astype(jnp.float32),
        lax.psum(placed(query_gain_term).astype(jnp.bfloat16), "tp").astype(jnp.float32),
        lax.psum(placed(key_gain_term).astype(jnp.bfloat16), "tp").astype(jnp.float32),
        lax.psum(attention_gain_term.astype(jnp.bfloat16), "tp").astype(jnp.float32),
        lax.psum(feed_gain_term.astype(jnp.bfloat16), "tp").astype(jnp.float32),
    )
    query_grad_low = (
        query_inv * query_gain * query_rot
        - queries * query_inv**3 * (query_dot / model_width)[..., None]
    ).astype(bf16)
    key_grad_low = (
        key_inv * key_gain * key_rot - keys_proj * key_inv**3 * (key_dot / model_width)[..., None]
    ).astype(bf16)
    query_term = jnp.einsum("tsd,tsh->dh", whole, query_grad_low, preferred_element_type=f32)
    key_term = jnp.einsum("tsd,tsh->dh", whole, key_grad_low, preferred_element_type=f32)
    value_term = jnp.einsum("tsd,tsh->dh", whole, value_grad_low, preferred_element_type=f32)
    query_part = query_grad_low
    key_part = key_grad_low
    value_part = value_grad_low
    input_grad = hidden_grad + lax.psum_scatter(
        (
            jnp.einsum("tsh,dh->tsd", query_part, query_weight, preferred_element_type=f32)
            + jnp.einsum("tsh,dh->tsd", key_part, key_weight, preferred_element_type=f32)
            + jnp.einsum("tsh,dh->tsd", value_part, value_weight, preferred_element_type=f32)
        ).astype(jnp.bfloat16),
        "tp",
        scatter_dimension=0,
        tiled=True,
    ).astype(jnp.float32)
    summed = (
        lax.psum_scatter(
            query_term.astype(jnp.bfloat16), "seq", scatter_dimension=0, tiled=True
        ).astype(jnp.float32),
        lax.psum_scatter(
            key_term.astype(jnp.bfloat16), "seq", scatter_dimension=0, tiled=True
        ).astype(jnp.float32),
        lax.psum_scatter(
            value_term.astype(jnp.bfloat16), "seq", scatter_dimension=0, tiled=True
        ).astype(jnp.float32),
        lax.psum_scatter(
            out_term.astype(jnp.bfloat16), "seq", scatter_dimension=0, tiled=True
        ).astype(jnp.float32),
        lax.psum_scatter(
            gate_term.astype(jnp.bfloat16), "seq", scatter_dimension=0, tiled=True
        ).astype(jnp.float32),
        lax.psum_scatter(
            up_term.astype(jnp.bfloat16), "seq", scatter_dimension=0, tiled=True
        ).astype(jnp.float32),
        lax.psum_scatter(
            down_term.astype(jnp.bfloat16), "seq", scatter_dimension=0, tiled=True
        ).astype(jnp.float32),
        lax.psum_scatter(
            query_gain_sum.astype(jnp.bfloat16), "seq", scatter_dimension=0, tiled=True
        ).astype(jnp.float32),
        lax.psum_scatter(
            key_gain_sum.astype(jnp.bfloat16), "seq", scatter_dimension=0, tiled=True
        ).astype(jnp.float32),
        lax.psum_scatter(
            attention_gain_sum.astype(jnp.bfloat16), "seq", scatter_dimension=0, tiled=True
        ).astype(jnp.float32),
        lax.psum_scatter(
            feed_gain_sum.astype(jnp.bfloat16), "seq", scatter_dimension=0, tiled=True
        ).astype(jnp.float32),
    )
    return (
        layer_out,
        input_grad,
        summed[0],
        summed[1],
        summed[2],
        summed[3].T,
        summed[4],
        summed[5],
        summed[6].T,
        summed[7],
        summed[8],
        summed[9],
        summed[10],
    )


def xor_pairs(size, bit):
    return [(index, index ^ bit) for index in range(size)]


def grouped(
    inputs,
    documents,
    query_weight,
    key_weight,
    value_weight,
    output_weight,
    query_gain,
    key_gain,
    attention_gain,
    gate_weight,
    up_weight,
    down_weight,
    feed_gain,
    cotangent,
):
    f32 = jnp.float32
    bf16 = jnp.bfloat16
    row_count, seq_count, width = inputs.shape
    own_count = row_count * seq_count
    half_count = own_count // 2
    all_count = 8 * own_count
    block = width // 8
    s = lax.axis_index("seq")
    t = lax.axis_index("tp")
    zh, zl, x = s // 4, (s // 2) % 2, s % 2
    y, c = t // 2, t % 2
    sequence = 2 * zh + x

    def by_seq(v, bits):
        return lax.ppermute(v, "seq", xor_pairs(8, bits))

    def by_tp(v, bits):
        return lax.ppermute(v, "tp", xor_pairs(4, bits))

    swap_x = lambda v: by_seq(v, 1)
    swap_zl = lambda v: by_seq(v, 2)
    swap_zh = lambda v: by_seq(v, 4)
    swap_c = lambda v: by_tp(v, 1)
    swap_y = lambda v: by_tp(v, 2)

    def to_sequence(v):
        pieces = []
        for k in range(4):
            part = lax.dynamic_index_in_dim(v, sequence ^ k, 1, keepdims=False)
            pieces.append(by_seq(part, (k // 2) * 4 + k % 2) if k else part)
        return jnp.concatenate(pieces, axis=0)

    def from_sequence(v):
        parts = v.astype(bf16).reshape(4, row_count, width)
        pieces = [parts[0]]
        for k in range(1, 4):
            pieces.append(by_seq(parts[k], (k // 2) * 4 + k % 2))
        rows = jnp.stack(pieces, axis=1).reshape(row_count, 2, 2, width)
        rows = jnp.where(zh == 1, rows[:, ::-1], rows)
        rows = jnp.where(x == 1, rows[:, :, ::-1], rows)
        return rows.reshape(row_count, 4, width).astype(f32)

    def gather(a):
        a0, b0 = a[:half_count], a[half_count:]
        a1 = swap_y(a0)
        b1 = swap_zl(b0)
        a23 = swap_zl(jnp.concatenate([a0, a1]))
        b13 = swap_y(jnp.concatenate([b0, b1]))
        a_all = jnp.concatenate([a0, a1, a23])
        b_all = jnp.concatenate(
            [b0, b13[:half_count], b1, b13[half_count:]]
        )
        return jnp.concatenate([a_all, swap_c(a_all), b_all, swap_c(b_all)])

    def scatter(p):
        p = p.astype(bf16).reshape(2, 2, 4 * half_count, width)
        p = (p[:, 0].astype(f32) + swap_c(p[:, 1]).astype(f32)).astype(bf16)
        a = p[0].reshape(2, 2 * half_count, width)
        a = (a[0].astype(f32) + swap_zl(a[1]).astype(f32)).astype(bf16)
        a = a[:half_count].astype(f32) + swap_y(a[half_count:]).astype(f32)
        b = p[1].reshape(2, 2, half_count, width)
        b = (b[:, 0].astype(f32) + swap_y(b[:, 1]).astype(f32)).astype(bf16)
        b = b[0].astype(f32) + swap_zl(b[1]).astype(f32)
        return jnp.concatenate([a, b])

    def group_sum(v):
        v = v.reshape(-1, 2, 2, 2, 2, half_count)
        v = v + swap_c(v)[:, :, ::-1]
        v = v + swap_y(v)[:, :, :, :, ::-1]
        v = v + swap_zl(v)[:, :, :, ::-1]
        return v.reshape(-1, all_count)

    def feature_blocks(v, bits):
        v = v.reshape(all_count, 8, block)
        return jnp.concatenate(
            [lax.dynamic_index_in_dim(v, s ^ k, 1, keepdims=False) for k in bits], axis=1
        )

    def weight_sum(features, units, units_first):
        def product(bits):
            left = feature_blocks(features, bits)
            if units_first:
                return jnp.einsum("tu,tf->uf", units, left, preferred_element_type=f32)
            return jnp.einsum("tf,tu->fu", left, units, preferred_element_type=f32)

        axis = 1 if units_first else 0

        def part(v, first, count):
            return lax.slice_in_dim(v, first * block, (first + count) * block, axis=axis)

        far = swap_x(product((5, 7, 1, 3)).astype(bf16))
        sent = (product((4, 6)) + part(far, 0, 2).astype(f32)).astype(bf16)
        sent = swap_zh(sent)
        kept = product((0, 2)) + part(far, 2, 2).astype(f32) + sent.astype(f32)
        other = swap_zl(part(kept, 1, 1).astype(bf16)).astype(f32)
        mine = part(kept, 0, 1)
        axis = 1 - axis
        return jnp.where(
            zl == 0,
            jnp.concatenate([mine, other], axis=axis),
            jnp.concatenate([other, mine], axis=axis),
        )

    def zl_half(w, axis):
        size = w.shape[axis] // 2
        return lax.dynamic_slice_in_dim(w, zl * size, size, axis)

    wq, wk, wv = zl_half(query_weight, 1), zl_half(key_weight, 1), zl_half(value_weight, 1)
    wo = zl_half(output_weight, 0)
    wg, wu, wd = zl_half(gate_weight, 1), zl_half(up_weight, 1), zl_half(down_weight, 0)
    gq, gk = zl_half(query_gain, 0), zl_half(key_gain, 0)
    heads_width = wq.shape[1]
    heads = heads_width // HEAD
    score_scale = HEAD ** (-0.5)

    rows_in = to_sequence(inputs)
    grad_top = to_sequence(cotangent).astype(f32)
    whole = gather(rows_in)

    def relative(v):
        v = v.reshape(2, 2, 2, 2, 2, row_count)
        for axis, bit in enumerate((zh, zl, x, y, c)):
            v = jnp.where(bit == 1, jnp.flip(v, axis), v)
        return jnp.transpose(v, (0, 4, 1, 3, 2, 5)).reshape(all_count)

    doc_row = lax.dynamic_index_in_dim(documents, sequence, 0, keepdims=False)
    places = relative(jnp.arange(all_count, dtype=jnp.int32))
    docs = relative(doc_row)
    starts = jnp.sum((doc_row[None, :] < docs[:, None]).astype(jnp.int32), axis=-1)
    cosine, sine_part = rope_tables(places - starts, HEAD)
    allowed = (docs[:, None] == docs[None, :]) & (places[None, :] <= places[:, None])

    def project(w):
        return jnp.einsum("rd,dh->rh", whole, w, preferred_element_type=f32)

    queries, keys_proj = project(wq), project(wk)
    value_low = project(wv).astype(bf16)
    sums = group_sum(
        jnp.stack([jnp.sum(queries * queries, axis=-1), jnp.sum(keys_proj * keys_proj, axis=-1)])
    )
    query_inv = lax.rsqrt(sums[0] / width + EPS)[:, None]
    key_inv = lax.rsqrt(sums[1] / width + EPS)[:, None]

    def heads_of(v):
        return v.reshape(all_count, heads, HEAD)

    query_low = rotate(heads_of(queries * query_inv * gq), cosine, sine_part).astype(bf16)
    key_low = rotate(heads_of(keys_proj * key_inv * gk), cosine, sine_part).astype(bf16)
    value_heads = heads_of(value_low)

    def scores_of():
        scores = (
            jnp.einsum("qhd,khd->hqk", query_low, key_low, preferred_element_type=f32)
            * score_scale
        )
        return jnp.where(allowed[None], scores, NEGATIVE)

    scores = scores_of()
    top_score = jnp.max(scores, axis=-1, keepdims=True)
    spread = jnp.exp(scores - top_score)
    total = jnp.sum(spread, axis=-1, keepdims=True)
    weights = (spread / total).astype(bf16)
    attended = jnp.einsum("hqk,khd->qhd", weights, value_heads, preferred_element_type=f32)
    log_total = top_score + jnp.log(total)
    mixed_low = attended.reshape(all_count, heads_width).astype(bf16)

    branch = scatter(jnp.einsum("rh,hd->rd", mixed_low, wo, preferred_element_type=f32))
    attn_inv = rms_scale(branch)
    hidden = rows_in.astype(f32) + branch * attn_inv * attention_gain
    hidden_whole = gather(hidden.astype(bf16))
    gate_value = jnp.einsum("rd,df->rf", hidden_whole, wg, preferred_element_type=f32)
    up_value = jnp.einsum("rd,df->rf", hidden_whole, wu, preferred_element_type=f32)
    sigmoid_value = jax.nn.sigmoid(gate_value)
    act_low = (gate_value * sigmoid_value * up_value).astype(bf16)
    down_value = scatter(jnp.einsum("rf,fd->rd", act_low, wd, preferred_element_type=f32))
    feed_inv = rms_scale(down_value)
    layer_out = from_sequence(hidden + down_value * feed_inv * feed_gain)
    feed_gain_term = jnp.sum(grad_top * down_value * feed_inv, axis=0)
    down_whole = gather(norm_back(down_value, feed_inv, feed_gain, grad_top).astype(bf16))

    down_term = weight_sum(down_whole, act_low, True)
    act_grad = jnp.einsum("rd,fd->rf", down_whole, wd, preferred_element_type=f32)
    up_grad_low = (act_grad * gate_value * sigmoid_value).astype(bf16)
    gate_grad_low = (
        act_grad * up_value * sigmoid_value * (1.0 + gate_value * (1.0 - sigmoid_value))
    ).astype(bf16)
    hidden_grad = grad_top + scatter(
        jnp.einsum("rf,df->rd", gate_grad_low, wg, preferred_element_type=f32)
        + jnp.einsum("rf,df->rd", up_grad_low, wu, preferred_element_type=f32)
    )
    gate_term = weight_sum(hidden_whole, gate_grad_low, False)
    up_term = weight_sum(hidden_whole, up_grad_low, False)
    attention_gain_term = jnp.sum(hidden_grad * branch * attn_inv, axis=0)
    branch_whole = gather(norm_back(branch, attn_inv, attention_gain, hidden_grad).astype(bf16))
    mixed_grad_low = jnp.einsum(
        "rd,hd->rh", branch_whole, wo, preferred_element_type=f32
    ).astype(bf16)
    out_term = weight_sum(branch_whole, mixed_low, True)

    grad_heads = heads_of(mixed_grad_low)
    delta = jnp.transpose(jnp.sum(grad_heads.astype(f32) * attended, axis=-1))
    weights = jnp.exp(scores_of() - log_total)
    weight_grad = jnp.einsum("qhd,khd->hqk", grad_heads, value_heads, preferred_element_type=f32)
    score_grad = (weights * (weight_grad - delta[:, :, None]) * score_scale).astype(bf16)
    query_back = jnp.einsum("hqk,khd->qhd", score_grad, key_low, preferred_element_type=f32)
    key_back = jnp.einsum("hqk,qhd->khd", score_grad, query_low, preferred_element_type=f32)
    value_grad_low = (
        jnp.einsum("hqk,qhd->khd", weights.astype(bf16), grad_heads, preferred_element_type=f32)
        .reshape(all_count, heads_width)
        .astype(bf16)
    )
    query_rot = unrotate(query_back, cosine, sine_part).reshape(all_count, heads_width)
    key_rot = unrotate(key_back, cosine, sine_part).reshape(all_count, heads_width)
    query_gain_term = jnp.sum(query_rot * queries * query_inv, axis=0)
    key_gain_term = jnp.sum(key_rot * keys_proj * key_inv, axis=0)
    dots = group_sum(
        jnp.stack(
            [
                jnp.sum(query_rot * gq * queries, axis=-1),
                jnp.sum(key_rot * gk * keys_proj, axis=-1),
            ]
        )
    )
    query_grad_low = (
        query_inv * gq * query_rot - queries * query_inv**3 * (dots[0] / width)[:, None]
    ).astype(bf16)
    key_grad_low = (
        key_inv * gk * key_rot - keys_proj * key_inv**3 * (dots[1] / width)[:, None]
    ).astype(bf16)
    input_grad = from_sequence(
        hidden_grad
        + scatter(
            jnp.einsum("rh,dh->rd", query_grad_low, wq, preferred_element_type=f32)
            + jnp.einsum("rh,dh->rd", key_grad_low, wk, preferred_element_type=f32)
            + jnp.einsum("rh,dh->rd", value_grad_low, wv, preferred_element_type=f32)
        )
    )
    query_term = weight_sum(whole, query_grad_low, False)
    key_term = weight_sum(whole, key_grad_low, False)
    value_term = weight_sum(whole, value_grad_low, False)

    place = (2 * t + zl) * heads_width

    def placed(term):
        return lax.dynamic_update_slice(jnp.zeros((width,), f32), term, (place,))

    gains = lax.psum(
        jnp.stack(
            [placed(query_gain_term), placed(key_gain_term), attention_gain_term, feed_gain_term]
        ),
        ("seq", "tp"),
    )
    gains = lax.dynamic_slice_in_dim(gains, s * block, block, 1)
    return (
        layer_out,
        input_grad,
        query_term,
        key_term,
        value_term,
        out_term,
        gate_term,
        up_term,
        down_term,
        gains[0],
        gains[1],
        gains[2],
        gains[3],
    )


def solution(mesh):
    step = grouped if mesh.shape["seq"] == 8 and mesh.shape["tp"] == 4 else local
    return jax.shard_map(
        step,
        mesh=mesh,
        in_specs=(
            P(("seq", "tp"), None, None),
            P(),
            P(None, "tp"),
            P(None, "tp"),
            P(None, "tp"),
            P("tp", None),
            P("tp"),
            P("tp"),
            P(),
            P(None, "tp"),
            P(None, "tp"),
            P("tp", None),
            P(),
            P(("seq", "tp"), None, None),
        ),
        out_specs=(
            P(("seq", "tp"), None, None),
            P(("seq", "tp"), None, None),
            P("seq", "tp"),
            P("seq", "tp"),
            P("seq", "tp"),
            P("tp", "seq"),
            P("seq", "tp"),
            P("seq", "tp"),
            P("tp", "seq"),
            P("seq"),
            P("seq"),
            P("seq"),
            P("seq"),
        ),
        check_vma=False,
    )
```

```python
import jax
import jax.numpy as jnp
from jax import lax
from jax.experimental.layout import Layout, with_layout_constraint
from jax.experimental import pallas as pl
from jax.experimental.pallas import tpu as pltpu
from jax.sharding import Mesh
from jax.sharding import PartitionSpec as P

HEAD = 128


EPS = 1e-06
THETA = 500000.0
NEGATIVE = -1e30


def rope_tables(positions, head_size):
    half_size = head_size // 2
    rates = jnp.exp(-jnp.log(THETA) * (2.0 * jnp.arange(half_size, dtype=jnp.float32) / head_size))
    angles = positions.astype(jnp.float32)[..., None] * rates
    cosine = jnp.cos(angles)
    sine_part = jnp.sin(angles)
    return (
        jnp.concatenate([cosine, cosine], axis=-1)[..., None, :],
        jnp.concatenate([sine_part, sine_part], axis=-1)[..., None, :],
    )


def rotate(tensor, cosine, sine_part):
    half_size = tensor.shape[-1] // 2
    turned = jnp.concatenate([-tensor[..., half_size:], tensor[..., :half_size]], axis=-1)
    return tensor * cosine + turned * sine_part


def unrotate(grad_in, cosine, sine_part):
    half_size = grad_in.shape[-1] // 2
    scaled = grad_in * sine_part
    return grad_in * cosine + jnp.concatenate(
        [scaled[..., half_size:], -scaled[..., :half_size]], axis=-1
    )


def rms_scale(tensor):
    return lax.rsqrt(jnp.mean(tensor * tensor, axis=-1, keepdims=True) + EPS)


def norm_back(tensor, inverse, gain, grad_in):
    weighted = grad_in * gain
    return inverse * weighted - tensor * inverse**3 * jnp.mean(
        weighted * tensor, axis=-1, keepdims=True
    )


def cycle_values(key_low, value_low):
    return (
        lax.all_gather(jnp.transpose(key_low, (1, 0, 2)), "seq", axis=1, tiled=True),
        lax.all_gather(jnp.transpose(value_low, (1, 0, 2)), "seq", axis=1, tiled=True),
    )


def allowed_mask(query_docs, key_docs, query_first, key_first):
    query_places = query_first + jnp.arange(query_docs.shape[0], dtype=jnp.int32)
    key_places = key_first + jnp.arange(key_docs.shape[0], dtype=jnp.int32)
    return (query_docs[:, None] == key_docs[None, :]) & (
        key_places[None, :] <= query_places[:, None]
    )


def local(
    inputs,
    documents,
    query_weight,
    key_weight,
    value_weight,
    output_weight,
    query_gain,
    key_gain,
    attention_gain,
    gate_weight,
    up_weight,
    down_weight,
    feed_gain,
    cotangent,
):
    row_count, seq_count, model_width = inputs.shape
    heads_width = query_weight.shape[1]
    local_heads = heads_width // HEAD
    score_scale = HEAD ** (-0.5)
    seq_index = lax.axis_index("seq")
    tp_index = lax.axis_index("tp")
    total_length = documents.shape[1]
    f32 = jnp.float32
    bf16 = jnp.bfloat16
    whole = lax.all_gather(inputs, "tp", axis=0, tiled=True)
    here_length = whole.shape[0]
    queries = jnp.einsum("tsd,dh->tsh", whole, query_weight, preferred_element_type=f32)
    keys_proj = jnp.einsum("tsd,dh->tsh", whole, key_weight, preferred_element_type=f32)
    values_proj = jnp.einsum("tsd,dh->tsh", whole, value_weight, preferred_element_type=f32)
    query_sq, key_sq = lax.psum(
        (jnp.sum(queries * queries, axis=-1), jnp.sum(keys_proj * keys_proj, axis=-1)), "tp"
    )
    query_inv = lax.rsqrt(query_sq / model_width + EPS)[..., None]
    key_inv = lax.rsqrt(key_sq / model_width + EPS)[..., None]
    first_row = seq_index * here_length
    own_docs = lax.dynamic_slice_in_dim(documents, first_row, here_length, 1)
    starts = jnp.sum((documents[:, None, :] < own_docs[:, :, None]).astype(jnp.int32), axis=-1)
    positions = (first_row + jnp.arange(here_length, dtype=jnp.int32))[:, None] - starts.T
    cosine, sine_part = rope_tables(positions, HEAD)

    def heads_of(tensor):
        return tensor.reshape(here_length, seq_count, local_heads, HEAD)

    query_low = rotate(heads_of(queries * query_inv * query_gain), cosine, sine_part).astype(bf16)
    key_low = rotate(heads_of(keys_proj * key_inv * key_gain), cosine, sine_part).astype(bf16)
    key_low = key_low.reshape(here_length, seq_count, heads_width)
    value_low = values_proj.astype(bf16)
    key_cycle, value_cycle = cycle_values(key_low, value_low)
    query_seq = jnp.transpose(query_low, (1, 0, 2, 3))

    def keys_in_reach(key_part, value_part):
        return (
            key_part.reshape(total_length, local_heads, HEAD),
            value_part.reshape(total_length, local_heads, HEAD),
        )

    def scores_of(query_part, key_heads, query_docs, key_docs, first_query, first_key):
        scores = (
            jnp.einsum("qhd,khd->hqk", query_part, key_heads, preferred_element_type=f32)
            * score_scale
        )
        return jnp.where(
            allowed_mask(query_docs, key_docs, first_query, first_key)[None], scores, NEGATIVE
        )

    def attend(pieces):
        query_part, key_part, value_part, own_part, doc_row = pieces
        key_heads, value_heads = keys_in_reach(key_part, value_part)
        scores = scores_of(query_part, key_heads, own_part, doc_row, first_row, 0)
        top_score = jnp.max(scores, axis=-1, keepdims=True)
        spread = jnp.exp(scores - top_score)
        total_sum = jnp.sum(spread, axis=-1, keepdims=True)
        weights = (spread / total_sum).astype(bf16)
        mixed_part = jnp.einsum("hqk,khd->qhd", weights, value_heads, preferred_element_type=f32)
        return (mixed_part, (top_score + jnp.log(total_sum))[..., 0])

    attended, log_total = lax.map(attend, (query_seq, key_cycle, value_cycle, own_docs, documents))
    mixed_low = (
        jnp.transpose(attended, (1, 0, 2, 3))
        .reshape(here_length, seq_count, heads_width)
        .astype(bf16)
    )
    part = mixed_low
    branch = lax.psum_scatter(
        jnp.einsum("tsh,hd->tsd", part, output_weight, preferred_element_type=f32).astype(
            jnp.bfloat16
        ),
        "tp",
        scatter_dimension=0,
        tiled=True,
    ).astype(jnp.float32)
    attn_inv = rms_scale(branch)
    hidden = inputs.astype(f32) + branch * attn_inv * attention_gain
    hidden_whole = lax.all_gather(hidden.astype(bf16), "tp", axis=0, tiled=True)
    gate_value = jnp.einsum("tsd,df->tsf", hidden_whole, gate_weight, preferred_element_type=f32)
    up_value = jnp.einsum("tsd,df->tsf", hidden_whole, up_weight, preferred_element_type=f32)
    sigmoid_value = jax.nn.sigmoid(gate_value)
    act_low = (gate_value * sigmoid_value * up_value).astype(bf16)
    part = act_low
    down_value = lax.psum_scatter(
        jnp.einsum("tsf,fd->tsd", part, down_weight, preferred_element_type=f32).astype(
            jnp.bfloat16
        ),
        "tp",
        scatter_dimension=0,
        tiled=True,
    ).astype(jnp.float32)
    feed_inv = rms_scale(down_value)
    layer_out = hidden + down_value * feed_inv * feed_gain
    grad_top = cotangent.astype(f32)
    feed_gain_term = jnp.sum(grad_top * down_value * feed_inv, axis=(0, 1))
    down_grad_low = norm_back(down_value, feed_inv, feed_gain, grad_top).astype(bf16)
    down_whole = lax.all_gather(down_grad_low, "tp", axis=0, tiled=True)
    act_grad = jnp.einsum("tsd,fd->tsf", down_whole, down_weight, preferred_element_type=f32)
    down_term = jnp.einsum("tsd,tsf->df", down_whole, act_low, preferred_element_type=f32)
    up_grad_low = (act_grad * gate_value * sigmoid_value).astype(bf16)
    gate_grad_low = (
        act_grad * up_value * sigmoid_value * (1.0 + gate_value * (1.0 - sigmoid_value))
    ).astype(bf16)
    gate_term = jnp.einsum("tsd,tsf->df", hidden_whole, gate_grad_low, preferred_element_type=f32)
    up_term = jnp.einsum("tsd,tsf->df", hidden_whole, up_grad_low, preferred_element_type=f32)
    hidden_grad = grad_top + lax.psum_scatter(
        (
            jnp.einsum("tsf,df->tsd", gate_grad_low, gate_weight, preferred_element_type=f32)
            + jnp.einsum("tsf,df->tsd", up_grad_low, up_weight, preferred_element_type=f32)
        ).astype(jnp.bfloat16),
        "tp",
        scatter_dimension=0,
        tiled=True,
    ).astype(jnp.float32)
    attention_gain_term = jnp.sum(hidden_grad * branch * attn_inv, axis=(0, 1))
    branch_grad_low = norm_back(branch, attn_inv, attention_gain, hidden_grad).astype(bf16)
    branch_whole = lax.all_gather(branch_grad_low, "tp", axis=0, tiled=True)
    out_term = jnp.einsum("tsd,tsh->dh", branch_whole, mixed_low, preferred_element_type=f32)
    mixed_grad_low = jnp.einsum(
        "tsd,hd->tsh", branch_whole, output_weight, preferred_element_type=f32
    ).astype(bf16)
    grad_seq = jnp.transpose(
        mixed_grad_low.reshape(here_length, seq_count, local_heads, HEAD), (1, 0, 2, 3)
    )
    delta_own = jnp.transpose(jnp.sum(grad_seq.astype(f32) * attended, axis=-1), (0, 2, 1))
    key_cycle, value_cycle = cycle_values(key_low, value_low)

    def query_back(pieces):
        query_part, key_part, value_part, own_part, doc_row, grad_part, log_part, delta_part = (
            pieces
        )
        key_heads, value_heads = keys_in_reach(key_part, value_part)
        scores = scores_of(query_part, key_heads, own_part, doc_row, first_row, 0)
        weights = jnp.exp(scores - log_part[..., None])
        weight_grad = jnp.einsum("qhd,khd->hqk", grad_part, value_heads, preferred_element_type=f32)
        score_grad = (weights * (weight_grad - delta_part[:, :, None]) * score_scale).astype(bf16)
        query_grad = jnp.einsum("hqk,khd->qhd", score_grad, key_heads, preferred_element_type=f32)
        key_grad = jnp.einsum("hqk,qhd->khd", score_grad, query_part, preferred_element_type=f32)
        value_grad = jnp.einsum(
            "hqk,qhd->khd", weights.astype(bf16), grad_part, preferred_element_type=f32
        )
        return (
            query_grad,
            key_grad.reshape(total_length, heads_width),
            value_grad.reshape(total_length, heads_width),
        )

    query_grads, key_full, value_full = lax.map(
        query_back,
        (query_seq, key_cycle, value_cycle, own_docs, documents, grad_seq, log_total, delta_own),
    )
    key_own, value_own = (
        lax.psum_scatter(
            key_full.astype(jnp.bfloat16), "seq", scatter_dimension=1, tiled=True
        ).astype(jnp.float32),
        lax.psum_scatter(
            value_full.astype(jnp.bfloat16), "seq", scatter_dimension=1, tiled=True
        ).astype(jnp.float32),
    )
    value_grad_low = jnp.transpose(value_own, (1, 0, 2)).astype(bf16)
    query_rot = unrotate(jnp.transpose(query_grads, (1, 0, 2, 3)), cosine, sine_part)
    query_rot = query_rot.reshape(here_length, seq_count, heads_width)
    key_rot = unrotate(heads_of(jnp.transpose(key_own, (1, 0, 2))), cosine, sine_part)
    key_rot = key_rot.reshape(here_length, seq_count, heads_width)
    query_gain_term = jnp.sum(query_rot * queries * query_inv, axis=(0, 1))
    key_gain_term = jnp.sum(key_rot * keys_proj * key_inv, axis=(0, 1))

    def placed(term):
        return lax.dynamic_update_slice(
            jnp.zeros((model_width,), f32), term, (tp_index * heads_width,)
        )

    query_dot, key_dot, query_gain_sum, key_gain_sum, attention_gain_sum, feed_gain_sum = (
        lax.psum(
            jnp.sum(query_rot * query_gain * queries, axis=-1).astype(jnp.bfloat16), "tp"
        ).astype(jnp.float32),
        lax.psum(
            jnp.sum(key_rot * key_gain * keys_proj, axis=-1).astype(jnp.bfloat16), "tp"
        ).astype(jnp.float32),
        lax.psum(placed(query_gain_term).astype(jnp.bfloat16), "tp").astype(jnp.float32),
        lax.psum(placed(key_gain_term).astype(jnp.bfloat16), "tp").astype(jnp.float32),
        lax.psum(attention_gain_term.astype(jnp.bfloat16), "tp").astype(jnp.float32),
        lax.psum(feed_gain_term.astype(jnp.bfloat16), "tp").astype(jnp.float32),
    )
    query_grad_low = (
        query_inv * query_gain * query_rot
        - queries * query_inv**3 * (query_dot / model_width)[..., None]
    ).astype(bf16)
    key_grad_low = (
        key_inv * key_gain * key_rot - keys_proj * key_inv**3 * (key_dot / model_width)[..., None]
    ).astype(bf16)
    query_term = jnp.einsum("tsd,tsh->dh", whole, query_grad_low, preferred_element_type=f32)
    key_term = jnp.einsum("tsd,tsh->dh", whole, key_grad_low, preferred_element_type=f32)
    value_term = jnp.einsum("tsd,tsh->dh", whole, value_grad_low, preferred_element_type=f32)
    query_part = query_grad_low
    key_part = key_grad_low
    value_part = value_grad_low
    input_grad = hidden_grad + lax.psum_scatter(
        (
            jnp.einsum("tsh,dh->tsd", query_part, query_weight, preferred_element_type=f32)
            + jnp.einsum("tsh,dh->tsd", key_part, key_weight, preferred_element_type=f32)
            + jnp.einsum("tsh,dh->tsd", value_part, value_weight, preferred_element_type=f32)
        ).astype(jnp.bfloat16),
        "tp",
        scatter_dimension=0,
        tiled=True,
    ).astype(jnp.float32)
    summed = (
        lax.psum_scatter(
            query_term.astype(jnp.bfloat16), "seq", scatter_dimension=0, tiled=True
        ).astype(jnp.float32),
        lax.psum_scatter(
            key_term.astype(jnp.bfloat16), "seq", scatter_dimension=0, tiled=True
        ).astype(jnp.float32),
        lax.psum_scatter(
            value_term.astype(jnp.bfloat16), "seq", scatter_dimension=0, tiled=True
        ).astype(jnp.float32),
        lax.psum_scatter(
            out_term.astype(jnp.bfloat16), "seq", scatter_dimension=0, tiled=True
        ).astype(jnp.float32),
        lax.psum_scatter(
            gate_term.astype(jnp.bfloat16), "seq", scatter_dimension=0, tiled=True
        ).astype(jnp.float32),
        lax.psum_scatter(
            up_term.astype(jnp.bfloat16), "seq", scatter_dimension=0, tiled=True
        ).astype(jnp.float32),
        lax.psum_scatter(
            down_term.astype(jnp.bfloat16), "seq", scatter_dimension=0, tiled=True
        ).astype(jnp.float32),
        lax.psum_scatter(
            query_gain_sum.astype(jnp.bfloat16), "seq", scatter_dimension=0, tiled=True
        ).astype(jnp.float32),
        lax.psum_scatter(
            key_gain_sum.astype(jnp.bfloat16), "seq", scatter_dimension=0, tiled=True
        ).astype(jnp.float32),
        lax.psum_scatter(
            attention_gain_sum.astype(jnp.bfloat16), "seq", scatter_dimension=0, tiled=True
        ).astype(jnp.float32),
        lax.psum_scatter(
            feed_gain_sum.astype(jnp.bfloat16), "seq", scatter_dimension=0, tiled=True
        ).astype(jnp.float32),
    )
    return (
        layer_out,
        input_grad,
        summed[0],
        summed[1],
        summed[2],
        summed[3].T,
        summed[4],
        summed[5],
        summed[6].T,
        summed[7],
        summed[8],
        summed[9],
        summed[10],
    )


VMEM_BYTES = 56 * 2**20
BITS = ("zh", "zl", "x", "y", "c")


def turn(v, table):
    return v * table[:, :HEAD] + pltpu.roll(v, HEAD // 2, 1) * table[:, HEAD:]


def turn_back(g, table):
    return g * table[:, :HEAD] - pltpu.roll(g, HEAD // 2, 1) * table[:, HEAD:]


def dot_last(left, right):
    return lax.dot_general(
        left, right, (((1,), (1,)), ((), ())), preferred_element_type=jnp.float32
    )


def dot_first(left, right):
    return lax.dot_general(
        left, right, (((0,), (0,)), ((), ())), preferred_element_type=jnp.float32
    )


def attend_kernel(
    heads, proj_ref, inv_ref, table_ref, place_ref, kp_ref, gain_ref,
    mixed_ref, o_ref, lse_ref, q_ref, k_ref, v_ref,
):
    bf16 = jnp.bfloat16
    width = heads * HEAD
    scale = HEAD ** (-0.5)

    def rows(ref, h, cols=slice(None)):
        v = ref[:, h, :, cols]
        return v.reshape(v.shape[0] * v.shape[1], v.shape[2])

    def put(ref, h, cols, v):
        ref[:, h, :, cols] = v.reshape(ref.shape[0], ref.shape[2], v.shape[1])

    for h in range(2):
        table = rows(table_ref, h)
        inv = rows(inv_ref, h)
        place = rows(place_ref, h)
        masks = [
            (kp_ref[e] >= place[:, 1:2]) & (kp_ref[e] <= place[:, 0:1]) for e in range(h + 1)
        ]
        for head in range(heads):
            cols = slice(head * HEAD, (head + 1) * HEAD)
            key_cols = slice(width + head * HEAD, width + (head + 1) * HEAD)
            value_cols = slice(2 * width + head * HEAD, 2 * width + (head + 1) * HEAD)
            query = turn(rows(proj_ref, h, cols) * inv[:, 0:1] * gain_ref[0:1, cols], table)
            key = turn(rows(proj_ref, h, key_cols) * inv[:, 1:2] * gain_ref[1:2, cols], table)
            query = query.astype(bf16)
            put(q_ref, h, cols, query)
            put(k_ref, h, cols, key.astype(bf16))
            put(v_ref, h, cols, rows(proj_ref, h, value_cols).astype(bf16))
            scores = [
                jnp.where(masks[e], dot_last(query, rows(k_ref, e, cols)), NEGATIVE)
                for e in range(h + 1)
            ]
            top = scores[0].max(axis=-1, keepdims=True)
            if h:
                top = jnp.maximum(top, scores[1].max(axis=-1, keepdims=True))
            spread = [jnp.exp((v - top) * scale) for v in scores]
            total = sum(v.sum(axis=-1, keepdims=True) for v in spread)
            mixed = sum(
                jnp.dot(p.astype(bf16), rows(v_ref, e, cols), preferred_element_type=jnp.float32)
                for e, p in enumerate(spread)
            )
            mixed = mixed / total
            put(o_ref, h, cols, mixed)
            put(mixed_ref, h, cols, mixed.astype(bf16))
            put(lse_ref, h, slice(head, head + 1), top * scale + jnp.log(total))


def attend_back_kernel(
    heads, q_ref, k_ref, v_ref, o_ref, lse_ref, g_ref, table_ref, place_ref, kp_ref,
    yq_ref, yk_ref, dv_ref, acc_k, acc_v,
):
    f32 = jnp.float32
    bf16 = jnp.bfloat16
    scale = HEAD ** (-0.5)

    def rows(ref, h, cols=slice(None)):
        v = ref[:, h, :, cols]
        return v.reshape(v.shape[0] * v.shape[1], v.shape[2])

    def put(ref, h, cols, v):
        ref[:, h, :, cols] = v.reshape(ref.shape[0], ref.shape[2], v.shape[1])

    for head in range(heads):
        cols = slice(head * HEAD, (head + 1) * HEAD)
        for h in range(2):
            query = rows(q_ref, h, cols)
            grad = rows(g_ref, h, cols)
            delta = jnp.sum(grad.astype(f32) * rows(o_ref, h, cols), axis=-1, keepdims=True)
            place = rows(place_ref, h)
            lse = rows(lse_ref, h, slice(head, head + 1))
            query_grad = 0.0
            for e in range(h + 1):
                key, value, kp = rows(k_ref, e, cols), rows(v_ref, e, cols), kp_ref[e]
                allowed = (kp >= place[:, 1:2]) & (kp <= place[:, 0:1])
                scores = jnp.where(allowed, dot_last(query, key) * scale, NEGATIVE)
                weights = jnp.exp(scores - lse)
                score_grad = (weights * (dot_last(grad, value) - delta) * scale).astype(bf16)
                query_grad += jnp.dot(score_grad, key, preferred_element_type=f32)
                key_part = dot_first(score_grad, query)
                value_part = dot_first(weights.astype(bf16), grad)
                if h > e:
                    key_part += acc_k[...]
                    value_part += acc_v[...]
                elif h == 0:
                    acc_k[...] = key_part
                    acc_v[...] = value_part
                    continue
                put(yk_ref, e, cols, turn_back(key_part, rows(table_ref, e)))
                put(dv_ref, e, cols, value_part.astype(bf16))
            put(yq_ref, h, cols, turn_back(query_grad, rows(table_ref, h)))


def feed_back_kernel(
    zl_ref, rows_ref, wg_ref, wu_ref, wd_ref, gate_ref, up_ref,
    gg_ref, ug_ref, own_ref, other0_ref, other1_ref, acc_ref,
):
    f32 = jnp.float32
    bf16 = jnp.bfloat16
    step = pl.program_id(0)
    half = rows_ref.shape[0] // 2
    for part in (1, 0):
        at = slice(part * half, (part + 1) * half)
        act_grad = dot_last(rows_ref[at, :], wd_ref[...])
        gate, up = gate_ref[at, :], up_ref[at, :]
        sig = jax.nn.sigmoid(gate)
        up_low = (act_grad * gate * sig).astype(bf16)
        gate_low = (act_grad * up * sig * (1.0 + gate * (1.0 - sig))).astype(bf16)
        ug_ref[at, :] = up_low
        gg_ref[at, :] = gate_low
        value = dot_last(gate_low, wg_ref[...]) + dot_last(up_low, wu_ref[...])

        @pl.when(step == 0)
        def _():
            acc_ref[at, :] = value

        @pl.when(step == 1)
        def _():
            total = (acc_ref[at, :] + value).astype(bf16)
            if part:
                other0_ref[...] = total[: half // 2]
                other1_ref[...] = total[half // 2 :]
            else:
                own_ref[...] = total


def mixed_back_kernel(zl_ref, rows_ref, weight_ref, out_ref):
    out_ref[...] = dot_last(rows_ref[...], weight_ref[...]).astype(out_ref.dtype)


def grads_kernel(count, ids_ref, features_ref, right_ref, *refs):
    value = dot_first(features_ref[...], right_ref[...])
    for ref in refs[:count]:
        value = value + ref[...].astype(jnp.float32)
    refs[count][...] = value.astype(refs[count].dtype)


def grads(features, right, ids, *terms, kind=jnp.bfloat16):
    tokens, units = right.shape
    block = features.shape[1] // 8
    count = ids.shape[0]
    return pl.pallas_call(
        lambda *refs: grads_kernel(len(terms), *refs),
        grid_spec=pltpu.PrefetchScalarGridSpec(
            num_scalar_prefetch=1,
            grid=(count,),
            in_specs=[
                pl.BlockSpec((tokens, block), lambda i, ids: (0, ids[i])),
                pl.BlockSpec((tokens, units), lambda i, ids: (0, 0)),
            ]
            + [
                pl.BlockSpec((block, units), lambda i, ids, first=first: (first + i, 0))
                for _, first in terms
            ],
            out_specs=pl.BlockSpec((block, units), lambda i, ids: (i, 0)),
        ),
        out_shape=jax.ShapeDtypeStruct((count * block, units), kind),
        compiler_params=pltpu.CompilerParams(vmem_limit_bytes=VMEM_BYTES),
        cost_estimate=pl.CostEstimate(flops=0, bytes_accessed=0, transcendentals=0),
        name="grads",
    )(ids, features, right, *(term for term, _ in terms))


def assemble_kernel(moves, *refs):
    pieces, out_ref, sems = refs[:-2], refs[-2], refs[-1]
    copies = [
        pltpu.make_async_copy(
            pieces[piece].at[pl.ds(first, rows)], out_ref.at[pl.ds(to, rows)], sems.at[index]
        )
        for index, (piece, first, rows, to) in enumerate(moves)
    ]
    for copy in copies:
        copy.start()
    for copy in copies:
        copy.wait()


def assemble(pieces, moves):
    rows = sum(move[2] for move in moves)
    return pl.pallas_call(
        lambda *refs: assemble_kernel(moves, *refs),
        in_specs=[pl.BlockSpec(memory_space=pltpu.VMEM)] * len(pieces),
        out_specs=pl.BlockSpec(memory_space=pl.ANY),
        out_shape=jax.ShapeDtypeStruct((rows, pieces[0].shape[1]), pieces[0].dtype),
        scratch_shapes=[pltpu.SemaphoreType.DMA((len(moves),))],
        compiler_params=pltpu.CompilerParams(vmem_limit_bytes=VMEM_BYTES),
        cost_estimate=pl.CostEstimate(flops=0, bytes_accessed=0, transcendentals=0),
        name="assemble",
    )(*pieces)


def both(*values):
    return lax.optimization_barrier(values)


def grouped(
    inputs,
    documents,
    query_weight,
    key_weight,
    value_weight,
    output_weight,
    query_gain,
    key_gain,
    attention_gain,
    gate_weight,
    up_weight,
    down_weight,
    feed_gain,
    cotangent,
):
    f32 = jnp.float32
    bf16 = jnp.bfloat16
    row_count, seq_count, width = inputs.shape
    half_count = 2 * row_count
    half_all = 8 * half_count
    all_count = 2 * half_all
    block = width // 8
    zh, zl, x, y, c = (lax.axis_index(name) for name in BITS)
    s = 4 * zh + 2 * zl + x
    t = 2 * y + c
    sequence = 2 * zh + x

    def swap(v, name):
        return lax.ppermute(v, name, ((0, 1), (1, 0)))

    def to_sequence(v):
        v = lax.all_to_all(jnp.transpose(v, (1, 0, 2)), ("zh", "x"), 0, 0, tiled=True)
        return v.reshape(2 * half_count, width)

    def from_sequence(v):
        v = v.astype(bf16).reshape(4, row_count, width)
        v = lax.all_to_all(v, ("zh", "x"), 0, 0, tiled=True)
        return jnp.transpose(v, (1, 0, 2)).astype(f32)

    def gather(a, late=None):
        a0, b0 = a[:half_count], a[half_count:]
        a1, b2 = both(swap(a0, "y"), swap(b0, "zl"))
        a01, b02 = jnp.concatenate([a0, a1]), jnp.concatenate([b0, b2])
        if late is None:
            a01, b02 = both(a01, b02)
        else:
            a01, b02, late = both(a01, b02, late)
        a01_c, b02_c = swap(a01, "c"), swap(b02, "c")
        a23, b13 = both(swap(a01, "zl"), swap(b02, "y"))
        a23_c, b13_c = both(swap(a23, "c"), swap(b13, "c"))
        k = half_count
        v = assemble(
            (a01, a23, b02, b13, a01_c, a23_c, b02_c, b13_c),
            [
                move
                for dc in range(2)
                for move in (
                    (4 * dc, 0, 2 * k, 8 * dc * k),
                    (4 * dc + 1, 0, 2 * k, (8 * dc + 2) * k),
                    (4 * dc + 2, 0, k, (8 * dc + 4) * k),
                    (4 * dc + 3, 0, k, (8 * dc + 5) * k),
                    (4 * dc + 2, k, k, (8 * dc + 6) * k),
                    (4 * dc + 3, k, k, (8 * dc + 7) * k),
                )
            ],
        )
        return v if late is None else (v, late)

    def swap_zy(v):
        return lax.ppermute(v, ("zl", "y"), ((0, 3), (3, 0), (1, 2), (2, 1)))

    def gather_direct(a, late):
        others = both(swap(a, "y"), swap(a, "zl"), swap_zy(a), swap(a, "c"), late)
        own, late = (a, *others[:3]), others[4]
        crossed = both(others[3], *(swap(v, "c") for v in own[1:]))
        k = half_count
        v = assemble(
            (*own, *crossed),
            [
                (4 * dc + chip, h * k, k, (8 * dc + 4 * h + chip) * k)
                for dc in range(2)
                for h in range(2)
                for chip in range(4)
            ],
        )
        return v, late

    def scatter_direct(own, *other):
        other = both(*(swap(v, "c") for v in other))
        p = [
            (v.astype(f32) + w.astype(f32)).astype(bf16)
            for v, w in zip(own.reshape(2, 4 * half_count, width), other)
        ]
        k = half_count
        mine, *sent = (
            jnp.concatenate([v[chip * k : (chip + 1) * k] for v in p]) for chip in range(4)
        )
        sent = both(swap(sent[0], "y"), swap(sent[1], "zl"), swap_zy(sent[2]))
        return sum(v.astype(f32) for v in (mine, *sent))

    def scatter(own, *other):
        a, b = own.reshape(2, 4 * half_count, width)
        a_c, b_c = both(*(swap(v, "c") for v in other))
        a = (a.astype(f32) + a_c.astype(f32)).astype(bf16).reshape(2, 2 * half_count, width)
        b = (b.astype(f32) + b_c.astype(f32)).astype(bf16).reshape(2, 2, half_count, width)
        a1, b1 = both(swap(a[1], "zl"), swap(b[:, 1], "y"))
        a = (a[0].astype(f32) + a1.astype(f32)).astype(bf16)
        b = (b[:, 0].astype(f32) + b1.astype(f32)).astype(bf16)
        a1, b1 = both(swap(a[half_count:], "y"), swap(b[1], "zl"))
        a = a[:half_count].astype(f32) + a1.astype(f32)
        b = b[0].astype(f32) + b1.astype(f32)
        return jnp.concatenate([a, b])

    def times(rows, weight, dims):
        parts = [
            jnp.einsum(dims, v, weight, preferred_element_type=f32).astype(bf16)
            for v in (rows[half_all:], rows[:half_all])
        ]
        return parts[1], *jnp.split(parts[0], 2)

    def group_sum(v):
        v = v.reshape(-1, 2, 2, 2, 2, half_count)
        v = v + swap(v, "c")[:, ::-1]
        v = v + swap(v, "y")[:, :, :, :, ::-1]
        v = v + swap(v, "zl")[:, :, :, ::-1]
        return v.reshape(-1, all_count)

    ids_x, ids_zh, ids_zl = (
        s ^ jnp.array(bits, jnp.int32) for bits in ((1, 3, 5, 7), (4, 6), (0, 2))
    )

    def grads_x(features, right):
        return grads(features, right, ids_x)

    def grads_zh(features, right, far):
        return grads(features, right, ids_zh, (far, 2))

    def finish(features, right, far, sent):
        kept = grads(features, right, ids_zl, (far, 0), (sent, 0))
        return kept[:block], swap(kept[block:], "zl")

    def joined(mine, other, transposed=False):
        mine, other = mine.astype(f32), other.astype(f32)
        if transposed:
            mine, other = mine.T, other.T
        axis = 0 if transposed else 1
        return jnp.where(
            zl == 0,
            jnp.concatenate([mine, other], axis=axis),
            jnp.concatenate([other, mine], axis=axis),
        )

    def zl_half(w, axis):
        size = w.shape[axis] // 2
        return lax.dynamic_slice_in_dim(w, zl * size, size, axis)

    rows_in = to_sequence(inputs)
    weights = (
        query_weight, key_weight, value_weight, output_weight, gate_weight, up_weight, down_weight
    )
    whole, (cotangent, weights) = gather(rows_in, (cotangent, weights))
    (
        query_weight, key_weight, value_weight, output_weight, gate_weight, up_weight, down_weight
    ) = weights
    wqkv = jnp.concatenate([zl_half(w, 1) for w in (query_weight, key_weight, value_weight)], 1)
    wo = zl_half(output_weight, 0)
    wg, wu, wd = zl_half(gate_weight, 1), zl_half(up_weight, 1), zl_half(down_weight, 0)
    gq, gk = zl_half(query_gain, 0), zl_half(key_gain, 0)
    heads_width = wo.shape[0]
    heads = heads_width // HEAD

    whole, grad_top = both(whole, to_sequence(cotangent))
    grad_top = grad_top.astype(f32)

    def gathered_order(v):
        v = v.reshape(2, 2, 2, 2, 2, row_count)
        for axis, bit in ((1, zl), (3, y), (4, c)):
            v = jnp.where(bit == 1, jnp.flip(v, axis), v)
        return jnp.transpose(v, (4, 0, 1, 3, 2, 5)).reshape(all_count)

    doc_row = lax.dynamic_index_in_dim(documents, sequence, 0, keepdims=False)
    places = gathered_order(jnp.arange(all_count, dtype=jnp.int32))
    docs = gathered_order(doc_row)
    starts = jnp.sum((doc_row[None, :] < docs[:, None]).astype(jnp.int32), axis=-1)
    cosine, sine_part = rope_tables(places - starts, HEAD)
    signs = jnp.where(jnp.arange(HEAD) < HEAD // 2, -1.0, 1.0).astype(f32)

    def by_half(v):
        return v.reshape(2, 2, half_all // 2, v.shape[-1])

    table = by_half(jnp.concatenate([cosine[:, 0], sine_part[:, 0] * signs], axis=-1))
    row_places = by_half(jnp.stack([places, starts], axis=-1))
    key_places = jnp.transpose(places.reshape(2, 2, half_all // 2), (1, 0, 2))
    key_places = key_places.reshape(2, 1, half_all)
    head_gain = jnp.stack([gq, gk])

    projected = jnp.einsum("rd,dh->rh", whole, wqkv, preferred_element_type=f32)
    queries, keys_proj = projected[:, :heads_width], projected[:, heads_width : 2 * heads_width]
    sums = group_sum(
        jnp.stack([jnp.sum(queries * queries, axis=-1), jnp.sum(keys_proj * keys_proj, axis=-1)])
    )
    inverse = lax.rsqrt(sums / width + EPS).T

    def rows_shape(size, kind):
        return jax.ShapeDtypeStruct((2, 2, half_all // 2, size), kind)

    mixed_low, attended, log_total, query_low, key_low, value_low = pl.pallas_call(
        lambda *refs: attend_kernel(heads, *refs),
        out_shape=[
            rows_shape(heads_width, bf16),
            rows_shape(heads_width, f32),
            rows_shape(heads, f32),
        ]
        + [rows_shape(heads_width, bf16)] * 3,
        compiler_params=pltpu.CompilerParams(vmem_limit_bytes=VMEM_BYTES),
        cost_estimate=pl.CostEstimate(flops=0, bytes_accessed=0, transcendentals=0),
        name="attend",
    )(by_half(projected), by_half(inverse), table, row_places, key_places, head_gain)
    mixed_low = mixed_low.reshape(all_count, heads_width)

    branch = scatter(*times(mixed_low, wo, "rh,hd->rd"))
    attn_inv = rms_scale(branch)
    hidden = rows_in.astype(f32) + branch * attn_inv * attention_gain
    hidden_whole = gather(hidden.astype(bf16))
    gate_value = jnp.einsum("rd,df->rf", hidden_whole, wg, preferred_element_type=f32)
    up_value = jnp.einsum("rd,df->rf", hidden_whole, wu, preferred_element_type=f32)
    sigmoid_value = jax.nn.sigmoid(gate_value)
    act_low = (gate_value * sigmoid_value * up_value).astype(bf16)
    down_value = scatter(*times(act_low, wd, "rf,fd->rd"))
    feed_inv = rms_scale(down_value)
    down_low = norm_back(down_value, feed_inv, feed_gain, grad_top).astype(bf16)
    down_whole, late_hidden = gather(down_low, hidden)
    layer_out = from_sequence(late_hidden + down_value * feed_inv * feed_gain)
    down_whole, layer_out = both(down_whole, layer_out)

    down_far = grads_x(down_whole, act_low)
    down_whole, down_far = both(down_whole, down_far)
    down_far = swap(down_far, "x")
    tile = gate_value.shape[1] // 2
    unit_tile = pl.BlockSpec((all_count, tile), lambda j, z: (0, j))
    rows_full = pl.BlockSpec((all_count, width), lambda j, z: (0, 0))
    rows_part = pl.BlockSpec((half_all // 2, width), lambda j, z: (0, 0))
    rows_half = pl.BlockSpec((half_all, width), lambda j, z: (0, 0))
    weight_tile = pl.BlockSpec((width, tile), lambda j, z: (0, 2 * z[0] + j))
    gate_low, up_low, *hidden_part = pl.pallas_call(
        feed_back_kernel,
        grid_spec=pltpu.PrefetchScalarGridSpec(
            num_scalar_prefetch=1,
            grid=(2,),
            in_specs=[
                rows_full,
                weight_tile,
                weight_tile,
                pl.BlockSpec((tile, width), lambda j, z: (2 * z[0] + j, 0)),
                unit_tile,
                unit_tile,
            ],
            out_specs=[unit_tile, unit_tile, rows_half, rows_part, rows_part],
            scratch_shapes=[pltpu.VMEM((all_count, width), f32)],
        ),
        out_shape=[
            jax.ShapeDtypeStruct(gate_value.shape, bf16),
            jax.ShapeDtypeStruct(gate_value.shape, bf16),
            jax.ShapeDtypeStruct((half_all, width), bf16),
        ]
        + [jax.ShapeDtypeStruct((half_all // 2, width), bf16)] * 2,
        compiler_params=pltpu.CompilerParams(vmem_limit_bytes=VMEM_BYTES),
        cost_estimate=pl.CostEstimate(flops=0, bytes_accessed=0, transcendentals=0),
        name="feed_back",
    )(
        zl[None], down_whole, gate_weight, up_weight, down_weight, gate_value,
        up_value,
    )
    gate_far = grads_x(hidden_whole, gate_low)
    hidden_grad = grad_top + scatter_direct(*hidden_part)
    hidden_grad, gate_far = both(hidden_grad, gate_far)
    gate_far = swap(gate_far, "x")
    hidden_grad, down_far = both(hidden_grad, down_far)
    down_sent = grads_zh(down_whole, act_low, down_far)
    hidden_grad, down_sent = both(hidden_grad, down_sent)
    down_sent = swap(down_sent, "zh")

    branch_low = norm_back(branch, attn_inv, attention_gain, hidden_grad).astype(bf16)
    branch_whole, late_up = gather_direct(branch_low, up_low)
    up_far = grads_x(hidden_whole, late_up)
    branch_whole, up_far = both(branch_whole, up_far)
    up_far = swap(up_far, "x")
    mixed_grad = pl.pallas_call(
        mixed_back_kernel,
        grid_spec=pltpu.PrefetchScalarGridSpec(
            num_scalar_prefetch=1,
            grid=(2,),
            in_specs=[
                pl.BlockSpec((half_all, width), lambda i, z: (i, 0)),
                pl.BlockSpec((heads_width, width), lambda i, z: (z[0], 0)),
            ],
            out_specs=pl.BlockSpec((half_all, heads_width), lambda i, z: (i, 0)),
        ),
        out_shape=jax.ShapeDtypeStruct((all_count, heads_width), bf16),
        compiler_params=pltpu.CompilerParams(vmem_limit_bytes=VMEM_BYTES),
        cost_estimate=pl.CostEstimate(flops=0, bytes_accessed=0, transcendentals=0),
        name="mixed_back",
    )(zl[None], branch_whole, output_weight)

    yq, yk, value_grad_low = pl.pallas_call(
        lambda *refs: attend_back_kernel(heads, *refs),
        out_shape=[rows_shape(heads_width, f32)] * 2 + [rows_shape(heads_width, bf16)],
        scratch_shapes=[pltpu.VMEM((half_all, HEAD), f32)] * 2,
        compiler_params=pltpu.CompilerParams(vmem_limit_bytes=VMEM_BYTES),
        cost_estimate=pl.CostEstimate(flops=0, bytes_accessed=0, transcendentals=0),
        name="attend_back",
    )(
        query_low, key_low, value_low, attended, log_total, by_half(mixed_grad), table,
        row_places, key_places,
    )
    yq, yk, value_grad_low = (
        v.reshape(all_count, heads_width) for v in (yq, yk, value_grad_low)
    )
    query_inv, key_inv = inverse[:, 0:1], inverse[:, 1:2]
    dots = jnp.stack([jnp.sum(yq * gq * queries, axis=-1), jnp.sum(yk * gk * keys_proj, axis=-1)])
    late_yq, gate_far, down_sent = both(yq, gate_far, down_sent)
    down_pair = finish(down_whole, act_low, down_far, down_sent)
    gate_sent = grads_zh(hidden_whole, gate_low, gate_far)
    dots, gate_sent, down_keep = both(group_sum(dots), gate_sent, down_pair[0])
    down_pair = (down_keep, down_pair[1])
    dots = dots.T
    gate_sent = swap(gate_sent, "zh")
    query_grad_low = (
        query_inv * gq * yq - queries * query_inv**3 * (dots[:, 0:1] / width)
    ).astype(bf16)
    key_grad_low = (
        key_inv * gk * yk - keys_proj * key_inv**3 * (dots[:, 1:2] / width)
    ).astype(bf16)
    projected_grad = jnp.concatenate([query_grad_low, key_grad_low, value_grad_low], axis=1)
    input_part = times(projected_grad, wqkv, "rh,dh->rd")
    input_own, late_grad = both(input_part[0], projected_grad)
    in_far = grads_x(whole, late_grad)
    input_sum, in_far = both(scatter_direct(input_own, *input_part[1:]), in_far)
    in_far = swap(in_far, "x")
    input_rows = hidden_grad + input_sum
    input_rows, up_far, late_mixed, gate_sent = both(input_rows, up_far, mixed_low, gate_sent)
    up_sent = grads_zh(hidden_whole, up_low, up_far)
    out_far = grads_x(branch_whole, late_mixed)
    input_rows, up_sent, out_far, late_yq = both(input_rows, up_sent, out_far, late_yq)
    up_sent, out_far = swap(up_sent, "zh"), swap(out_far, "x")
    input_grad = from_sequence(input_rows)
    gate_pair = finish(hidden_whole, gate_low, gate_far, gate_sent)
    in_far, gate_keep = both(in_far, gate_pair[0])
    gate_pair = (gate_keep, gate_pair[1])
    in_sent = swap(grads_zh(whole, projected_grad, in_far), "zh")
    up_pair = finish(hidden_whole, up_low, up_far, up_sent)
    out_far, up_keep = both(out_far, up_pair[0])
    up_pair = (up_keep, up_pair[1])
    out_sent = swap(grads_zh(branch_whole, mixed_low, out_far), "zh")
    in_mine, in_other = finish(whole, projected_grad, in_far, in_sent)
    out_pair = finish(branch_whole, mixed_low, out_far, out_sent)
    head_gains = jnp.stack(
        [jnp.sum(late_yq * queries * query_inv, axis=0), jnp.sum(yk * keys_proj * key_inv, axis=0)]
    )
    head_gains = lax.dynamic_update_slice(
        jnp.zeros((2, width), f32), head_gains, (0, (2 * t + zl) * heads_width)
    )
    row_gains = jnp.stack(
        [
            jnp.sum(hidden_grad * branch * attn_inv, axis=0),
            jnp.sum(grad_top * down_value * feed_inv, axis=0),
        ]
    )
    gains = jnp.concatenate([head_gains, row_gains])
    for name in ("c", "y", "zl"):
        gains = gains + swap(gains, name)
    gains, up_keep = both(gains, up_pair[0])
    up_pair = (up_keep, up_pair[1])
    gains = gains + swap(gains, "x")
    gains, in_mine = both(gains, in_mine)
    gains = gains + swap(gains, "zh")
    gains = lax.dynamic_slice_in_dim(gains, s * block, block, 1)
    down_term = joined(*down_pair, True)
    gate_term = joined(*gate_pair)
    up_term = joined(*up_pair)
    out_term = joined(*out_pair, True)
    query_term, key_term, value_term = (
        joined(
            in_mine[:, k * heads_width : (k + 1) * heads_width],
            in_other[:, k * heads_width : (k + 1) * heads_width],
        )
        for k in range(3)
    )
    return (
        layer_out,
        input_grad,
        query_term,
        key_term,
        value_term,
        out_term,
        gate_term,
        up_term,
        down_term,
        gains[0],
        gains[1],
        gains[2],
        gains[3],
    )


def solution(mesh):
    rows, columns, inner = ("seq", "tp"), ("tp",), ("seq",)
    step = local
    if mesh.shape["seq"] == 8 and mesh.shape["tp"] == 4:
        mesh = Mesh(mesh.devices.reshape(2, 2, 2, 2, 2), BITS)
        rows, columns, inner = BITS, BITS[3:], BITS[:3]
        step = grouped
    return jax.shard_map(
        step,
        mesh=mesh,
        in_specs=(
            P(rows, None, None),
            P(),
            P(None, columns),
            P(None, columns),
            P(None, columns),
            P(columns, None),
            P(columns),
            P(columns),
            P(),
            P(None, columns),
            P(None, columns),
            P(columns, None),
            P(),
            P(rows, None, None),
        ),
        out_specs=(
            P(rows, None, None),
            P(rows, None, None),
            P(inner, columns),
            P(inner, columns),
            P(inner, columns),
            P(columns, inner),
            P(inner, columns),
            P(inner, columns),
            P(columns, inner),
            P(inner),
            P(inner),
            P(inner),
            P(inner),
        ),
        check_vma=False,
    )
```

```python
import jax
import jax.numpy as jnp
from jax import lax
from jax.experimental.layout import Layout, with_layout_constraint
from jax.experimental import pallas as pl
from jax.experimental.pallas import tpu as pltpu
from jax.sharding import Mesh
from jax.sharding import PartitionSpec as P

HEAD = 128


EPS = 1e-06
THETA = 500000.0
NEGATIVE = -1e30


def rope_tables(positions, head_size):
    half_size = head_size // 2
    rates = jnp.exp(-jnp.log(THETA) * (2.0 * jnp.arange(half_size, dtype=jnp.float32) / head_size))
    angles = positions.astype(jnp.float32)[..., None] * rates
    cosine = jnp.cos(angles)
    sine_part = jnp.sin(angles)
    return (
        jnp.concatenate([cosine, cosine], axis=-1)[..., None, :],
        jnp.concatenate([sine_part, sine_part], axis=-1)[..., None, :],
    )


def rotate(tensor, cosine, sine_part):
    half_size = tensor.shape[-1] // 2
    turned = jnp.concatenate([-tensor[..., half_size:], tensor[..., :half_size]], axis=-1)
    return tensor * cosine + turned * sine_part


def unrotate(grad_in, cosine, sine_part):
    half_size = grad_in.shape[-1] // 2
    scaled = grad_in * sine_part
    return grad_in * cosine + jnp.concatenate(
        [scaled[..., half_size:], -scaled[..., :half_size]], axis=-1
    )


def rms_scale(tensor):
    return lax.rsqrt(jnp.mean(tensor * tensor, axis=-1, keepdims=True) + EPS)


def norm_back(tensor, inverse, gain, grad_in):
    weighted = grad_in * gain
    return inverse * weighted - tensor * inverse**3 * jnp.mean(
        weighted * tensor, axis=-1, keepdims=True
    )


def cycle_values(key_low, value_low):
    return (
        lax.all_gather(jnp.transpose(key_low, (1, 0, 2)), "seq", axis=1, tiled=True),
        lax.all_gather(jnp.transpose(value_low, (1, 0, 2)), "seq", axis=1, tiled=True),
    )


def allowed_mask(query_docs, key_docs, query_first, key_first):
    query_places = query_first + jnp.arange(query_docs.shape[0], dtype=jnp.int32)
    key_places = key_first + jnp.arange(key_docs.shape[0], dtype=jnp.int32)
    return (query_docs[:, None] == key_docs[None, :]) & (
        key_places[None, :] <= query_places[:, None]
    )


def local(
    inputs,
    documents,
    query_weight,
    key_weight,
    value_weight,
    output_weight,
    query_gain,
    key_gain,
    attention_gain,
    gate_weight,
    up_weight,
    down_weight,
    feed_gain,
    cotangent,
):
    row_count, seq_count, model_width = inputs.shape
    heads_width = query_weight.shape[1]
    local_heads = heads_width // HEAD
    score_scale = HEAD ** (-0.5)
    seq_index = lax.axis_index("seq")
    tp_index = lax.axis_index("tp")
    total_length = documents.shape[1]
    f32 = jnp.float32
    bf16 = jnp.bfloat16
    whole = lax.all_gather(inputs, "tp", axis=0, tiled=True)
    here_length = whole.shape[0]
    queries = jnp.einsum("tsd,dh->tsh", whole, query_weight, preferred_element_type=f32)
    keys_proj = jnp.einsum("tsd,dh->tsh", whole, key_weight, preferred_element_type=f32)
    values_proj = jnp.einsum("tsd,dh->tsh", whole, value_weight, preferred_element_type=f32)
    query_sq, key_sq = lax.psum(
        (jnp.sum(queries * queries, axis=-1), jnp.sum(keys_proj * keys_proj, axis=-1)), "tp"
    )
    query_inv = lax.rsqrt(query_sq / model_width + EPS)[..., None]
    key_inv = lax.rsqrt(key_sq / model_width + EPS)[..., None]
    first_row = seq_index * here_length
    own_docs = lax.dynamic_slice_in_dim(documents, first_row, here_length, 1)
    starts = jnp.sum((documents[:, None, :] < own_docs[:, :, None]).astype(jnp.int32), axis=-1)
    positions = (first_row + jnp.arange(here_length, dtype=jnp.int32))[:, None] - starts.T
    cosine, sine_part = rope_tables(positions, HEAD)

    def heads_of(tensor):
        return tensor.reshape(here_length, seq_count, local_heads, HEAD)

    query_low = rotate(heads_of(queries * query_inv * query_gain), cosine, sine_part).astype(bf16)
    key_low = rotate(heads_of(keys_proj * key_inv * key_gain), cosine, sine_part).astype(bf16)
    key_low = key_low.reshape(here_length, seq_count, heads_width)
    value_low = values_proj.astype(bf16)
    key_cycle, value_cycle = cycle_values(key_low, value_low)
    query_seq = jnp.transpose(query_low, (1, 0, 2, 3))

    def keys_in_reach(key_part, value_part):
        return (
            key_part.reshape(total_length, local_heads, HEAD),
            value_part.reshape(total_length, local_heads, HEAD),
        )

    def scores_of(query_part, key_heads, query_docs, key_docs, first_query, first_key):
        scores = (
            jnp.einsum("qhd,khd->hqk", query_part, key_heads, preferred_element_type=f32)
            * score_scale
        )
        return jnp.where(
            allowed_mask(query_docs, key_docs, first_query, first_key)[None], scores, NEGATIVE
        )

    def attend(pieces):
        query_part, key_part, value_part, own_part, doc_row = pieces
        key_heads, value_heads = keys_in_reach(key_part, value_part)
        scores = scores_of(query_part, key_heads, own_part, doc_row, first_row, 0)
        top_score = jnp.max(scores, axis=-1, keepdims=True)
        spread = jnp.exp(scores - top_score)
        total_sum = jnp.sum(spread, axis=-1, keepdims=True)
        weights = (spread / total_sum).astype(bf16)
        mixed_part = jnp.einsum("hqk,khd->qhd", weights, value_heads, preferred_element_type=f32)
        return (mixed_part, (top_score + jnp.log(total_sum))[..., 0])

    attended, log_total = lax.map(attend, (query_seq, key_cycle, value_cycle, own_docs, documents))
    mixed_low = (
        jnp.transpose(attended, (1, 0, 2, 3))
        .reshape(here_length, seq_count, heads_width)
        .astype(bf16)
    )
    part = mixed_low
    branch = lax.psum_scatter(
        jnp.einsum("tsh,hd->tsd", part, output_weight, preferred_element_type=f32).astype(
            jnp.bfloat16
        ),
        "tp",
        scatter_dimension=0,
        tiled=True,
    ).astype(jnp.float32)
    attn_inv = rms_scale(branch)
    hidden = inputs.astype(f32) + branch * attn_inv * attention_gain
    hidden_whole = lax.all_gather(hidden.astype(bf16), "tp", axis=0, tiled=True)
    gate_value = jnp.einsum("tsd,df->tsf", hidden_whole, gate_weight, preferred_element_type=f32)
    up_value = jnp.einsum("tsd,df->tsf", hidden_whole, up_weight, preferred_element_type=f32)
    sigmoid_value = jax.nn.sigmoid(gate_value)
    act_low = (gate_value * sigmoid_value * up_value).astype(bf16)
    part = act_low
    down_value = lax.psum_scatter(
        jnp.einsum("tsf,fd->tsd", part, down_weight, preferred_element_type=f32).astype(
            jnp.bfloat16
        ),
        "tp",
        scatter_dimension=0,
        tiled=True,
    ).astype(jnp.float32)
    feed_inv = rms_scale(down_value)
    layer_out = hidden + down_value * feed_inv * feed_gain
    grad_top = cotangent.astype(f32)
    feed_gain_term = jnp.sum(grad_top * down_value * feed_inv, axis=(0, 1))
    down_grad_low = norm_back(down_value, feed_inv, feed_gain, grad_top).astype(bf16)
    down_whole = lax.all_gather(down_grad_low, "tp", axis=0, tiled=True)
    act_grad = jnp.einsum("tsd,fd->tsf", down_whole, down_weight, preferred_element_type=f32)
    down_term = jnp.einsum("tsd,tsf->df", down_whole, act_low, preferred_element_type=f32)
    up_grad_low = (act_grad * gate_value * sigmoid_value).astype(bf16)
    gate_grad_low = (
        act_grad * up_value * sigmoid_value * (1.0 + gate_value * (1.0 - sigmoid_value))
    ).astype(bf16)
    gate_term = jnp.einsum("tsd,tsf->df", hidden_whole, gate_grad_low, preferred_element_type=f32)
    up_term = jnp.einsum("tsd,tsf->df", hidden_whole, up_grad_low, preferred_element_type=f32)
    hidden_grad = grad_top + lax.psum_scatter(
        (
            jnp.einsum("tsf,df->tsd", gate_grad_low, gate_weight, preferred_element_type=f32)
            + jnp.einsum("tsf,df->tsd", up_grad_low, up_weight, preferred_element_type=f32)
        ).astype(jnp.bfloat16),
        "tp",
        scatter_dimension=0,
        tiled=True,
    ).astype(jnp.float32)
    attention_gain_term = jnp.sum(hidden_grad * branch * attn_inv, axis=(0, 1))
    branch_grad_low = norm_back(branch, attn_inv, attention_gain, hidden_grad).astype(bf16)
    branch_whole = lax.all_gather(branch_grad_low, "tp", axis=0, tiled=True)
    out_term = jnp.einsum("tsd,tsh->dh", branch_whole, mixed_low, preferred_element_type=f32)
    mixed_grad_low = jnp.einsum(
        "tsd,hd->tsh", branch_whole, output_weight, preferred_element_type=f32
    ).astype(bf16)
    grad_seq = jnp.transpose(
        mixed_grad_low.reshape(here_length, seq_count, local_heads, HEAD), (1, 0, 2, 3)
    )
    delta_own = jnp.transpose(jnp.sum(grad_seq.astype(f32) * attended, axis=-1), (0, 2, 1))
    key_cycle, value_cycle = cycle_values(key_low, value_low)

    def query_back(pieces):
        query_part, key_part, value_part, own_part, doc_row, grad_part, log_part, delta_part = (
            pieces
        )
        key_heads, value_heads = keys_in_reach(key_part, value_part)
        scores = scores_of(query_part, key_heads, own_part, doc_row, first_row, 0)
        weights = jnp.exp(scores - log_part[..., None])
        weight_grad = jnp.einsum("qhd,khd->hqk", grad_part, value_heads, preferred_element_type=f32)
        score_grad = (weights * (weight_grad - delta_part[:, :, None]) * score_scale).astype(bf16)
        query_grad = jnp.einsum("hqk,khd->qhd", score_grad, key_heads, preferred_element_type=f32)
        key_grad = jnp.einsum("hqk,qhd->khd", score_grad, query_part, preferred_element_type=f32)
        value_grad = jnp.einsum(
            "hqk,qhd->khd", weights.astype(bf16), grad_part, preferred_element_type=f32
        )
        return (
            query_grad,
            key_grad.reshape(total_length, heads_width),
            value_grad.reshape(total_length, heads_width),
        )

    query_grads, key_full, value_full = lax.map(
        query_back,
        (query_seq, key_cycle, value_cycle, own_docs, documents, grad_seq, log_total, delta_own),
    )
    key_own, value_own = (
        lax.psum_scatter(
            key_full.astype(jnp.bfloat16), "seq", scatter_dimension=1, tiled=True
        ).astype(jnp.float32),
        lax.psum_scatter(
            value_full.astype(jnp.bfloat16), "seq", scatter_dimension=1, tiled=True
        ).astype(jnp.float32),
    )
    value_grad_low = jnp.transpose(value_own, (1, 0, 2)).astype(bf16)
    query_rot = unrotate(jnp.transpose(query_grads, (1, 0, 2, 3)), cosine, sine_part)
    query_rot = query_rot.reshape(here_length, seq_count, heads_width)
    key_rot = unrotate(heads_of(jnp.transpose(key_own, (1, 0, 2))), cosine, sine_part)
    key_rot = key_rot.reshape(here_length, seq_count, heads_width)
    query_gain_term = jnp.sum(query_rot * queries * query_inv, axis=(0, 1))
    key_gain_term = jnp.sum(key_rot * keys_proj * key_inv, axis=(0, 1))

    def placed(term):
        return lax.dynamic_update_slice(
            jnp.zeros((model_width,), f32), term, (tp_index * heads_width,)
        )

    query_dot, key_dot, query_gain_sum, key_gain_sum, attention_gain_sum, feed_gain_sum = (
        lax.psum(
            jnp.sum(query_rot * query_gain * queries, axis=-1).astype(jnp.bfloat16), "tp"
        ).astype(jnp.float32),
        lax.psum(
            jnp.sum(key_rot * key_gain * keys_proj, axis=-1).astype(jnp.bfloat16), "tp"
        ).astype(jnp.float32),
        lax.psum(placed(query_gain_term).astype(jnp.bfloat16), "tp").astype(jnp.float32),
        lax.psum(placed(key_gain_term).astype(jnp.bfloat16), "tp").astype(jnp.float32),
        lax.psum(attention_gain_term.astype(jnp.bfloat16), "tp").astype(jnp.float32),
        lax.psum(feed_gain_term.astype(jnp.bfloat16), "tp").astype(jnp.float32),
    )
    query_grad_low = (
        query_inv * query_gain * query_rot
        - queries * query_inv**3 * (query_dot / model_width)[..., None]
    ).astype(bf16)
    key_grad_low = (
        key_inv * key_gain * key_rot - keys_proj * key_inv**3 * (key_dot / model_width)[..., None]
    ).astype(bf16)
    query_term = jnp.einsum("tsd,tsh->dh", whole, query_grad_low, preferred_element_type=f32)
    key_term = jnp.einsum("tsd,tsh->dh", whole, key_grad_low, preferred_element_type=f32)
    value_term = jnp.einsum("tsd,tsh->dh", whole, value_grad_low, preferred_element_type=f32)
    query_part = query_grad_low
    key_part = key_grad_low
    value_part = value_grad_low
    input_grad = hidden_grad + lax.psum_scatter(
        (
            jnp.einsum("tsh,dh->tsd", query_part, query_weight, preferred_element_type=f32)
            + jnp.einsum("tsh,dh->tsd", key_part, key_weight, preferred_element_type=f32)
            + jnp.einsum("tsh,dh->tsd", value_part, value_weight, preferred_element_type=f32)
        ).astype(jnp.bfloat16),
        "tp",
        scatter_dimension=0,
        tiled=True,
    ).astype(jnp.float32)
    summed = (
        lax.psum_scatter(
            query_term.astype(jnp.bfloat16), "seq", scatter_dimension=0, tiled=True
        ).astype(jnp.float32),
        lax.psum_scatter(
            key_term.astype(jnp.bfloat16), "seq", scatter_dimension=0, tiled=True
        ).astype(jnp.float32),
        lax.psum_scatter(
            value_term.astype(jnp.bfloat16), "seq", scatter_dimension=0, tiled=True
        ).astype(jnp.float32),
        lax.psum_scatter(
            out_term.astype(jnp.bfloat16), "seq", scatter_dimension=0, tiled=True
        ).astype(jnp.float32),
        lax.psum_scatter(
            gate_term.astype(jnp.bfloat16), "seq", scatter_dimension=0, tiled=True
        ).astype(jnp.float32),
        lax.psum_scatter(
            up_term.astype(jnp.bfloat16), "seq", scatter_dimension=0, tiled=True
        ).astype(jnp.float32),
        lax.psum_scatter(
            down_term.astype(jnp.bfloat16), "seq", scatter_dimension=0, tiled=True
        ).astype(jnp.float32),
        lax.psum_scatter(
            query_gain_sum.astype(jnp.bfloat16), "seq", scatter_dimension=0, tiled=True
        ).astype(jnp.float32),
        lax.psum_scatter(
            key_gain_sum.astype(jnp.bfloat16), "seq", scatter_dimension=0, tiled=True
        ).astype(jnp.float32),
        lax.psum_scatter(
            attention_gain_sum.astype(jnp.bfloat16), "seq", scatter_dimension=0, tiled=True
        ).astype(jnp.float32),
        lax.psum_scatter(
            feed_gain_sum.astype(jnp.bfloat16), "seq", scatter_dimension=0, tiled=True
        ).astype(jnp.float32),
    )
    return (
        layer_out,
        input_grad,
        summed[0],
        summed[1],
        summed[2],
        summed[3].T,
        summed[4],
        summed[5],
        summed[6].T,
        summed[7],
        summed[8],
        summed[9],
        summed[10],
    )


VMEM_BYTES = 56 * 2**20
BITS = ("zh", "zl", "x", "y", "c")


def turn(v, table):
    return v * table[:, :HEAD] + pltpu.roll(v, HEAD // 2, 1) * table[:, HEAD:]


def turn_back(g, table):
    return g * table[:, :HEAD] - pltpu.roll(g, HEAD // 2, 1) * table[:, HEAD:]


def dot_last(left, right):
    return lax.dot_general(
        left, right, (((1,), (1,)), ((), ())), preferred_element_type=jnp.float32
    )


def dot_first(left, right):
    return lax.dot_general(
        left, right, (((0,), (0,)), ((), ())), preferred_element_type=jnp.float32
    )


def attend_kernel(
    heads, proj_ref, inv_ref, table_ref, place_ref, kp_ref, gain_ref,
    mixed_ref, o_ref, lse_ref, q_ref, k_ref, v_ref,
):
    bf16 = jnp.bfloat16
    width = heads * HEAD
    scale = HEAD ** (-0.5)

    def rows(ref, h, cols=slice(None)):
        v = ref[:, h, :, cols]
        return v.reshape(v.shape[0] * v.shape[1], v.shape[2])

    def put(ref, h, cols, v):
        ref[:, h, :, cols] = v.reshape(ref.shape[0], ref.shape[2], v.shape[1])

    for h in range(2):
        table = rows(table_ref, h)
        inv = rows(inv_ref, h)
        place = rows(place_ref, h)
        masks = [
            (kp_ref[e] >= place[:, 1:2]) & (kp_ref[e] <= place[:, 0:1]) for e in range(h + 1)
        ]
        for head in range(heads):
            cols = slice(head * HEAD, (head + 1) * HEAD)
            key_cols = slice(width + head * HEAD, width + (head + 1) * HEAD)
            value_cols = slice(2 * width + head * HEAD, 2 * width + (head + 1) * HEAD)
            query = turn(rows(proj_ref, h, cols) * inv[:, 0:1] * gain_ref[0:1, cols], table)
            key = turn(rows(proj_ref, h, key_cols) * inv[:, 1:2] * gain_ref[1:2, cols], table)
            query = query.astype(bf16)
            put(q_ref, h, cols, query)
            put(k_ref, h, cols, key.astype(bf16))
            put(v_ref, h, cols, rows(proj_ref, h, value_cols).astype(bf16))
            scores = [
                jnp.where(masks[e], dot_last(query, rows(k_ref, e, cols)), NEGATIVE)
                for e in range(h + 1)
            ]
            top = scores[0].max(axis=-1, keepdims=True)
            if h:
                top = jnp.maximum(top, scores[1].max(axis=-1, keepdims=True))
            spread = [jnp.exp((v - top) * scale) for v in scores]
            total = sum(v.sum(axis=-1, keepdims=True) for v in spread)
            mixed = sum(
                jnp.dot(p.astype(bf16), rows(v_ref, e, cols), preferred_element_type=jnp.float32)
                for e, p in enumerate(spread)
            )
            mixed = mixed / total
            put(o_ref, h, cols, mixed)
            put(mixed_ref, h, cols, mixed.astype(bf16))
            put(lse_ref, h, slice(head, head + 1), top * scale + jnp.log(total))


def attend_back_kernel(
    heads, q_ref, k_ref, v_ref, o_ref, lse_ref, g_ref, table_ref, place_ref, kp_ref,
    yq_ref, yk_ref, dv_ref, acc_k, acc_v,
):
    f32 = jnp.float32
    bf16 = jnp.bfloat16
    scale = HEAD ** (-0.5)

    def rows(ref, h, cols=slice(None)):
        v = ref[:, h, :, cols]
        return v.reshape(v.shape[0] * v.shape[1], v.shape[2])

    def put(ref, h, cols, v):
        ref[:, h, :, cols] = v.reshape(ref.shape[0], ref.shape[2], v.shape[1])

    for head in range(heads):
        cols = slice(head * HEAD, (head + 1) * HEAD)
        for h in range(2):
            query = rows(q_ref, h, cols)
            grad = rows(g_ref, h, cols)
            delta = jnp.sum(grad.astype(f32) * rows(o_ref, h, cols), axis=-1, keepdims=True)
            place = rows(place_ref, h)
            lse = rows(lse_ref, h, slice(head, head + 1))
            query_grad = 0.0
            for e in range(h + 1):
                key, value, kp = rows(k_ref, e, cols), rows(v_ref, e, cols), kp_ref[e]
                allowed = (kp >= place[:, 1:2]) & (kp <= place[:, 0:1])
                scores = jnp.where(allowed, dot_last(query, key) * scale, NEGATIVE)
                weights = jnp.exp(scores - lse)
                score_grad = (weights * (dot_last(grad, value) - delta) * scale).astype(bf16)
                query_grad += jnp.dot(score_grad, key, preferred_element_type=f32)
                key_part = dot_first(score_grad, query)
                value_part = dot_first(weights.astype(bf16), grad)
                if h > e:
                    key_part += acc_k[...]
                    value_part += acc_v[...]
                elif h == 0:
                    acc_k[...] = key_part
                    acc_v[...] = value_part
                    continue
                put(yk_ref, e, cols, turn_back(key_part, rows(table_ref, e)))
                put(dv_ref, e, cols, value_part.astype(bf16))
            put(yq_ref, h, cols, turn_back(query_grad, rows(table_ref, h)))


def feed_back_kernel(
    zl_ref, rows_ref, wg_ref, wu_ref, wd_ref, gate_ref, up_ref,
    gg_ref, ug_ref, own_ref, other0_ref, other1_ref, acc_ref,
):
    f32 = jnp.float32
    bf16 = jnp.bfloat16
    step = pl.program_id(0)
    half = rows_ref.shape[0] // 2
    for part in (1, 0):
        at = slice(part * half, (part + 1) * half)
        act_grad = dot_last(rows_ref[at, :], wd_ref[...])
        gate, up = gate_ref[at, :], up_ref[at, :]
        sig = jax.nn.sigmoid(gate)
        up_low = (act_grad * gate * sig).astype(bf16)
        gate_low = (act_grad * up * sig * (1.0 + gate * (1.0 - sig))).astype(bf16)
        ug_ref[at, :] = up_low
        gg_ref[at, :] = gate_low
        value = dot_last(gate_low, wg_ref[...]) + dot_last(up_low, wu_ref[...])

        @pl.when(step == 0)
        def _():
            acc_ref[at, :] = value

        @pl.when(step == 1)
        def _():
            total = (acc_ref[at, :] + value).astype(bf16)
            if part:
                other0_ref[...] = total[: half // 2]
                other1_ref[...] = total[half // 2 :]
            else:
                own_ref[...] = total


def mixed_back_kernel(zl_ref, rows_ref, weight_ref, out_ref):
    out_ref[...] = dot_last(rows_ref[...], weight_ref[...]).astype(out_ref.dtype)


def grads_kernel(count, ids_ref, features_ref, right_ref, *refs):
    value = dot_first(features_ref[...], right_ref[...])
    for ref in refs[:count]:
        value = value + ref[...].astype(jnp.float32)
    refs[count][...] = value.astype(refs[count].dtype)


def grads(features, right, ids, *terms, kind=jnp.bfloat16):
    tokens, units = right.shape
    block = features.shape[1] // 8
    count = ids.shape[0]
    return pl.pallas_call(
        lambda *refs: grads_kernel(len(terms), *refs),
        grid_spec=pltpu.PrefetchScalarGridSpec(
            num_scalar_prefetch=1,
            grid=(count,),
            in_specs=[
                pl.BlockSpec((tokens, block), lambda i, ids: (0, ids[i])),
                pl.BlockSpec((tokens, units), lambda i, ids: (0, 0)),
            ]
            + [
                pl.BlockSpec((block, units), lambda i, ids, first=first: (first + i, 0))
                for _, first in terms
            ],
            out_specs=pl.BlockSpec((block, units), lambda i, ids: (i, 0)),
        ),
        out_shape=jax.ShapeDtypeStruct((count * block, units), kind),
        compiler_params=pltpu.CompilerParams(vmem_limit_bytes=VMEM_BYTES),
        cost_estimate=pl.CostEstimate(flops=0, bytes_accessed=0, transcendentals=0),
        name="grads",
    )(ids, features, right, *(term for term, _ in terms))


def assemble_kernel(moves, *refs):
    pieces, out_ref, sems = refs[:-2], refs[-2], refs[-1]
    copies = [
        pltpu.make_async_copy(
            pieces[piece].at[pl.ds(first, rows)], out_ref.at[pl.ds(to, rows)], sems.at[index]
        )
        for index, (piece, first, rows, to) in enumerate(moves)
    ]
    for copy in copies:
        copy.start()
    for copy in copies:
        copy.wait()


def assemble(pieces, moves):
    rows = sum(move[2] for move in moves)
    return pl.pallas_call(
        lambda *refs: assemble_kernel(moves, *refs),
        in_specs=[pl.BlockSpec(memory_space=pltpu.VMEM)] * len(pieces),
        out_specs=pl.BlockSpec(memory_space=pl.ANY),
        out_shape=jax.ShapeDtypeStruct((rows, pieces[0].shape[1]), pieces[0].dtype),
        scratch_shapes=[pltpu.SemaphoreType.DMA((len(moves),))],
        compiler_params=pltpu.CompilerParams(vmem_limit_bytes=VMEM_BYTES),
        cost_estimate=pl.CostEstimate(flops=0, bytes_accessed=0, transcendentals=0),
        name="assemble",
    )(*pieces)


def both(*values):
    return lax.optimization_barrier(values)


def grouped(
    inputs,
    documents,
    query_weight,
    key_weight,
    value_weight,
    output_weight,
    query_gain,
    key_gain,
    attention_gain,
    gate_weight,
    up_weight,
    down_weight,
    feed_gain,
    cotangent,
):
    f32 = jnp.float32
    bf16 = jnp.bfloat16
    row_count, seq_count, width = inputs.shape
    half_count = 2 * row_count
    half_all = 8 * half_count
    all_count = 2 * half_all
    block = width // 8
    zh, zl, x, y, c = (lax.axis_index(name) for name in BITS)
    s = 4 * zh + 2 * zl + x
    t = 2 * y + c
    sequence = 2 * zh + x

    def swap(v, name):
        return lax.ppermute(v, name, ((0, 1), (1, 0)))

    def to_sequence(v):
        v = lax.all_to_all(jnp.transpose(v, (1, 0, 2)), ("zh", "x"), 0, 0, tiled=True)
        return v.reshape(2 * half_count, width)

    def from_sequence(v):
        v = v.astype(bf16).reshape(4, row_count, width)
        v = lax.all_to_all(v, ("zh", "x"), 0, 0, tiled=True)
        return jnp.transpose(v, (1, 0, 2)).astype(f32)

    def gather(a, late=None):
        a0, b0 = a[:half_count], a[half_count:]
        a1, b2 = both(swap(a0, "y"), swap(b0, "zl"))
        a01, b02 = jnp.concatenate([a0, a1]), jnp.concatenate([b0, b2])
        if late is None:
            a01, b02 = both(a01, b02)
        else:
            a01, b02, late = both(a01, b02, late)
        a01_c, b02_c = swap(a01, "c"), swap(b02, "c")
        a23, b13 = both(swap(a01, "zl"), swap(b02, "y"))
        a23_c, b13_c = both(swap(a23, "c"), swap(b13, "c"))
        k = half_count
        v = assemble(
            (a01, a23, b02, b13, a01_c, a23_c, b02_c, b13_c),
            [
                move
                for dc in range(2)
                for move in (
                    (4 * dc, 0, 2 * k, 8 * dc * k),
                    (4 * dc + 1, 0, 2 * k, (8 * dc + 2) * k),
                    (4 * dc + 2, 0, k, (8 * dc + 4) * k),
                    (4 * dc + 3, 0, k, (8 * dc + 5) * k),
                    (4 * dc + 2, k, k, (8 * dc + 6) * k),
                    (4 * dc + 3, k, k, (8 * dc + 7) * k),
                )
            ],
        )
        return v if late is None else (v, late)

    def swap_zy(v):
        return lax.ppermute(v, ("zl", "y"), ((0, 3), (3, 0), (1, 2), (2, 1)))

    def gather_direct(a, late):
        others = both(swap(a, "y"), swap(a, "zl"), swap_zy(a), swap(a, "c"), late)
        own, late = (a, *others[:3]), others[4]
        crossed = both(others[3], *(swap(v, "c") for v in own[1:]))
        k = half_count
        v = assemble(
            (*own, *crossed),
            [
                (4 * dc + chip, h * k, k, (8 * dc + 4 * h + chip) * k)
                for dc in range(2)
                for h in range(2)
                for chip in range(4)
            ],
        )
        return v, late

    def scatter_direct(own, *other):
        other = both(*(swap(v, "c") for v in other))
        p = [
            (v.astype(f32) + w.astype(f32)).astype(bf16)
            for v, w in zip(own.reshape(2, 4 * half_count, width), other)
        ]
        k = half_count
        mine, *sent = (
            jnp.concatenate([v[chip * k : (chip + 1) * k] for v in p]) for chip in range(4)
        )
        sent = both(swap(sent[0], "y"), swap(sent[1], "zl"), swap_zy(sent[2]))
        return sum(v.astype(f32) for v in (mine, *sent))

    def scatter(own, *other):
        a, b = own.reshape(2, 4 * half_count, width)
        a_c, b_c = both(*(swap(v, "c") for v in other))
        a = (a.astype(f32) + a_c.astype(f32)).astype(bf16).reshape(2, 2 * half_count, width)
        b = (b.astype(f32) + b_c.astype(f32)).astype(bf16).reshape(2, 2, half_count, width)
        a1, b1 = both(swap(a[1], "zl"), swap(b[:, 1], "y"))
        a = (a[0].astype(f32) + a1.astype(f32)).astype(bf16)
        b = (b[:, 0].astype(f32) + b1.astype(f32)).astype(bf16)
        a1, b1 = both(swap(a[half_count:], "y"), swap(b[1], "zl"))
        a = a[:half_count].astype(f32) + a1.astype(f32)
        b = b[0].astype(f32) + b1.astype(f32)
        return jnp.concatenate([a, b])

    def times(rows, weight, dims):
        parts = [
            jnp.einsum(dims, v, weight, preferred_element_type=f32).astype(bf16)
            for v in (rows[half_all:], rows[:half_all])
        ]
        return parts[1], *jnp.split(parts[0], 2)

    def group_sum(v, extra=None):
        for name, axis in (("c", 1), ("y", 4), ("zl", 3)):
            if extra is None:
                other = swap(v, name)
            else:
                other = swap(jnp.concatenate([v, extra]), name)
                other, other_extra = other[: v.shape[0]], other[v.shape[0] :]
                extra = extra + other_extra
            other = jnp.flip(other.reshape(-1, 2, 2, 2, 2, half_count), axis)
            v = v + other.reshape(-1, all_count)
        return v if extra is None else (v, extra)

    ids_all = (2 * zl + jnp.array([0, 0, 1, 1, 4, 4, 5, 5], jnp.int32)) ^ jnp.array(
        [0, 2] * 4, jnp.int32
    )
    ids_x, ids_zh, ids_zl = (
        s ^ jnp.array(bits, jnp.int32) for bits in ((1, 3, 5, 7), (4, 6), (0, 2))
    )

    def whole_sum(v):
        return lax.psum_scatter(v, ("zh", "x"), scatter_dimension=0, tiled=True)

    def cross_zl(kept):
        return kept[:block], swap(kept[block:], "zl")

    def finish(features, right, far, sent):
        return cross_zl(grads(features, right, ids_zl, (far, 0), (sent, 0)))

    def joined(mine, other, transposed=False):
        mine, other = mine.astype(f32), other.astype(f32)
        if transposed:
            mine, other = mine.T, other.T
        axis = 0 if transposed else 1
        return jnp.where(
            zl == 0,
            jnp.concatenate([mine, other], axis=axis),
            jnp.concatenate([other, mine], axis=axis),
        )

    def zl_half(w, axis):
        size = w.shape[axis] // 2
        return lax.dynamic_slice_in_dim(w, zl * size, size, axis)

    rows_in = to_sequence(inputs)
    weights = (
        query_weight, key_weight, value_weight, output_weight, gate_weight, up_weight, down_weight
    )
    whole, (cotangent, weights) = gather(rows_in, (cotangent, weights))
    (
        query_weight, key_weight, value_weight, output_weight, gate_weight, up_weight, down_weight
    ) = weights
    wqkv = jnp.concatenate([zl_half(w, 1) for w in (query_weight, key_weight, value_weight)], 1)
    wo = zl_half(output_weight, 0)
    wg, wu, wd = zl_half(gate_weight, 1), zl_half(up_weight, 1), zl_half(down_weight, 0)
    gq, gk = zl_half(query_gain, 0), zl_half(key_gain, 0)
    heads_width = wo.shape[0]
    heads = heads_width // HEAD

    whole, grad_top = both(whole, to_sequence(cotangent))
    grad_top = grad_top.astype(f32)

    def gathered_order(v):
        v = v.reshape(2, 2, 2, 2, 2, row_count)
        for axis, bit in ((1, zl), (3, y), (4, c)):
            v = jnp.where(bit == 1, jnp.flip(v, axis), v)
        return jnp.transpose(v, (4, 0, 1, 3, 2, 5)).reshape(all_count)

    doc_row = lax.dynamic_index_in_dim(documents, sequence, 0, keepdims=False)
    places = gathered_order(jnp.arange(all_count, dtype=jnp.int32))
    docs = gathered_order(doc_row)
    starts = jnp.sum((doc_row[None, :] < docs[:, None]).astype(jnp.int32), axis=-1)
    cosine, sine_part = rope_tables(places - starts, HEAD)
    signs = jnp.where(jnp.arange(HEAD) < HEAD // 2, -1.0, 1.0).astype(f32)

    def by_half(v):
        return v.reshape(2, 2, half_all // 2, v.shape[-1])

    table = by_half(jnp.concatenate([cosine[:, 0], sine_part[:, 0] * signs], axis=-1))
    row_places = by_half(jnp.stack([places, starts], axis=-1))
    key_places = jnp.transpose(places.reshape(2, 2, half_all // 2), (1, 0, 2))
    key_places = key_places.reshape(2, 1, half_all)
    head_gain = jnp.stack([gq, gk])

    projected = jnp.einsum("rd,dh->rh", whole, wqkv, preferred_element_type=f32)
    queries, keys_proj = projected[:, :heads_width], projected[:, heads_width : 2 * heads_width]
    sums = group_sum(
        jnp.stack([jnp.sum(queries * queries, axis=-1), jnp.sum(keys_proj * keys_proj, axis=-1)])
    )
    inverse = lax.rsqrt(sums / width + EPS).T

    def rows_shape(size, kind):
        return jax.ShapeDtypeStruct((2, 2, half_all // 2, size), kind)

    mixed_low, attended, log_total, query_low, key_low, value_low = pl.pallas_call(
        lambda *refs: attend_kernel(heads, *refs),
        out_shape=[
            rows_shape(heads_width, bf16),
            rows_shape(heads_width, f32),
            rows_shape(heads, f32),
        ]
        + [rows_shape(heads_width, bf16)] * 3,
        compiler_params=pltpu.CompilerParams(vmem_limit_bytes=VMEM_BYTES),
        cost_estimate=pl.CostEstimate(flops=0, bytes_accessed=0, transcendentals=0),
        name="attend",
    )(by_half(projected), by_half(inverse), table, row_places, key_places, head_gain)
    mixed_low = mixed_low.reshape(all_count, heads_width)

    branch = scatter(*times(mixed_low, wo, "rh,hd->rd"))
    attn_inv = rms_scale(branch)
    hidden = rows_in.astype(f32) + branch * attn_inv * attention_gain
    hidden_whole = gather(hidden.astype(bf16))
    gate_value = jnp.einsum("rd,df->rf", hidden_whole, wg, preferred_element_type=f32)
    up_value = jnp.einsum("rd,df->rf", hidden_whole, wu, preferred_element_type=f32)
    sigmoid_value = jax.nn.sigmoid(gate_value)
    act_low = (gate_value * sigmoid_value * up_value).astype(bf16)
    down_value = scatter(*times(act_low, wd, "rf,fd->rd"))
    feed_inv = rms_scale(down_value)
    down_low = norm_back(down_value, feed_inv, feed_gain, grad_top).astype(bf16)
    down_whole, late_hidden = gather(down_low, hidden)
    layer_out = from_sequence(late_hidden + down_value * feed_inv * feed_gain)
    down_whole, layer_out = both(down_whole, layer_out)

    down_part = grads(down_whole, act_low, ids_all)
    down_whole, down_part = both(down_whole, down_part)
    down_sum = whole_sum(down_part)
    tile = gate_value.shape[1] // 2
    unit_tile = pl.BlockSpec((all_count, tile), lambda j, z: (0, j))
    rows_full = pl.BlockSpec((all_count, width), lambda j, z: (0, 0))
    rows_part = pl.BlockSpec((half_all // 2, width), lambda j, z: (0, 0))
    rows_half = pl.BlockSpec((half_all, width), lambda j, z: (0, 0))
    weight_tile = pl.BlockSpec((width, tile), lambda j, z: (0, 2 * z[0] + j))
    gate_low, up_low, *hidden_part = pl.pallas_call(
        feed_back_kernel,
        grid_spec=pltpu.PrefetchScalarGridSpec(
            num_scalar_prefetch=1,
            grid=(2,),
            in_specs=[
                rows_full,
                weight_tile,
                weight_tile,
                pl.BlockSpec((tile, width), lambda j, z: (2 * z[0] + j, 0)),
                unit_tile,
                unit_tile,
            ],
            out_specs=[unit_tile, unit_tile, rows_half, rows_part, rows_part],
            scratch_shapes=[pltpu.VMEM((all_count, width), f32)],
        ),
        out_shape=[
            jax.ShapeDtypeStruct(gate_value.shape, bf16),
            jax.ShapeDtypeStruct(gate_value.shape, bf16),
            jax.ShapeDtypeStruct((half_all, width), bf16),
        ]
        + [jax.ShapeDtypeStruct((half_all // 2, width), bf16)] * 2,
        compiler_params=pltpu.CompilerParams(vmem_limit_bytes=VMEM_BYTES),
        cost_estimate=pl.CostEstimate(flops=0, bytes_accessed=0, transcendentals=0),
        name="feed_back",
    )(
        zl[None], down_whole, gate_weight, up_weight, down_weight, gate_value,
        up_value,
    )
    gate_part = grads(hidden_whole, gate_low, ids_all)
    hidden_grad = grad_top + scatter_direct(*hidden_part)
    hidden_grad, gate_part = both(hidden_grad, gate_part)
    gate_sum = whole_sum(gate_part)

    branch_low = norm_back(branch, attn_inv, attention_gain, hidden_grad).astype(bf16)
    branch_whole, late_up = gather_direct(branch_low, up_low)
    up_part = grads(hidden_whole, late_up, ids_all)
    branch_whole, up_part = both(branch_whole, up_part)
    up_sum = whole_sum(up_part)
    mixed_grad = pl.pallas_call(
        mixed_back_kernel,
        grid_spec=pltpu.PrefetchScalarGridSpec(
            num_scalar_prefetch=1,
            grid=(2,),
            in_specs=[
                pl.BlockSpec((half_all, width), lambda i, z: (i, 0)),
                pl.BlockSpec((heads_width, width), lambda i, z: (z[0], 0)),
            ],
            out_specs=pl.BlockSpec((half_all, heads_width), lambda i, z: (i, 0)),
        ),
        out_shape=jax.ShapeDtypeStruct((all_count, heads_width), bf16),
        compiler_params=pltpu.CompilerParams(vmem_limit_bytes=VMEM_BYTES),
        cost_estimate=pl.CostEstimate(flops=0, bytes_accessed=0, transcendentals=0),
        name="mixed_back",
    )(zl[None], branch_whole, output_weight)

    yq, yk, value_grad_low = pl.pallas_call(
        lambda *refs: attend_back_kernel(heads, *refs),
        out_shape=[rows_shape(heads_width, f32)] * 2 + [rows_shape(heads_width, bf16)],
        scratch_shapes=[pltpu.VMEM((half_all, HEAD), f32)] * 2,
        compiler_params=pltpu.CompilerParams(vmem_limit_bytes=VMEM_BYTES),
        cost_estimate=pl.CostEstimate(flops=0, bytes_accessed=0, transcendentals=0),
        name="attend_back",
    )(
        query_low, key_low, value_low, attended, log_total, by_half(mixed_grad), table,
        row_places, key_places,
    )
    yq, yk, value_grad_low = (
        v.reshape(all_count, heads_width) for v in (yq, yk, value_grad_low)
    )
    query_inv, key_inv = inverse[:, 0:1], inverse[:, 1:2]
    dots = jnp.stack([jnp.sum(yq * gq * queries, axis=-1), jnp.sum(yk * gk * keys_proj, axis=-1)])
    head_gains = jnp.stack(
        [jnp.sum(yq * queries * query_inv, axis=0), jnp.sum(yk * keys_proj * key_inv, axis=0)]
    )
    head_gains = lax.dynamic_update_slice(
        jnp.zeros((2, width), f32), head_gains, (0, (2 * t + zl) * heads_width)
    )
    row_gains = jnp.stack(
        [
            jnp.sum(hidden_grad * branch * attn_inv, axis=0),
            jnp.sum(grad_top * down_value * feed_inv, axis=0),
        ]
    )
    gains = jnp.concatenate([head_gains, row_gains]).reshape(-1, all_count)
    yq, late_mixed = both(yq, mixed_low)
    out_far = grads(branch_whole, late_mixed, ids_x)
    dots, gains = group_sum(dots, gains)
    dots, out_far, down_sum = both(dots, out_far, down_sum)
    out_far = swap(out_far, "x")
    down_mine, down_other = cross_zl(down_sum)
    dots = dots.T
    gains = gains.reshape(4, width)
    gains = gains + swap(gains, "x")
    query_grad_low = (
        query_inv * gq * yq - queries * query_inv**3 * (dots[:, 0:1] / width)
    ).astype(bf16)
    key_grad_low = (
        key_inv * gk * yk - keys_proj * key_inv**3 * (dots[:, 1:2] / width)
    ).astype(bf16)
    projected_grad = jnp.concatenate([query_grad_low, key_grad_low, value_grad_low], axis=1)
    input_part = times(projected_grad, wqkv, "rh,dh->rd")
    input_own, late_grad, out_far, gains, down_other = both(
        input_part[0], projected_grad, out_far, gains, down_other
    )
    in_far = swap(grads(whole, late_grad, ids_x), "x")
    gains = gains + swap(gains, "zh")
    out_sent = grads(branch_whole, late_mixed, ids_zh, (out_far, 2))
    down_term = joined(down_mine, down_other, True)
    input_sum = scatter_direct(input_own, *input_part[1:])
    input_sum, in_far, out_sent, gate_sum, down_term = both(
        input_sum, in_far, out_sent, gate_sum, down_term
    )
    in_sent = grads(whole, projected_grad, ids_zh, (in_far, 2))
    input_sum, in_sent, out_sent, gate_sum = both(input_sum, in_sent, out_sent, gate_sum)
    in_sent, out_sent = swap(in_sent, "zh"), swap(out_sent, "zh")
    gate_mine, gate_other = cross_zl(gate_sum)
    gate_term = joined(gate_mine, gate_other)
    in_sent, gate_term, input_sum = both(in_sent, gate_term, input_sum)
    in_mine, in_other = finish(whole, projected_grad, in_far, in_sent)
    out_sent, in_mine = both(out_sent, in_mine)
    out_mine, out_other = finish(branch_whole, mixed_low, out_far, out_sent)
    out_term = joined(out_mine, out_other, True)
    up_pair = cross_zl(up_sum)
    input_grad = from_sequence(hidden_grad + input_sum)
    gains = lax.dynamic_slice_in_dim(gains, s * block, block, 1)
    up_term = joined(*up_pair)
    query_term, key_term, value_term = (
        joined(
            in_mine[:, k * heads_width : (k + 1) * heads_width],
            in_other[:, k * heads_width : (k + 1) * heads_width],
        )
        for k in range(3)
    )
    return (
        layer_out,
        input_grad,
        query_term,
        key_term,
        value_term,
        out_term,
        gate_term,
        up_term,
        down_term,
        gains[0],
        gains[1],
        gains[2],
        gains[3],
    )


def solution(mesh):
    rows, columns, inner = ("seq", "tp"), ("tp",), ("seq",)
    step = local
    if mesh.shape["seq"] == 8 and mesh.shape["tp"] == 4:
        mesh = Mesh(mesh.devices.reshape(2, 2, 2, 2, 2), BITS)
        rows, columns, inner = BITS, BITS[3:], BITS[:3]
        step = grouped
    return jax.shard_map(
        step,
        mesh=mesh,
        in_specs=(
            P(rows, None, None),
            P(),
            P(None, columns),
            P(None, columns),
            P(None, columns),
            P(columns, None),
            P(columns),
            P(columns),
            P(),
            P(None, columns),
            P(None, columns),
            P(columns, None),
            P(),
            P(rows, None, None),
        ),
        out_specs=(
            P(rows, None, None),
            P(rows, None, None),
            P(inner, columns),
            P(inner, columns),
            P(inner, columns),
            P(columns, inner),
            P(inner, columns),
            P(inner, columns),
            P(columns, inner),
            P(inner),
            P(inner),
            P(inner),
            P(inner),
        ),
        check_vma=False,
    )
```

```python
import jax
import jax.numpy as jnp
from jax import lax
from jax.experimental.layout import Layout, with_layout_constraint
from jax.experimental import pallas as pl
from jax.experimental.pallas import tpu as pltpu
from jax.sharding import Mesh
from jax.sharding import PartitionSpec as P

HEAD = 128


EPS = 1e-06
THETA = 500000.0
NEGATIVE = -1e30


def rope_tables(positions, head_size):
    half_size = head_size // 2
    rates = jnp.exp(-jnp.log(THETA) * (2.0 * jnp.arange(half_size, dtype=jnp.float32) / head_size))
    angles = positions.astype(jnp.float32)[..., None] * rates
    cosine = jnp.cos(angles)
    sine_part = jnp.sin(angles)
    return (
        jnp.concatenate([cosine, cosine], axis=-1)[..., None, :],
        jnp.concatenate([sine_part, sine_part], axis=-1)[..., None, :],
    )


def rotate(tensor, cosine, sine_part):
    half_size = tensor.shape[-1] // 2
    turned = jnp.concatenate([-tensor[..., half_size:], tensor[..., :half_size]], axis=-1)
    return tensor * cosine + turned * sine_part


def unrotate(grad_in, cosine, sine_part):
    half_size = grad_in.shape[-1] // 2
    scaled = grad_in * sine_part
    return grad_in * cosine + jnp.concatenate(
        [scaled[..., half_size:], -scaled[..., :half_size]], axis=-1
    )


def rms_scale(tensor):
    return lax.rsqrt(jnp.mean(tensor * tensor, axis=-1, keepdims=True) + EPS)


def norm_back(tensor, inverse, gain, grad_in):
    weighted = grad_in * gain
    return inverse * weighted - tensor * inverse**3 * jnp.mean(
        weighted * tensor, axis=-1, keepdims=True
    )


def cycle_values(key_low, value_low):
    return (
        lax.all_gather(jnp.transpose(key_low, (1, 0, 2)), "seq", axis=1, tiled=True),
        lax.all_gather(jnp.transpose(value_low, (1, 0, 2)), "seq", axis=1, tiled=True),
    )


def allowed_mask(query_docs, key_docs, query_first, key_first):
    query_places = query_first + jnp.arange(query_docs.shape[0], dtype=jnp.int32)
    key_places = key_first + jnp.arange(key_docs.shape[0], dtype=jnp.int32)
    return (query_docs[:, None] == key_docs[None, :]) & (
        key_places[None, :] <= query_places[:, None]
    )


def local(
    inputs,
    documents,
    query_weight,
    key_weight,
    value_weight,
    output_weight,
    query_gain,
    key_gain,
    attention_gain,
    gate_weight,
    up_weight,
    down_weight,
    feed_gain,
    cotangent,
):
    row_count, seq_count, model_width = inputs.shape
    heads_width = query_weight.shape[1]
    local_heads = heads_width // HEAD
    score_scale = HEAD ** (-0.5)
    seq_index = lax.axis_index("seq")
    tp_index = lax.axis_index("tp")
    total_length = documents.shape[1]
    f32 = jnp.float32
    bf16 = jnp.bfloat16
    whole = lax.all_gather(inputs, "tp", axis=0, tiled=True)
    here_length = whole.shape[0]
    queries = jnp.einsum("tsd,dh->tsh", whole, query_weight, preferred_element_type=f32)
    keys_proj = jnp.einsum("tsd,dh->tsh", whole, key_weight, preferred_element_type=f32)
    values_proj = jnp.einsum("tsd,dh->tsh", whole, value_weight, preferred_element_type=f32)
    query_sq, key_sq = lax.psum(
        (jnp.sum(queries * queries, axis=-1), jnp.sum(keys_proj * keys_proj, axis=-1)), "tp"
    )
    query_inv = lax.rsqrt(query_sq / model_width + EPS)[..., None]
    key_inv = lax.rsqrt(key_sq / model_width + EPS)[..., None]
    first_row = seq_index * here_length
    own_docs = lax.dynamic_slice_in_dim(documents, first_row, here_length, 1)
    starts = jnp.sum((documents[:, None, :] < own_docs[:, :, None]).astype(jnp.int32), axis=-1)
    positions = (first_row + jnp.arange(here_length, dtype=jnp.int32))[:, None] - starts.T
    cosine, sine_part = rope_tables(positions, HEAD)

    def heads_of(tensor):
        return tensor.reshape(here_length, seq_count, local_heads, HEAD)

    query_low = rotate(heads_of(queries * query_inv * query_gain), cosine, sine_part).astype(bf16)
    key_low = rotate(heads_of(keys_proj * key_inv * key_gain), cosine, sine_part).astype(bf16)
    key_low = key_low.reshape(here_length, seq_count, heads_width)
    value_low = values_proj.astype(bf16)
    key_cycle, value_cycle = cycle_values(key_low, value_low)
    query_seq = jnp.transpose(query_low, (1, 0, 2, 3))

    def keys_in_reach(key_part, value_part):
        return (
            key_part.reshape(total_length, local_heads, HEAD),
            value_part.reshape(total_length, local_heads, HEAD),
        )

    def scores_of(query_part, key_heads, query_docs, key_docs, first_query, first_key):
        scores = (
            jnp.einsum("qhd,khd->hqk", query_part, key_heads, preferred_element_type=f32)
            * score_scale
        )
        return jnp.where(
            allowed_mask(query_docs, key_docs, first_query, first_key)[None], scores, NEGATIVE
        )

    def attend(pieces):
        query_part, key_part, value_part, own_part, doc_row = pieces
        key_heads, value_heads = keys_in_reach(key_part, value_part)
        scores = scores_of(query_part, key_heads, own_part, doc_row, first_row, 0)
        top_score = jnp.max(scores, axis=-1, keepdims=True)
        spread = jnp.exp(scores - top_score)
        total_sum = jnp.sum(spread, axis=-1, keepdims=True)
        weights = (spread / total_sum).astype(bf16)
        mixed_part = jnp.einsum("hqk,khd->qhd", weights, value_heads, preferred_element_type=f32)
        return (mixed_part, (top_score + jnp.log(total_sum))[..., 0])

    attended, log_total = lax.map(attend, (query_seq, key_cycle, value_cycle, own_docs, documents))
    mixed_low = (
        jnp.transpose(attended, (1, 0, 2, 3))
        .reshape(here_length, seq_count, heads_width)
        .astype(bf16)
    )
    part = mixed_low
    branch = lax.psum_scatter(
        jnp.einsum("tsh,hd->tsd", part, output_weight, preferred_element_type=f32).astype(
            jnp.bfloat16
        ),
        "tp",
        scatter_dimension=0,
        tiled=True,
    ).astype(jnp.float32)
    attn_inv = rms_scale(branch)
    hidden = inputs.astype(f32) + branch * attn_inv * attention_gain
    hidden_whole = lax.all_gather(hidden.astype(bf16), "tp", axis=0, tiled=True)
    gate_value = jnp.einsum("tsd,df->tsf", hidden_whole, gate_weight, preferred_element_type=f32)
    up_value = jnp.einsum("tsd,df->tsf", hidden_whole, up_weight, preferred_element_type=f32)
    sigmoid_value = jax.nn.sigmoid(gate_value)
    act_low = (gate_value * sigmoid_value * up_value).astype(bf16)
    part = act_low
    down_value = lax.psum_scatter(
        jnp.einsum("tsf,fd->tsd", part, down_weight, preferred_element_type=f32).astype(
            jnp.bfloat16
        ),
        "tp",
        scatter_dimension=0,
        tiled=True,
    ).astype(jnp.float32)
    feed_inv = rms_scale(down_value)
    layer_out = hidden + down_value * feed_inv * feed_gain
    grad_top = cotangent.astype(f32)
    feed_gain_term = jnp.sum(grad_top * down_value * feed_inv, axis=(0, 1))
    down_grad_low = norm_back(down_value, feed_inv, feed_gain, grad_top).astype(bf16)
    down_whole = lax.all_gather(down_grad_low, "tp", axis=0, tiled=True)
    act_grad = jnp.einsum("tsd,fd->tsf", down_whole, down_weight, preferred_element_type=f32)
    down_term = jnp.einsum("tsd,tsf->df", down_whole, act_low, preferred_element_type=f32)
    up_grad_low = (act_grad * gate_value * sigmoid_value).astype(bf16)
    gate_grad_low = (
        act_grad * up_value * sigmoid_value * (1.0 + gate_value * (1.0 - sigmoid_value))
    ).astype(bf16)
    gate_term = jnp.einsum("tsd,tsf->df", hidden_whole, gate_grad_low, preferred_element_type=f32)
    up_term = jnp.einsum("tsd,tsf->df", hidden_whole, up_grad_low, preferred_element_type=f32)
    hidden_grad = grad_top + lax.psum_scatter(
        (
            jnp.einsum("tsf,df->tsd", gate_grad_low, gate_weight, preferred_element_type=f32)
            + jnp.einsum("tsf,df->tsd", up_grad_low, up_weight, preferred_element_type=f32)
        ).astype(jnp.bfloat16),
        "tp",
        scatter_dimension=0,
        tiled=True,
    ).astype(jnp.float32)
    attention_gain_term = jnp.sum(hidden_grad * branch * attn_inv, axis=(0, 1))
    branch_grad_low = norm_back(branch, attn_inv, attention_gain, hidden_grad).astype(bf16)
    branch_whole = lax.all_gather(branch_grad_low, "tp", axis=0, tiled=True)
    out_term = jnp.einsum("tsd,tsh->dh", branch_whole, mixed_low, preferred_element_type=f32)
    mixed_grad_low = jnp.einsum(
        "tsd,hd->tsh", branch_whole, output_weight, preferred_element_type=f32
    ).astype(bf16)
    grad_seq = jnp.transpose(
        mixed_grad_low.reshape(here_length, seq_count, local_heads, HEAD), (1, 0, 2, 3)
    )
    delta_own = jnp.transpose(jnp.sum(grad_seq.astype(f32) * attended, axis=-1), (0, 2, 1))
    key_cycle, value_cycle = cycle_values(key_low, value_low)

    def query_back(pieces):
        query_part, key_part, value_part, own_part, doc_row, grad_part, log_part, delta_part = (
            pieces
        )
        key_heads, value_heads = keys_in_reach(key_part, value_part)
        scores = scores_of(query_part, key_heads, own_part, doc_row, first_row, 0)
        weights = jnp.exp(scores - log_part[..., None])
        weight_grad = jnp.einsum("qhd,khd->hqk", grad_part, value_heads, preferred_element_type=f32)
        score_grad = (weights * (weight_grad - delta_part[:, :, None]) * score_scale).astype(bf16)
        query_grad = jnp.einsum("hqk,khd->qhd", score_grad, key_heads, preferred_element_type=f32)
        key_grad = jnp.einsum("hqk,qhd->khd", score_grad, query_part, preferred_element_type=f32)
        value_grad = jnp.einsum(
            "hqk,qhd->khd", weights.astype(bf16), grad_part, preferred_element_type=f32
        )
        return (
            query_grad,
            key_grad.reshape(total_length, heads_width),
            value_grad.reshape(total_length, heads_width),
        )

    query_grads, key_full, value_full = lax.map(
        query_back,
        (query_seq, key_cycle, value_cycle, own_docs, documents, grad_seq, log_total, delta_own),
    )
    key_own, value_own = (
        lax.psum_scatter(
            key_full.astype(jnp.bfloat16), "seq", scatter_dimension=1, tiled=True
        ).astype(jnp.float32),
        lax.psum_scatter(
            value_full.astype(jnp.bfloat16), "seq", scatter_dimension=1, tiled=True
        ).astype(jnp.float32),
    )
    value_grad_low = jnp.transpose(value_own, (1, 0, 2)).astype(bf16)
    query_rot = unrotate(jnp.transpose(query_grads, (1, 0, 2, 3)), cosine, sine_part)
    query_rot = query_rot.reshape(here_length, seq_count, heads_width)
    key_rot = unrotate(heads_of(jnp.transpose(key_own, (1, 0, 2))), cosine, sine_part)
    key_rot = key_rot.reshape(here_length, seq_count, heads_width)
    query_gain_term = jnp.sum(query_rot * queries * query_inv, axis=(0, 1))
    key_gain_term = jnp.sum(key_rot * keys_proj * key_inv, axis=(0, 1))

    def placed(term):
        return lax.dynamic_update_slice(
            jnp.zeros((model_width,), f32), term, (tp_index * heads_width,)
        )

    query_dot, key_dot, query_gain_sum, key_gain_sum, attention_gain_sum, feed_gain_sum = (
        lax.psum(
            jnp.sum(query_rot * query_gain * queries, axis=-1).astype(jnp.bfloat16), "tp"
        ).astype(jnp.float32),
        lax.psum(
            jnp.sum(key_rot * key_gain * keys_proj, axis=-1).astype(jnp.bfloat16), "tp"
        ).astype(jnp.float32),
        lax.psum(placed(query_gain_term).astype(jnp.bfloat16), "tp").astype(jnp.float32),
        lax.psum(placed(key_gain_term).astype(jnp.bfloat16), "tp").astype(jnp.float32),
        lax.psum(attention_gain_term.astype(jnp.bfloat16), "tp").astype(jnp.float32),
        lax.psum(feed_gain_term.astype(jnp.bfloat16), "tp").astype(jnp.float32),
    )
    query_grad_low = (
        query_inv * query_gain * query_rot
        - queries * query_inv**3 * (query_dot / model_width)[..., None]
    ).astype(bf16)
    key_grad_low = (
        key_inv * key_gain * key_rot - keys_proj * key_inv**3 * (key_dot / model_width)[..., None]
    ).astype(bf16)
    query_term = jnp.einsum("tsd,tsh->dh", whole, query_grad_low, preferred_element_type=f32)
    key_term = jnp.einsum("tsd,tsh->dh", whole, key_grad_low, preferred_element_type=f32)
    value_term = jnp.einsum("tsd,tsh->dh", whole, value_grad_low, preferred_element_type=f32)
    query_part = query_grad_low
    key_part = key_grad_low
    value_part = value_grad_low
    input_grad = hidden_grad + lax.psum_scatter(
        (
            jnp.einsum("tsh,dh->tsd", query_part, query_weight, preferred_element_type=f32)
            + jnp.einsum("tsh,dh->tsd", key_part, key_weight, preferred_element_type=f32)
            + jnp.einsum("tsh,dh->tsd", value_part, value_weight, preferred_element_type=f32)
        ).astype(jnp.bfloat16),
        "tp",
        scatter_dimension=0,
        tiled=True,
    ).astype(jnp.float32)
    summed = (
        lax.psum_scatter(
            query_term.astype(jnp.bfloat16), "seq", scatter_dimension=0, tiled=True
        ).astype(jnp.float32),
        lax.psum_scatter(
            key_term.astype(jnp.bfloat16), "seq", scatter_dimension=0, tiled=True
        ).astype(jnp.float32),
        lax.psum_scatter(
            value_term.astype(jnp.bfloat16), "seq", scatter_dimension=0, tiled=True
        ).astype(jnp.float32),
        lax.psum_scatter(
            out_term.astype(jnp.bfloat16), "seq", scatter_dimension=0, tiled=True
        ).astype(jnp.float32),
        lax.psum_scatter(
            gate_term.astype(jnp.bfloat16), "seq", scatter_dimension=0, tiled=True
        ).astype(jnp.float32),
        lax.psum_scatter(
            up_term.astype(jnp.bfloat16), "seq", scatter_dimension=0, tiled=True
        ).astype(jnp.float32),
        lax.psum_scatter(
            down_term.astype(jnp.bfloat16), "seq", scatter_dimension=0, tiled=True
        ).astype(jnp.float32),
        lax.psum_scatter(
            query_gain_sum.astype(jnp.bfloat16), "seq", scatter_dimension=0, tiled=True
        ).astype(jnp.float32),
        lax.psum_scatter(
            key_gain_sum.astype(jnp.bfloat16), "seq", scatter_dimension=0, tiled=True
        ).astype(jnp.float32),
        lax.psum_scatter(
            attention_gain_sum.astype(jnp.bfloat16), "seq", scatter_dimension=0, tiled=True
        ).astype(jnp.float32),
        lax.psum_scatter(
            feed_gain_sum.astype(jnp.bfloat16), "seq", scatter_dimension=0, tiled=True
        ).astype(jnp.float32),
    )
    return (
        layer_out,
        input_grad,
        summed[0],
        summed[1],
        summed[2],
        summed[3].T,
        summed[4],
        summed[5],
        summed[6].T,
        summed[7],
        summed[8],
        summed[9],
        summed[10],
    )


VMEM_BYTES = 56 * 2**20
BITS = ("zh", "zl", "x", "y", "c")


def turn(v, table):
    return v * table[:, :HEAD] + pltpu.roll(v, HEAD // 2, 1) * table[:, HEAD:]


def turn_back(g, table):
    return g * table[:, :HEAD] - pltpu.roll(g, HEAD // 2, 1) * table[:, HEAD:]


def dot_last(left, right):
    return lax.dot_general(
        left, right, (((1,), (1,)), ((), ())), preferred_element_type=jnp.float32
    )


def dot_first(left, right):
    return lax.dot_general(
        left, right, (((0,), (0,)), ((), ())), preferred_element_type=jnp.float32
    )


def attend_kernel(
    heads, proj_ref, inv_ref, table_ref, place_ref, kp_ref, gain_ref,
    mixed_ref, o_ref, lse_ref, q_ref, k_ref, v_ref,
):
    bf16 = jnp.bfloat16
    width = heads * HEAD
    scale = HEAD ** (-0.5)

    def rows(ref, h, cols=slice(None)):
        v = ref[:, h, :, cols]
        return v.reshape(v.shape[0] * v.shape[1], v.shape[2])

    def put(ref, h, cols, v):
        ref[:, h, :, cols] = v.reshape(ref.shape[0], ref.shape[2], v.shape[1])

    for h in range(2):
        table = rows(table_ref, h)
        inv = rows(inv_ref, h)
        place = rows(place_ref, h)
        masks = [
            (kp_ref[e] >= place[:, 1:2]) & (kp_ref[e] <= place[:, 0:1]) for e in range(h + 1)
        ]
        for head in range(heads):
            cols = slice(head * HEAD, (head + 1) * HEAD)
            key_cols = slice(width + head * HEAD, width + (head + 1) * HEAD)
            value_cols = slice(2 * width + head * HEAD, 2 * width + (head + 1) * HEAD)
            query = turn(rows(proj_ref, h, cols) * inv[:, 0:1] * gain_ref[0:1, cols], table)
            key = turn(rows(proj_ref, h, key_cols) * inv[:, 1:2] * gain_ref[1:2, cols], table)
            query = query.astype(bf16)
            put(q_ref, h, cols, query)
            put(k_ref, h, cols, key.astype(bf16))
            put(v_ref, h, cols, rows(proj_ref, h, value_cols).astype(bf16))
            scores = [
                jnp.where(masks[e], dot_last(query, rows(k_ref, e, cols)), NEGATIVE)
                for e in range(h + 1)
            ]
            top = scores[0].max(axis=-1, keepdims=True)
            if h:
                top = jnp.maximum(top, scores[1].max(axis=-1, keepdims=True))
            spread = [jnp.exp((v - top) * scale) for v in scores]
            total = sum(v.sum(axis=-1, keepdims=True) for v in spread)
            mixed = sum(
                jnp.dot(p.astype(bf16), rows(v_ref, e, cols), preferred_element_type=jnp.float32)
                for e, p in enumerate(spread)
            )
            mixed = mixed / total
            put(o_ref, h, cols, mixed)
            put(mixed_ref, h, cols, mixed.astype(bf16))
            put(lse_ref, h, slice(head, head + 1), top * scale + jnp.log(total))


def attend_back_kernel(
    heads, q_ref, k_ref, v_ref, o_ref, lse_ref, g_ref, table_ref, place_ref, kp_ref,
    yq_ref, yk_ref, dv_ref, acc_k, acc_v,
):
    f32 = jnp.float32
    bf16 = jnp.bfloat16
    scale = HEAD ** (-0.5)

    def rows(ref, h, cols=slice(None)):
        v = ref[:, h, :, cols]
        return v.reshape(v.shape[0] * v.shape[1], v.shape[2])

    def put(ref, h, cols, v):
        ref[:, h, :, cols] = v.reshape(ref.shape[0], ref.shape[2], v.shape[1])

    for head in range(heads):
        cols = slice(head * HEAD, (head + 1) * HEAD)
        for h in range(2):
            query = rows(q_ref, h, cols)
            grad = rows(g_ref, h, cols)
            delta = jnp.sum(grad.astype(f32) * rows(o_ref, h, cols), axis=-1, keepdims=True)
            place = rows(place_ref, h)
            lse = rows(lse_ref, h, slice(head, head + 1))
            query_grad = 0.0
            for e in range(h + 1):
                key, value, kp = rows(k_ref, e, cols), rows(v_ref, e, cols), kp_ref[e]
                allowed = (kp >= place[:, 1:2]) & (kp <= place[:, 0:1])
                scores = jnp.where(allowed, dot_last(query, key) * scale, NEGATIVE)
                weights = jnp.exp(scores - lse)
                score_grad = (weights * (dot_last(grad, value) - delta) * scale).astype(bf16)
                query_grad += jnp.dot(score_grad, key, preferred_element_type=f32)
                key_part = dot_first(score_grad, query)
                value_part = dot_first(weights.astype(bf16), grad)
                if h > e:
                    key_part += acc_k[...]
                    value_part += acc_v[...]
                elif h == 0:
                    acc_k[...] = key_part
                    acc_v[...] = value_part
                    continue
                put(yk_ref, e, cols, turn_back(key_part, rows(table_ref, e)))
                put(dv_ref, e, cols, value_part.astype(bf16))
            put(yq_ref, h, cols, turn_back(query_grad, rows(table_ref, h)))


def feed_back_kernel(
    zl_ref, rows_ref, wg_ref, wu_ref, wd_ref, gate_ref, up_ref,
    gg_ref, ug_ref, own_ref, other0_ref, other1_ref, acc_ref,
):
    f32 = jnp.float32
    bf16 = jnp.bfloat16
    step = pl.program_id(0)
    half = rows_ref.shape[0] // 2
    for part in (1, 0):
        at = slice(part * half, (part + 1) * half)
        act_grad = dot_last(rows_ref[at, :], wd_ref[...])
        gate, up = gate_ref[at, :].astype(f32), up_ref[at, :].astype(f32)
        sig = jax.nn.sigmoid(gate)
        up_low = (act_grad * gate * sig).astype(bf16)
        gate_low = (act_grad * up * sig * (1.0 + gate * (1.0 - sig))).astype(bf16)
        ug_ref[at, :] = up_low
        gg_ref[at, :] = gate_low
        value = dot_last(gate_low, wg_ref[...]) + dot_last(up_low, wu_ref[...])

        @pl.when(step == 0)
        def _():
            acc_ref[at, :] = value

        @pl.when(step == 1)
        def _():
            total = (acc_ref[at, :] + value).astype(bf16)
            if part:
                other0_ref[...] = total[: half // 2]
                other1_ref[...] = total[half // 2 :]
            else:
                own_ref[...] = total


def mixed_back_kernel(zl_ref, rows_ref, weight_ref, out_ref):
    out_ref[...] = dot_last(rows_ref[...], weight_ref[...]).astype(out_ref.dtype)


def grads_kernel(count, ids_ref, features_ref, right_ref, *refs):
    value = dot_first(features_ref[...], right_ref[...])
    for ref in refs[:count]:
        value = value + ref[...].astype(jnp.float32)
    refs[count][...] = value.astype(refs[count].dtype)


def grads(features, right, ids, *terms, kind=jnp.bfloat16):
    tokens, units = right.shape
    block = features.shape[1] // 8
    count = ids.shape[0]
    return pl.pallas_call(
        lambda *refs: grads_kernel(len(terms), *refs),
        grid_spec=pltpu.PrefetchScalarGridSpec(
            num_scalar_prefetch=1,
            grid=(count,),
            in_specs=[
                pl.BlockSpec((tokens, block), lambda i, ids: (0, ids[i])),
                pl.BlockSpec((tokens, units), lambda i, ids: (0, 0)),
            ]
            + [
                pl.BlockSpec((block, units), lambda i, ids, first=first: (first + i, 0))
                for _, first in terms
            ],
            out_specs=pl.BlockSpec((block, units), lambda i, ids: (i, 0)),
        ),
        out_shape=jax.ShapeDtypeStruct((count * block, units), kind),
        compiler_params=pltpu.CompilerParams(vmem_limit_bytes=VMEM_BYTES),
        cost_estimate=pl.CostEstimate(flops=0, bytes_accessed=0, transcendentals=0),
        name="grads",
    )(ids, features, right, *(term for term, _ in terms))


def assemble_kernel(moves, *refs):
    pieces, out_ref, sems = refs[:-2], refs[-2], refs[-1]
    copies = [
        pltpu.make_async_copy(
            pieces[piece].at[pl.ds(first, rows)], out_ref.at[pl.ds(to, rows)], sems.at[index]
        )
        for index, (piece, first, rows, to) in enumerate(moves)
    ]
    for copy in copies:
        copy.start()
    for copy in copies:
        copy.wait()


def assemble(pieces, moves):
    rows = sum(move[2] for move in moves)
    return pl.pallas_call(
        lambda *refs: assemble_kernel(moves, *refs),
        in_specs=[pl.BlockSpec(memory_space=pltpu.VMEM)] * len(pieces),
        out_specs=pl.BlockSpec(memory_space=pl.ANY),
        out_shape=jax.ShapeDtypeStruct((rows, pieces[0].shape[1]), pieces[0].dtype),
        scratch_shapes=[pltpu.SemaphoreType.DMA((len(moves),))],
        compiler_params=pltpu.CompilerParams(vmem_limit_bytes=VMEM_BYTES),
        cost_estimate=pl.CostEstimate(flops=0, bytes_accessed=0, transcendentals=0),
        name="assemble",
    )(*pieces)


def both(*values):
    return lax.optimization_barrier(values)


def grouped(
    inputs,
    documents,
    query_weight,
    key_weight,
    value_weight,
    output_weight,
    query_gain,
    key_gain,
    attention_gain,
    gate_weight,
    up_weight,
    down_weight,
    feed_gain,
    cotangent,
):
    f32 = jnp.float32
    bf16 = jnp.bfloat16
    row_count, seq_count, width = inputs.shape
    half_count = 2 * row_count
    half_all = 8 * half_count
    all_count = 2 * half_all
    block = width // 8
    zh, zl, x, y, c = (lax.axis_index(name) for name in BITS)
    s = 4 * zh + 2 * zl + x
    t = 2 * y + c
    sequence = 2 * zh + x

    def swap(v, name):
        return lax.ppermute(v, name, ((0, 1), (1, 0)))

    def to_sequence(v):
        v = lax.all_to_all(jnp.transpose(v, (1, 0, 2)), ("zh", "x"), 0, 0, tiled=True)
        return v.reshape(2 * half_count, width)

    def from_sequence(v):
        v = v.astype(bf16).reshape(4, row_count, width)
        v = lax.all_to_all(v, ("zh", "x"), 0, 0, tiled=True)
        return jnp.transpose(v, (1, 0, 2)).astype(f32)

    def swap_zhx(v):
        return lax.ppermute(v, ("zh", "x"), ((0, 3), (3, 0), (1, 2), (2, 1)))

    def from_sequence_direct(v):
        v = v.astype(bf16).reshape(4, row_count, width)
        p = [lax.dynamic_index_in_dim(v, sequence ^ k, 0, keepdims=False) for k in range(4)]
        p = jnp.stack([p[0], swap(p[1], "x"), swap(p[2], "zh"), swap_zhx(p[3])])
        p = [lax.dynamic_index_in_dim(p, sequence ^ k, 0, keepdims=False) for k in range(4)]
        return jnp.stack(p, axis=1).astype(f32)

    def gather(a, late=None):
        a0, b0 = a[:half_count], a[half_count:]
        a1, b2 = both(swap(a0, "y"), swap(b0, "zl"))
        a01, b02 = jnp.concatenate([a0, a1]), jnp.concatenate([b0, b2])
        if late is None:
            a01, b02 = both(a01, b02)
        else:
            a01, b02, late = both(a01, b02, late)
        a01_c, b02_c = swap(a01, "c"), swap(b02, "c")
        a23, b13 = both(swap(a01, "zl"), swap(b02, "y"))
        a23_c, b13_c = both(swap(a23, "c"), swap(b13, "c"))
        k = half_count
        v = assemble(
            (a01, a23, b02, b13, a01_c, a23_c, b02_c, b13_c),
            [
                move
                for dc in range(2)
                for move in (
                    (4 * dc, 0, 2 * k, 8 * dc * k),
                    (4 * dc + 1, 0, 2 * k, (8 * dc + 2) * k),
                    (4 * dc + 2, 0, k, (8 * dc + 4) * k),
                    (4 * dc + 3, 0, k, (8 * dc + 5) * k),
                    (4 * dc + 2, k, k, (8 * dc + 6) * k),
                    (4 * dc + 3, k, k, (8 * dc + 7) * k),
                )
            ],
        )
        return v if late is None else (v, late)

    def swap_zy(v):
        return lax.ppermute(v, ("zl", "y"), ((0, 3), (3, 0), (1, 2), (2, 1)))

    def gather_direct(a, late):
        others = both(swap(a, "y"), swap(a, "zl"), swap_zy(a), swap(a, "c"), late)
        own, late = (a, *others[:3]), others[4]
        crossed = both(others[3], *(swap(v, "c") for v in own[1:]))
        k = half_count
        v = assemble(
            (*own, *crossed),
            [
                (4 * dc + chip, h * k, k, (8 * dc + 4 * h + chip) * k)
                for dc in range(2)
                for h in range(2)
                for chip in range(4)
            ],
        )
        return v, late

    def scatter_direct(own, *other, late=None):
        *other, late = both(*(swap(v, "c") for v in other), 0.0 if late is None else late)
        p = [
            (v.astype(f32) + w.astype(f32)).astype(bf16)
            for v, w in zip(own.reshape(2, 4 * half_count, width), other)
        ]
        k = half_count
        mine, *sent = (
            jnp.concatenate([v[chip * k : (chip + 1) * k] for v in p]) for chip in range(4)
        )
        sent = both(swap(sent[0], "y"), swap(sent[1], "zl"), swap_zy(sent[2]))
        v = sum(v.astype(f32) for v in (mine, *sent))
        return v, late

    def scatter(own, *other):
        a, b = own.reshape(2, 4 * half_count, width)
        a_c, b_c = both(*(swap(v, "c") for v in other))
        a = (a.astype(f32) + a_c.astype(f32)).astype(bf16).reshape(2, 2 * half_count, width)
        b = (b.astype(f32) + b_c.astype(f32)).astype(bf16).reshape(2, 2, half_count, width)
        a1, b1 = both(swap(a[1], "zl"), swap(b[:, 1], "y"))
        a = (a[0].astype(f32) + a1.astype(f32)).astype(bf16)
        b = (b[:, 0].astype(f32) + b1.astype(f32)).astype(bf16)
        a1, b1 = both(swap(a[half_count:], "y"), swap(b[1], "zl"))
        a = a[:half_count].astype(f32) + a1.astype(f32)
        b = b[0].astype(f32) + b1.astype(f32)
        return jnp.concatenate([a, b])

    def times(rows, weight, dims):
        parts = [
            jnp.einsum(dims, v, weight, preferred_element_type=f32).astype(bf16)
            for v in (rows[half_all:], rows[:half_all])
        ]
        return parts[1], *jnp.split(parts[0], 2)

    def group_sum(v, extra=None):
        for name, axis in (("c", 1), ("y", 4), ("zl", 3)):
            if extra is None:
                other = swap(v, name)
            else:
                other = swap(jnp.concatenate([v, extra]), name)
                other, other_extra = other[: v.shape[0]], other[v.shape[0] :]
                extra = extra + other_extra
            other = jnp.flip(other.reshape(-1, 2, 2, 2, 2, half_count), axis)
            v = v + other.reshape(-1, all_count)
        return v if extra is None else (v, extra)

    ids_all = (2 * zl + jnp.array([0, 0, 1, 1, 4, 4, 5, 5], jnp.int32)) ^ jnp.array(
        [0, 2] * 4, jnp.int32
    )
    ids_x, ids_zh, ids_zl = (
        s ^ jnp.array(bits, jnp.int32) for bits in ((1, 3, 5, 7), (4, 6), (0, 2))
    )

    def whole_sum(v):
        return lax.psum_scatter(v, ("zh", "x"), scatter_dimension=0, tiled=True)

    def cross_zl(kept):
        return kept[:block], swap(kept[block:], "zl")

    def finish(features, right, far, sent):
        return cross_zl(grads(features, right, ids_zl, (far, 0), (sent, 0)))

    def joined(mine, other, transposed=False):
        mine, other = mine.astype(f32), other.astype(f32)
        if transposed:
            mine, other = mine.T, other.T
        axis = 0 if transposed else 1
        return jnp.where(
            zl == 0,
            jnp.concatenate([mine, other], axis=axis),
            jnp.concatenate([other, mine], axis=axis),
        )

    def zl_half(w, axis):
        size = w.shape[axis] // 2
        return lax.dynamic_slice_in_dim(w, zl * size, size, axis)

    rows_in = to_sequence(inputs)
    weights = (
        query_weight, key_weight, value_weight, output_weight, gate_weight, up_weight, down_weight
    )
    whole, (cotangent, weights) = gather(rows_in, (cotangent, weights))
    (
        query_weight, key_weight, value_weight, output_weight, gate_weight, up_weight, down_weight
    ) = weights
    wqkv = jnp.concatenate([zl_half(w, 1) for w in (query_weight, key_weight, value_weight)], 1)
    wo = zl_half(output_weight, 0)
    wg, wu, wd = zl_half(gate_weight, 1), zl_half(up_weight, 1), zl_half(down_weight, 0)
    gq, gk = zl_half(query_gain, 0), zl_half(key_gain, 0)
    heads_width = wo.shape[0]
    heads = heads_width // HEAD

    whole, grad_top = both(whole, to_sequence(cotangent))
    grad_top = grad_top.astype(f32)

    def gathered_order(v):
        v = v.reshape(2, 2, 2, 2, 2, row_count)
        for axis, bit in ((1, zl), (3, y), (4, c)):
            v = jnp.where(bit == 1, jnp.flip(v, axis), v)
        return jnp.transpose(v, (4, 0, 1, 3, 2, 5)).reshape(all_count)

    doc_row = lax.dynamic_index_in_dim(documents, sequence, 0, keepdims=False)
    places = gathered_order(jnp.arange(all_count, dtype=jnp.int32))
    docs = gathered_order(doc_row)
    starts = jnp.sum((doc_row[None, :] < docs[:, None]).astype(jnp.int32), axis=-1)
    cosine, sine_part = rope_tables(places - starts, HEAD)
    signs = jnp.where(jnp.arange(HEAD) < HEAD // 2, -1.0, 1.0).astype(f32)

    def by_half(v):
        return v.reshape(2, 2, half_all // 2, v.shape[-1])

    table = by_half(jnp.concatenate([cosine[:, 0], sine_part[:, 0] * signs], axis=-1))
    row_places = by_half(jnp.stack([places, starts], axis=-1))
    key_places = jnp.transpose(places.reshape(2, 2, half_all // 2), (1, 0, 2))
    key_places = key_places.reshape(2, 1, half_all)
    head_gain = jnp.stack([gq, gk])

    projected = jnp.einsum("rd,dh->rh", whole, wqkv, preferred_element_type=f32)
    queries, keys_proj = projected[:, :heads_width], projected[:, heads_width : 2 * heads_width]
    sums = group_sum(
        jnp.stack([jnp.sum(queries * queries, axis=-1), jnp.sum(keys_proj * keys_proj, axis=-1)])
    )
    inverse = lax.rsqrt(sums / width + EPS).T

    def rows_shape(size, kind):
        return jax.ShapeDtypeStruct((2, 2, half_all // 2, size), kind)

    mixed_low, attended, log_total, query_low, key_low, value_low = pl.pallas_call(
        lambda *refs: attend_kernel(heads, *refs),
        out_shape=[
            rows_shape(heads_width, bf16),
            rows_shape(heads_width, f32),
            rows_shape(heads, f32),
        ]
        + [rows_shape(heads_width, bf16)] * 3,
        compiler_params=pltpu.CompilerParams(vmem_limit_bytes=VMEM_BYTES),
        cost_estimate=pl.CostEstimate(flops=0, bytes_accessed=0, transcendentals=0),
        name="attend",
    )(by_half(projected), by_half(inverse), table, row_places, key_places, head_gain)
    mixed_low = mixed_low.reshape(all_count, heads_width)

    branch = scatter(*times(mixed_low, wo, "rh,hd->rd"))
    attn_inv = rms_scale(branch)
    hidden = rows_in.astype(f32) + branch * attn_inv * attention_gain
    hidden_whole = gather(hidden.astype(bf16))
    gate_value = jnp.einsum("rd,df->rf", hidden_whole, wg, preferred_element_type=f32)
    gate_value = gate_value.astype(bf16)
    up_value = jnp.einsum("rd,df->rf", hidden_whole, wu, preferred_element_type=f32)
    gate_wide = gate_value.astype(f32)
    act_low = (gate_wide * jax.nn.sigmoid(gate_wide) * up_value).astype(bf16)
    up_value = up_value.astype(bf16)
    down_value = scatter(*times(act_low, wd, "rf,fd->rd"))
    feed_inv = rms_scale(down_value)
    down_low = norm_back(down_value, feed_inv, feed_gain, grad_top).astype(bf16)
    down_whole = gather(down_low)

    down_part = grads(down_whole, act_low, ids_all)
    down_whole, down_part = both(down_whole, down_part)
    down_sum = whole_sum(down_part)
    tile = gate_value.shape[1] // 2
    unit_tile = pl.BlockSpec((all_count, tile), lambda j, z: (0, j))
    rows_full = pl.BlockSpec((all_count, width), lambda j, z: (0, 0))
    rows_part = pl.BlockSpec((half_all // 2, width), lambda j, z: (0, 0))
    rows_half = pl.BlockSpec((half_all, width), lambda j, z: (0, 0))
    weight_tile = pl.BlockSpec((width, tile), lambda j, z: (0, 2 * z[0] + j))
    gate_low, up_low, *hidden_part = pl.pallas_call(
        feed_back_kernel,
        grid_spec=pltpu.PrefetchScalarGridSpec(
            num_scalar_prefetch=1,
            grid=(2,),
            in_specs=[
                rows_full,
                weight_tile,
                weight_tile,
                pl.BlockSpec((tile, width), lambda j, z: (2 * z[0] + j, 0)),
                unit_tile,
                unit_tile,
            ],
            out_specs=[unit_tile, unit_tile, rows_half, rows_part, rows_part],
            scratch_shapes=[pltpu.VMEM((all_count, width), f32)],
        ),
        out_shape=[
            jax.ShapeDtypeStruct(gate_value.shape, bf16),
            jax.ShapeDtypeStruct(gate_value.shape, bf16),
            jax.ShapeDtypeStruct((half_all, width), bf16),
        ]
        + [jax.ShapeDtypeStruct((half_all // 2, width), bf16)] * 2,
        compiler_params=pltpu.CompilerParams(vmem_limit_bytes=VMEM_BYTES),
        cost_estimate=pl.CostEstimate(flops=0, bytes_accessed=0, transcendentals=0),
        name="feed_back",
    )(
        zl[None], down_whole, gate_weight, up_weight, down_weight, gate_value,
        up_value,
    )
    gate_part = grads(hidden_whole, gate_low, ids_all)
    hidden_grad, late_hidden = scatter_direct(*hidden_part, late=hidden)
    layer_out = from_sequence(late_hidden + down_value * feed_inv * feed_gain)
    hidden_grad, layer_out = both(grad_top + hidden_grad, layer_out)
    hidden_grad, gate_part = both(hidden_grad, gate_part)
    gate_sum = whole_sum(gate_part)

    branch_low = norm_back(branch, attn_inv, attention_gain, hidden_grad).astype(bf16)
    branch_whole, late_up = gather_direct(branch_low, up_low)
    up_part = grads(hidden_whole, late_up, ids_all)
    branch_whole, up_part = both(branch_whole, up_part)
    up_sum = whole_sum(up_part)
    mixed_grad = pl.pallas_call(
        mixed_back_kernel,
        grid_spec=pltpu.PrefetchScalarGridSpec(
            num_scalar_prefetch=1,
            grid=(2,),
            in_specs=[
                pl.BlockSpec((half_all, width), lambda i, z: (i, 0)),
                pl.BlockSpec((heads_width, width), lambda i, z: (z[0], 0)),
            ],
            out_specs=pl.BlockSpec((half_all, heads_width), lambda i, z: (i, 0)),
        ),
        out_shape=jax.ShapeDtypeStruct((all_count, heads_width), bf16),
        compiler_params=pltpu.CompilerParams(vmem_limit_bytes=VMEM_BYTES),
        cost_estimate=pl.CostEstimate(flops=0, bytes_accessed=0, transcendentals=0),
        name="mixed_back",
    )(zl[None], branch_whole, output_weight)

    yq, yk, value_grad_low = pl.pallas_call(
        lambda *refs: attend_back_kernel(heads, *refs),
        out_shape=[rows_shape(heads_width, f32)] * 2 + [rows_shape(heads_width, bf16)],
        scratch_shapes=[pltpu.VMEM((half_all, HEAD), f32)] * 2,
        compiler_params=pltpu.CompilerParams(vmem_limit_bytes=VMEM_BYTES),
        cost_estimate=pl.CostEstimate(flops=0, bytes_accessed=0, transcendentals=0),
        name="attend_back",
    )(
        query_low, key_low, value_low, attended, log_total, by_half(mixed_grad), table,
        row_places, key_places,
    )
    yq, yk, value_grad_low = (
        v.reshape(all_count, heads_width) for v in (yq, yk, value_grad_low)
    )
    query_inv, key_inv = inverse[:, 0:1], inverse[:, 1:2]
    dots = jnp.stack([jnp.sum(yq * gq * queries, axis=-1), jnp.sum(yk * gk * keys_proj, axis=-1)])
    head_gains = jnp.stack(
        [jnp.sum(yq * queries * query_inv, axis=0), jnp.sum(yk * keys_proj * key_inv, axis=0)]
    )
    head_gains = lax.dynamic_update_slice(
        jnp.zeros((2, width), f32), head_gains, (0, (2 * t + zl) * heads_width)
    )
    row_gains = jnp.stack(
        [
            jnp.sum(hidden_grad * branch * attn_inv, axis=0),
            jnp.sum(grad_top * down_value * feed_inv, axis=0),
        ]
    )
    gains = jnp.concatenate([head_gains, row_gains]).reshape(-1, all_count)
    yq, late_mixed = both(yq, mixed_low)
    out_far = grads(branch_whole, late_mixed, ids_x)
    dots, gains = group_sum(dots, gains)
    dots, out_far, down_sum = both(dots, out_far, down_sum)
    out_far = swap(out_far, "x")
    down_mine, down_other = cross_zl(down_sum)
    dots = dots.T
    gains = gains.reshape(4, width)
    gains = gains + swap(gains, "x")
    query_grad_low = (
        query_inv * gq * yq - queries * query_inv**3 * (dots[:, 0:1] / width)
    ).astype(bf16)
    key_grad_low = (
        key_inv * gk * yk - keys_proj * key_inv**3 * (dots[:, 1:2] / width)
    ).astype(bf16)
    projected_grad = jnp.concatenate([query_grad_low, key_grad_low, value_grad_low], axis=1)
    input_part = times(projected_grad, wqkv, "rh,dh->rd")
    input_own, late_grad, out_far, gains, down_other = both(
        input_part[0], projected_grad, out_far, gains, down_other
    )
    in_far = swap(grads(whole, late_grad, ids_x), "x")
    gains = gains + swap(gains, "zh")
    out_sent = grads(branch_whole, late_mixed, ids_zh, (out_far, 2))
    down_term = joined(down_mine, down_other, True)
    input_sum, _ = scatter_direct(input_own, *input_part[1:])
    out_sent = swap(out_sent, "zh")
    input_sum, in_far, out_sent, gate_sum, down_term = both(
        input_sum, in_far, out_sent, gate_sum, down_term
    )
    in_sent = grads(whole, projected_grad, ids_zh, (in_far, 2))
    input_sum, in_sent, gate_sum, out_sent = both(input_sum, in_sent, gate_sum, out_sent)
    in_sent = swap(in_sent, "zh")
    gate_mine, gate_other = cross_zl(gate_sum)
    out_mine, out_other = finish(branch_whole, mixed_low, out_far, out_sent)
    gate_term = joined(gate_mine, gate_other)
    out_term = joined(out_mine, out_other, True)
    input_grad = from_sequence_direct(hidden_grad + input_sum)
    up_sum, input_grad, out_term, gate_term = both(up_sum, input_grad, out_term, gate_term)
    up_pair = cross_zl(up_sum)
    in_mine, in_other = finish(whole, projected_grad, in_far, in_sent)
    gains = lax.dynamic_slice_in_dim(gains, s * block, block, 1)
    up_term = joined(*up_pair)
    query_term, key_term, value_term = (
        joined(
            in_mine[:, k * heads_width : (k + 1) * heads_width],
            in_other[:, k * heads_width : (k + 1) * heads_width],
        )
        for k in range(3)
    )
    return (
        layer_out,
        input_grad,
        query_term,
        key_term,
        value_term,
        out_term,
        gate_term,
        up_term,
        down_term,
        gains[0],
        gains[1],
        gains[2],
        gains[3],
    )


def solution(mesh):
    rows, columns, inner = ("seq", "tp"), ("tp",), ("seq",)
    step = local
    if mesh.shape["seq"] == 8 and mesh.shape["tp"] == 4:
        mesh = Mesh(mesh.devices.reshape(2, 2, 2, 2, 2), BITS)
        rows, columns, inner = BITS, BITS[3:], BITS[:3]
        step = grouped
    return jax.shard_map(
        step,
        mesh=mesh,
        in_specs=(
            P(rows, None, None),
            P(),
            P(None, columns),
            P(None, columns),
            P(None, columns),
            P(columns, None),
            P(columns),
            P(columns),
            P(),
            P(None, columns),
            P(None, columns),
            P(columns, None),
            P(),
            P(rows, None, None),
        ),
        out_specs=(
            P(rows, None, None),
            P(rows, None, None),
            P(inner, columns),
            P(inner, columns),
            P(inner, columns),
            P(columns, inner),
            P(inner, columns),
            P(inner, columns),
            P(columns, inner),
            P(inner),
            P(inner),
            P(inner),
            P(inner),
        ),
        check_vma=False,
    )
```

```python
import jax
import jax.numpy as jnp
from jax import lax
from jax.experimental.layout import Layout, with_layout_constraint
from jax.experimental import pallas as pl
from jax.experimental.pallas import tpu as pltpu
from jax.sharding import Mesh
from jax.sharding import PartitionSpec as P

HEAD = 128


EPS = 1e-06
THETA = 500000.0
NEGATIVE = -1e30


def rope_tables(positions, head_size):
    half_size = head_size // 2
    rates = jnp.exp(-jnp.log(THETA) * (2.0 * jnp.arange(half_size, dtype=jnp.float32) / head_size))
    angles = positions.astype(jnp.float32)[..., None] * rates
    cosine = jnp.cos(angles)
    sine_part = jnp.sin(angles)
    return (
        jnp.concatenate([cosine, cosine], axis=-1)[..., None, :],
        jnp.concatenate([sine_part, sine_part], axis=-1)[..., None, :],
    )


def rotate(tensor, cosine, sine_part):
    half_size = tensor.shape[-1] // 2
    turned = jnp.concatenate([-tensor[..., half_size:], tensor[..., :half_size]], axis=-1)
    return tensor * cosine + turned * sine_part


def unrotate(grad_in, cosine, sine_part):
    half_size = grad_in.shape[-1] // 2
    scaled = grad_in * sine_part
    return grad_in * cosine + jnp.concatenate(
        [scaled[..., half_size:], -scaled[..., :half_size]], axis=-1
    )


def rms_scale(tensor):
    return lax.rsqrt(jnp.mean(tensor * tensor, axis=-1, keepdims=True) + EPS)


def norm_back(tensor, inverse, gain, grad_in):
    weighted = grad_in * gain
    return inverse * weighted - tensor * inverse**3 * jnp.mean(
        weighted * tensor, axis=-1, keepdims=True
    )


def cycle_values(key_low, value_low):
    return (
        lax.all_gather(jnp.transpose(key_low, (1, 0, 2)), "seq", axis=1, tiled=True),
        lax.all_gather(jnp.transpose(value_low, (1, 0, 2)), "seq", axis=1, tiled=True),
    )


def allowed_mask(query_docs, key_docs, query_first, key_first):
    query_places = query_first + jnp.arange(query_docs.shape[0], dtype=jnp.int32)
    key_places = key_first + jnp.arange(key_docs.shape[0], dtype=jnp.int32)
    return (query_docs[:, None] == key_docs[None, :]) & (
        key_places[None, :] <= query_places[:, None]
    )


def local(
    inputs,
    documents,
    query_weight,
    key_weight,
    value_weight,
    output_weight,
    query_gain,
    key_gain,
    attention_gain,
    gate_weight,
    up_weight,
    down_weight,
    feed_gain,
    cotangent,
):
    row_count, seq_count, model_width = inputs.shape
    heads_width = query_weight.shape[1]
    local_heads = heads_width // HEAD
    score_scale = HEAD ** (-0.5)
    seq_index = lax.axis_index("seq")
    tp_index = lax.axis_index("tp")
    total_length = documents.shape[1]
    f32 = jnp.float32
    bf16 = jnp.bfloat16
    whole = lax.all_gather(inputs, "tp", axis=0, tiled=True)
    here_length = whole.shape[0]
    queries = jnp.einsum("tsd,dh->tsh", whole, query_weight, preferred_element_type=f32)
    keys_proj = jnp.einsum("tsd,dh->tsh", whole, key_weight, preferred_element_type=f32)
    values_proj = jnp.einsum("tsd,dh->tsh", whole, value_weight, preferred_element_type=f32)
    query_sq, key_sq = lax.psum(
        (jnp.sum(queries * queries, axis=-1), jnp.sum(keys_proj * keys_proj, axis=-1)), "tp"
    )
    query_inv = lax.rsqrt(query_sq / model_width + EPS)[..., None]
    key_inv = lax.rsqrt(key_sq / model_width + EPS)[..., None]
    first_row = seq_index * here_length
    own_docs = lax.dynamic_slice_in_dim(documents, first_row, here_length, 1)
    starts = jnp.sum((documents[:, None, :] < own_docs[:, :, None]).astype(jnp.int32), axis=-1)
    positions = (first_row + jnp.arange(here_length, dtype=jnp.int32))[:, None] - starts.T
    cosine, sine_part = rope_tables(positions, HEAD)

    def heads_of(tensor):
        return tensor.reshape(here_length, seq_count, local_heads, HEAD)

    query_low = rotate(heads_of(queries * query_inv * query_gain), cosine, sine_part).astype(bf16)
    key_low = rotate(heads_of(keys_proj * key_inv * key_gain), cosine, sine_part).astype(bf16)
    key_low = key_low.reshape(here_length, seq_count, heads_width)
    value_low = values_proj.astype(bf16)
    key_cycle, value_cycle = cycle_values(key_low, value_low)
    query_seq = jnp.transpose(query_low, (1, 0, 2, 3))

    def keys_in_reach(key_part, value_part):
        return (
            key_part.reshape(total_length, local_heads, HEAD),
            value_part.reshape(total_length, local_heads, HEAD),
        )

    def scores_of(query_part, key_heads, query_docs, key_docs, first_query, first_key):
        scores = (
            jnp.einsum("qhd,khd->hqk", query_part, key_heads, preferred_element_type=f32)
            * score_scale
        )
        return jnp.where(
            allowed_mask(query_docs, key_docs, first_query, first_key)[None], scores, NEGATIVE
        )

    def attend(pieces):
        query_part, key_part, value_part, own_part, doc_row = pieces
        key_heads, value_heads = keys_in_reach(key_part, value_part)
        scores = scores_of(query_part, key_heads, own_part, doc_row, first_row, 0)
        top_score = jnp.max(scores, axis=-1, keepdims=True)
        spread = jnp.exp(scores - top_score)
        total_sum = jnp.sum(spread, axis=-1, keepdims=True)
        weights = (spread / total_sum).astype(bf16)
        mixed_part = jnp.einsum("hqk,khd->qhd", weights, value_heads, preferred_element_type=f32)
        return (mixed_part, (top_score + jnp.log(total_sum))[..., 0])

    attended, log_total = lax.map(attend, (query_seq, key_cycle, value_cycle, own_docs, documents))
    mixed_low = (
        jnp.transpose(attended, (1, 0, 2, 3))
        .reshape(here_length, seq_count, heads_width)
        .astype(bf16)
    )
    part = mixed_low
    branch = lax.psum_scatter(
        jnp.einsum("tsh,hd->tsd", part, output_weight, preferred_element_type=f32).astype(
            jnp.bfloat16
        ),
        "tp",
        scatter_dimension=0,
        tiled=True,
    ).astype(jnp.float32)
    attn_inv = rms_scale(branch)
    hidden = inputs.astype(f32) + branch * attn_inv * attention_gain
    hidden_whole = lax.all_gather(hidden.astype(bf16), "tp", axis=0, tiled=True)
    gate_value = jnp.einsum("tsd,df->tsf", hidden_whole, gate_weight, preferred_element_type=f32)
    up_value = jnp.einsum("tsd,df->tsf", hidden_whole, up_weight, preferred_element_type=f32)
    sigmoid_value = jax.nn.sigmoid(gate_value)
    act_low = (gate_value * sigmoid_value * up_value).astype(bf16)
    part = act_low
    down_value = lax.psum_scatter(
        jnp.einsum("tsf,fd->tsd", part, down_weight, preferred_element_type=f32).astype(
            jnp.bfloat16
        ),
        "tp",
        scatter_dimension=0,
        tiled=True,
    ).astype(jnp.float32)
    feed_inv = rms_scale(down_value)
    layer_out = hidden + down_value * feed_inv * feed_gain
    grad_top = cotangent.astype(f32)
    feed_gain_term = jnp.sum(grad_top * down_value * feed_inv, axis=(0, 1))
    down_grad_low = norm_back(down_value, feed_inv, feed_gain, grad_top).astype(bf16)
    down_whole = lax.all_gather(down_grad_low, "tp", axis=0, tiled=True)
    act_grad = jnp.einsum("tsd,fd->tsf", down_whole, down_weight, preferred_element_type=f32)
    down_term = jnp.einsum("tsd,tsf->df", down_whole, act_low, preferred_element_type=f32)
    up_grad_low = (act_grad * gate_value * sigmoid_value).astype(bf16)
    gate_grad_low = (
        act_grad * up_value * sigmoid_value * (1.0 + gate_value * (1.0 - sigmoid_value))
    ).astype(bf16)
    gate_term = jnp.einsum("tsd,tsf->df", hidden_whole, gate_grad_low, preferred_element_type=f32)
    up_term = jnp.einsum("tsd,tsf->df", hidden_whole, up_grad_low, preferred_element_type=f32)
    hidden_grad = grad_top + lax.psum_scatter(
        (
            jnp.einsum("tsf,df->tsd", gate_grad_low, gate_weight, preferred_element_type=f32)
            + jnp.einsum("tsf,df->tsd", up_grad_low, up_weight, preferred_element_type=f32)
        ).astype(jnp.bfloat16),
        "tp",
        scatter_dimension=0,
        tiled=True,
    ).astype(jnp.float32)
    attention_gain_term = jnp.sum(hidden_grad * branch * attn_inv, axis=(0, 1))
    branch_grad_low = norm_back(branch, attn_inv, attention_gain, hidden_grad).astype(bf16)
    branch_whole = lax.all_gather(branch_grad_low, "tp", axis=0, tiled=True)
    out_term = jnp.einsum("tsd,tsh->dh", branch_whole, mixed_low, preferred_element_type=f32)
    mixed_grad_low = jnp.einsum(
        "tsd,hd->tsh", branch_whole, output_weight, preferred_element_type=f32
    ).astype(bf16)
    grad_seq = jnp.transpose(
        mixed_grad_low.reshape(here_length, seq_count, local_heads, HEAD), (1, 0, 2, 3)
    )
    delta_own = jnp.transpose(jnp.sum(grad_seq.astype(f32) * attended, axis=-1), (0, 2, 1))
    key_cycle, value_cycle = cycle_values(key_low, value_low)

    def query_back(pieces):
        query_part, key_part, value_part, own_part, doc_row, grad_part, log_part, delta_part = (
            pieces
        )
        key_heads, value_heads = keys_in_reach(key_part, value_part)
        scores = scores_of(query_part, key_heads, own_part, doc_row, first_row, 0)
        weights = jnp.exp(scores - log_part[..., None])
        weight_grad = jnp.einsum("qhd,khd->hqk", grad_part, value_heads, preferred_element_type=f32)
        score_grad = (weights * (weight_grad - delta_part[:, :, None]) * score_scale).astype(bf16)
        query_grad = jnp.einsum("hqk,khd->qhd", score_grad, key_heads, preferred_element_type=f32)
        key_grad = jnp.einsum("hqk,qhd->khd", score_grad, query_part, preferred_element_type=f32)
        value_grad = jnp.einsum(
            "hqk,qhd->khd", weights.astype(bf16), grad_part, preferred_element_type=f32
        )
        return (
            query_grad,
            key_grad.reshape(total_length, heads_width),
            value_grad.reshape(total_length, heads_width),
        )

    query_grads, key_full, value_full = lax.map(
        query_back,
        (query_seq, key_cycle, value_cycle, own_docs, documents, grad_seq, log_total, delta_own),
    )
    key_own, value_own = (
        lax.psum_scatter(
            key_full.astype(jnp.bfloat16), "seq", scatter_dimension=1, tiled=True
        ).astype(jnp.float32),
        lax.psum_scatter(
            value_full.astype(jnp.bfloat16), "seq", scatter_dimension=1, tiled=True
        ).astype(jnp.float32),
    )
    value_grad_low = jnp.transpose(value_own, (1, 0, 2)).astype(bf16)
    query_rot = unrotate(jnp.transpose(query_grads, (1, 0, 2, 3)), cosine, sine_part)
    query_rot = query_rot.reshape(here_length, seq_count, heads_width)
    key_rot = unrotate(heads_of(jnp.transpose(key_own, (1, 0, 2))), cosine, sine_part)
    key_rot = key_rot.reshape(here_length, seq_count, heads_width)
    query_gain_term = jnp.sum(query_rot * queries * query_inv, axis=(0, 1))
    key_gain_term = jnp.sum(key_rot * keys_proj * key_inv, axis=(0, 1))

    def placed(term):
        return lax.dynamic_update_slice(
            jnp.zeros((model_width,), f32), term, (tp_index * heads_width,)
        )

    query_dot, key_dot, query_gain_sum, key_gain_sum, attention_gain_sum, feed_gain_sum = (
        lax.psum(
            jnp.sum(query_rot * query_gain * queries, axis=-1).astype(jnp.bfloat16), "tp"
        ).astype(jnp.float32),
        lax.psum(
            jnp.sum(key_rot * key_gain * keys_proj, axis=-1).astype(jnp.bfloat16), "tp"
        ).astype(jnp.float32),
        lax.psum(placed(query_gain_term).astype(jnp.bfloat16), "tp").astype(jnp.float32),
        lax.psum(placed(key_gain_term).astype(jnp.bfloat16), "tp").astype(jnp.float32),
        lax.psum(attention_gain_term.astype(jnp.bfloat16), "tp").astype(jnp.float32),
        lax.psum(feed_gain_term.astype(jnp.bfloat16), "tp").astype(jnp.float32),
    )
    query_grad_low = (
        query_inv * query_gain * query_rot
        - queries * query_inv**3 * (query_dot / model_width)[..., None]
    ).astype(bf16)
    key_grad_low = (
        key_inv * key_gain * key_rot - keys_proj * key_inv**3 * (key_dot / model_width)[..., None]
    ).astype(bf16)
    query_term = jnp.einsum("tsd,tsh->dh", whole, query_grad_low, preferred_element_type=f32)
    key_term = jnp.einsum("tsd,tsh->dh", whole, key_grad_low, preferred_element_type=f32)
    value_term = jnp.einsum("tsd,tsh->dh", whole, value_grad_low, preferred_element_type=f32)
    query_part = query_grad_low
    key_part = key_grad_low
    value_part = value_grad_low
    input_grad = hidden_grad + lax.psum_scatter(
        (
            jnp.einsum("tsh,dh->tsd", query_part, query_weight, preferred_element_type=f32)
            + jnp.einsum("tsh,dh->tsd", key_part, key_weight, preferred_element_type=f32)
            + jnp.einsum("tsh,dh->tsd", value_part, value_weight, preferred_element_type=f32)
        ).astype(jnp.bfloat16),
        "tp",
        scatter_dimension=0,
        tiled=True,
    ).astype(jnp.float32)
    summed = (
        lax.psum_scatter(
            query_term.astype(jnp.bfloat16), "seq", scatter_dimension=0, tiled=True
        ).astype(jnp.float32),
        lax.psum_scatter(
            key_term.astype(jnp.bfloat16), "seq", scatter_dimension=0, tiled=True
        ).astype(jnp.float32),
        lax.psum_scatter(
            value_term.astype(jnp.bfloat16), "seq", scatter_dimension=0, tiled=True
        ).astype(jnp.float32),
        lax.psum_scatter(
            out_term.astype(jnp.bfloat16), "seq", scatter_dimension=0, tiled=True
        ).astype(jnp.float32),
        lax.psum_scatter(
            gate_term.astype(jnp.bfloat16), "seq", scatter_dimension=0, tiled=True
        ).astype(jnp.float32),
        lax.psum_scatter(
            up_term.astype(jnp.bfloat16), "seq", scatter_dimension=0, tiled=True
        ).astype(jnp.float32),
        lax.psum_scatter(
            down_term.astype(jnp.bfloat16), "seq", scatter_dimension=0, tiled=True
        ).astype(jnp.float32),
        lax.psum_scatter(
            query_gain_sum.astype(jnp.bfloat16), "seq", scatter_dimension=0, tiled=True
        ).astype(jnp.float32),
        lax.psum_scatter(
            key_gain_sum.astype(jnp.bfloat16), "seq", scatter_dimension=0, tiled=True
        ).astype(jnp.float32),
        lax.psum_scatter(
            attention_gain_sum.astype(jnp.bfloat16), "seq", scatter_dimension=0, tiled=True
        ).astype(jnp.float32),
        lax.psum_scatter(
            feed_gain_sum.astype(jnp.bfloat16), "seq", scatter_dimension=0, tiled=True
        ).astype(jnp.float32),
    )
    return (
        layer_out,
        input_grad,
        summed[0],
        summed[1],
        summed[2],
        summed[3].T,
        summed[4],
        summed[5],
        summed[6].T,
        summed[7],
        summed[8],
        summed[9],
        summed[10],
    )


VMEM_BYTES = 56 * 2**20
BITS = ("zh", "zl", "x", "y", "c")


def turn(v, table):
    return v * table[:, :HEAD] + pltpu.roll(v, HEAD // 2, 1) * table[:, HEAD:]


def turn_back(g, table):
    return g * table[:, :HEAD] - pltpu.roll(g, HEAD // 2, 1) * table[:, HEAD:]


def dot_last(left, right):
    return lax.dot_general(
        left, right, (((1,), (1,)), ((), ())), preferred_element_type=jnp.float32
    )


def dot_first(left, right):
    return lax.dot_general(
        left, right, (((0,), (0,)), ((), ())), preferred_element_type=jnp.float32
    )


def attend_kernel(
    heads, proj_ref, inv_ref, table_ref, place_ref, kp_ref, gain_ref,
    mixed_ref, o_ref, lse_ref, q_ref, k_ref, v_ref,
):
    bf16 = jnp.bfloat16
    width = heads * HEAD
    scale = HEAD ** (-0.5)

    def rows(ref, h, cols=slice(None)):
        v = ref[:, h, :, cols]
        return v.reshape(v.shape[0] * v.shape[1], v.shape[2])

    def put(ref, h, cols, v):
        ref[:, h, :, cols] = v.reshape(ref.shape[0], ref.shape[2], v.shape[1])

    for h in range(2):
        table = rows(table_ref, h)
        inv = rows(inv_ref, h)
        place = rows(place_ref, h)
        masks = [
            (kp_ref[e] >= place[:, 1:2]) & (kp_ref[e] <= place[:, 0:1]) for e in range(h + 1)
        ]
        for head in range(heads):
            cols = slice(head * HEAD, (head + 1) * HEAD)
            key_cols = slice(width + head * HEAD, width + (head + 1) * HEAD)
            value_cols = slice(2 * width + head * HEAD, 2 * width + (head + 1) * HEAD)
            query = turn(rows(proj_ref, h, cols) * inv[:, 0:1] * gain_ref[0:1, cols], table)
            key = turn(rows(proj_ref, h, key_cols) * inv[:, 1:2] * gain_ref[1:2, cols], table)
            query = query.astype(bf16)
            put(q_ref, h, cols, query)
            put(k_ref, h, cols, key.astype(bf16))
            put(v_ref, h, cols, rows(proj_ref, h, value_cols).astype(bf16))
            scores = [
                jnp.where(masks[e], dot_last(query, rows(k_ref, e, cols)), NEGATIVE)
                for e in range(h + 1)
            ]
            top = scores[0].max(axis=-1, keepdims=True)
            if h:
                top = jnp.maximum(top, scores[1].max(axis=-1, keepdims=True))
            spread = [jnp.exp((v - top) * scale) for v in scores]
            total = sum(v.sum(axis=-1, keepdims=True) for v in spread)
            mixed = sum(
                jnp.dot(p.astype(bf16), rows(v_ref, e, cols), preferred_element_type=jnp.float32)
                for e, p in enumerate(spread)
            )
            mixed = mixed / total
            put(o_ref, h, cols, mixed)
            put(mixed_ref, h, cols, mixed.astype(bf16))
            put(lse_ref, h, slice(head, head + 1), top * scale + jnp.log(total))


def attend_back_kernel(
    heads, q_ref, k_ref, v_ref, o_ref, lse_ref, g_ref, table_ref, place_ref, kp_ref,
    yq_ref, yk_ref, dv_ref, acc_k, acc_v,
):
    f32 = jnp.float32
    bf16 = jnp.bfloat16
    scale = HEAD ** (-0.5)

    def rows(ref, h, cols=slice(None)):
        v = ref[:, h, :, cols]
        return v.reshape(v.shape[0] * v.shape[1], v.shape[2])

    def put(ref, h, cols, v):
        ref[:, h, :, cols] = v.reshape(ref.shape[0], ref.shape[2], v.shape[1])

    for head in range(heads):
        cols = slice(head * HEAD, (head + 1) * HEAD)
        for h in range(2):
            query = rows(q_ref, h, cols)
            grad = rows(g_ref, h, cols)
            delta = jnp.sum(grad.astype(f32) * rows(o_ref, h, cols), axis=-1, keepdims=True)
            place = rows(place_ref, h)
            lse = rows(lse_ref, h, slice(head, head + 1))
            query_grad = 0.0
            for e in range(h + 1):
                key, value, kp = rows(k_ref, e, cols), rows(v_ref, e, cols), kp_ref[e]
                allowed = (kp >= place[:, 1:2]) & (kp <= place[:, 0:1])
                scores = jnp.where(allowed, dot_last(query, key) * scale, NEGATIVE)
                weights = jnp.exp(scores - lse)
                score_grad = (weights * (dot_last(grad, value) - delta) * scale).astype(bf16)
                query_grad += jnp.dot(score_grad, key, preferred_element_type=f32)
                key_part = dot_first(score_grad, query)
                value_part = dot_first(weights.astype(bf16), grad)
                if h > e:
                    key_part += acc_k[...]
                    value_part += acc_v[...]
                elif h == 0:
                    acc_k[...] = key_part
                    acc_v[...] = value_part
                    continue
                put(yk_ref, e, cols, turn_back(key_part, rows(table_ref, e)))
                put(dv_ref, e, cols, value_part.astype(bf16))
            put(yq_ref, h, cols, turn_back(query_grad, rows(table_ref, h)))


def feed_back_kernel(
    zl_ref, rows_ref, wg_ref, wu_ref, wd_ref, gate_ref, up_ref,
    gg_ref, ug_ref, own_ref, other0_ref, other1_ref, acc_ref,
):
    f32 = jnp.float32
    bf16 = jnp.bfloat16
    step = pl.program_id(0)
    half = rows_ref.shape[0] // 2
    for part in (1, 0):
        at = slice(part * half, (part + 1) * half)
        act_grad = dot_last(rows_ref[at, :], wd_ref[...])
        gate, up = gate_ref[at, :].astype(f32), up_ref[at, :].astype(f32)
        sig = jax.nn.sigmoid(gate)
        up_low = (act_grad * gate * sig).astype(bf16)
        gate_low = (act_grad * up * sig * (1.0 + gate * (1.0 - sig))).astype(bf16)
        ug_ref[at, :] = up_low
        gg_ref[at, :] = gate_low
        value = dot_last(gate_low, wg_ref[...]) + dot_last(up_low, wu_ref[...])

        @pl.when(step == 0)
        def _():
            acc_ref[at, :] = value

        @pl.when(step == 1)
        def _():
            total = (acc_ref[at, :] + value).astype(bf16)
            if part:
                other0_ref[...] = total[: half // 2]
                other1_ref[...] = total[half // 2 :]
            else:
                own_ref[...] = total


def mixed_back_kernel(zl_ref, rows_ref, weight_ref, out_ref):
    out_ref[...] = dot_last(rows_ref[...], weight_ref[...]).astype(out_ref.dtype)


def grads_kernel(count, ids_ref, features_ref, right_ref, *refs):
    value = dot_first(features_ref[...], right_ref[...])
    for ref in refs[:count]:
        value = value + ref[...].astype(jnp.float32)
    refs[count][...] = value.astype(refs[count].dtype)


def grads(features, right, ids, *terms, kind=jnp.bfloat16):
    tokens, units = right.shape
    block = features.shape[1] // 8
    count = ids.shape[0]
    return pl.pallas_call(
        lambda *refs: grads_kernel(len(terms), *refs),
        grid_spec=pltpu.PrefetchScalarGridSpec(
            num_scalar_prefetch=1,
            grid=(count,),
            in_specs=[
                pl.BlockSpec((tokens, block), lambda i, ids: (0, ids[i])),
                pl.BlockSpec((tokens, units), lambda i, ids: (0, 0)),
            ]
            + [
                pl.BlockSpec((block, units), lambda i, ids, first=first: (first + i, 0))
                for _, first in terms
            ],
            out_specs=pl.BlockSpec((block, units), lambda i, ids: (i, 0)),
        ),
        out_shape=jax.ShapeDtypeStruct((count * block, units), kind),
        compiler_params=pltpu.CompilerParams(vmem_limit_bytes=VMEM_BYTES),
        cost_estimate=pl.CostEstimate(flops=0, bytes_accessed=0, transcendentals=0),
        name="grads",
    )(ids, features, right, *(term for term, _ in terms))


def assemble_kernel(moves, *refs):
    pieces, out_ref, sems = refs[:-2], refs[-2], refs[-1]
    copies = [
        pltpu.make_async_copy(
            pieces[piece].at[pl.ds(first, rows)], out_ref.at[pl.ds(to, rows)], sems.at[index]
        )
        for index, (piece, first, rows, to) in enumerate(moves)
    ]
    for copy in copies:
        copy.start()
    for copy in copies:
        copy.wait()


def assemble(pieces, moves):
    rows = sum(move[2] for move in moves)
    return pl.pallas_call(
        lambda *refs: assemble_kernel(moves, *refs),
        in_specs=[pl.BlockSpec(memory_space=pltpu.VMEM)] * len(pieces),
        out_specs=pl.BlockSpec(memory_space=pl.ANY),
        out_shape=jax.ShapeDtypeStruct((rows, pieces[0].shape[1]), pieces[0].dtype),
        scratch_shapes=[pltpu.SemaphoreType.DMA((len(moves),))],
        compiler_params=pltpu.CompilerParams(vmem_limit_bytes=VMEM_BYTES),
        cost_estimate=pl.CostEstimate(flops=0, bytes_accessed=0, transcendentals=0),
        name="assemble",
    )(*pieces)


def both(*values):
    return lax.optimization_barrier(values)


def grouped(
    inputs,
    documents,
    query_weight,
    key_weight,
    value_weight,
    output_weight,
    query_gain,
    key_gain,
    attention_gain,
    gate_weight,
    up_weight,
    down_weight,
    feed_gain,
    cotangent,
):
    f32 = jnp.float32
    bf16 = jnp.bfloat16
    row_count, seq_count, width = inputs.shape
    half_count = 2 * row_count
    half_all = 8 * half_count
    all_count = 2 * half_all
    block = width // 8
    zh, zl, x, y, c = (lax.axis_index(name) for name in BITS)
    s = 4 * zh + 2 * zl + x
    t = 2 * y + c
    sequence = 2 * zh + x

    def swap(v, name):
        return lax.ppermute(v, name, ((0, 1), (1, 0)))

    def to_sequence(v):
        v = lax.all_to_all(jnp.transpose(v, (1, 0, 2)), ("zh", "x"), 0, 0, tiled=True)
        return v.reshape(2 * half_count, width)

    def from_sequence(v):
        v = v.astype(bf16).reshape(4, row_count, width)
        v = lax.all_to_all(v, ("zh", "x"), 0, 0, tiled=True)
        return jnp.transpose(v, (1, 0, 2)).astype(f32)

    def gather(a, late=None):
        a0, b0 = a[:half_count], a[half_count:]
        a1, b2 = both(swap(a0, "y"), swap(b0, "zl"))
        a01, b02 = jnp.concatenate([a0, a1]), jnp.concatenate([b0, b2])
        if late is None:
            a01, b02 = both(a01, b02)
        else:
            a01, b02, late = both(a01, b02, late)
        a01_c, b02_c = swap(a01, "c"), swap(b02, "c")
        a23, b13 = both(swap(a01, "zl"), swap(b02, "y"))
        a23_c, b13_c = both(swap(a23, "c"), swap(b13, "c"))
        k = half_count
        v = assemble(
            (a01, a23, b02, b13, a01_c, a23_c, b02_c, b13_c),
            [
                move
                for dc in range(2)
                for move in (
                    (4 * dc, 0, 2 * k, 8 * dc * k),
                    (4 * dc + 1, 0, 2 * k, (8 * dc + 2) * k),
                    (4 * dc + 2, 0, k, (8 * dc + 4) * k),
                    (4 * dc + 3, 0, k, (8 * dc + 5) * k),
                    (4 * dc + 2, k, k, (8 * dc + 6) * k),
                    (4 * dc + 3, k, k, (8 * dc + 7) * k),
                )
            ],
        )
        return v if late is None else (v, late)

    def swap_zy(v):
        return lax.ppermute(v, ("zl", "y"), ((0, 3), (3, 0), (1, 2), (2, 1)))

    def gather_direct(a, late):
        others = both(swap(a, "y"), swap(a, "zl"), swap_zy(a), swap(a, "c"), late)
        own, late = (a, *others[:3]), others[4]
        crossed = both(others[3], *(swap(v, "c") for v in own[1:]))
        k = half_count
        v = assemble(
            (*own, *crossed),
            [
                (4 * dc + chip, h * k, k, (8 * dc + 4 * h + chip) * k)
                for dc in range(2)
                for h in range(2)
                for chip in range(4)
            ],
        )
        return v, late

    def scatter_direct(own, *other):
        other = both(*(swap(v, "c") for v in other))
        p = [
            (v.astype(f32) + w.astype(f32)).astype(bf16)
            for v, w in zip(own.reshape(2, 4 * half_count, width), other)
        ]
        k = half_count
        mine, *sent = (
            jnp.concatenate([v[chip * k : (chip + 1) * k] for v in p]) for chip in range(4)
        )
        sent = both(swap(sent[0], "y"), swap(sent[1], "zl"), swap_zy(sent[2]))
        return sum(v.astype(f32) for v in (mine, *sent))

    def scatter(own, *other):
        a, b = own.reshape(2, 4 * half_count, width)
        a_c, b_c = both(*(swap(v, "c") for v in other))
        a = (a.astype(f32) + a_c.astype(f32)).astype(bf16).reshape(2, 2 * half_count, width)
        b = (b.astype(f32) + b_c.astype(f32)).astype(bf16).reshape(2, 2, half_count, width)
        a1, b1 = both(swap(a[1], "zl"), swap(b[:, 1], "y"))
        a = (a[0].astype(f32) + a1.astype(f32)).astype(bf16)
        b = (b[:, 0].astype(f32) + b1.astype(f32)).astype(bf16)
        a1, b1 = both(swap(a[half_count:], "y"), swap(b[1], "zl"))
        a = a[:half_count].astype(f32) + a1.astype(f32)
        b = b[0].astype(f32) + b1.astype(f32)
        return jnp.concatenate([a, b])

    def times(rows, weight, dims):
        parts = [
            jnp.einsum(dims, v, weight, preferred_element_type=f32).astype(bf16)
            for v in (rows[half_all:], rows[:half_all])
        ]
        return parts[1], *jnp.split(parts[0], 2)

    def group_sum(v, extra=None):
        for name, axis in (("c", 1), ("y", 4), ("zl", 3)):
            if extra is None:
                other = swap(v, name)
            else:
                other = swap(jnp.concatenate([v, extra]), name)
                other, other_extra = other[: v.shape[0]], other[v.shape[0] :]
                extra = extra + other_extra
            other = jnp.flip(other.reshape(-1, 2, 2, 2, 2, half_count), axis)
            v = v + other.reshape(-1, all_count)
        return v if extra is None else (v, extra)

    ids_all = (2 * zl + jnp.array([0, 0, 1, 1, 4, 4, 5, 5], jnp.int32)) ^ jnp.array(
        [0, 2] * 4, jnp.int32
    )
    ids_x, ids_zh, ids_zl = (
        s ^ jnp.array(bits, jnp.int32) for bits in ((1, 3, 5, 7), (4, 6), (0, 2))
    )

    def whole_sum(v):
        return lax.psum_scatter(v, ("zh", "x"), scatter_dimension=0, tiled=True)

    def cross_zl(kept):
        return kept[:block], swap(kept[block:], "zl")

    def finish(features, right, far, sent):
        return cross_zl(grads(features, right, ids_zl, (far, 0), (sent, 0)))

    def joined(mine, other, transposed=False):
        mine, other = mine.astype(f32), other.astype(f32)
        if transposed:
            mine, other = mine.T, other.T
        axis = 0 if transposed else 1
        return jnp.where(
            zl == 0,
            jnp.concatenate([mine, other], axis=axis),
            jnp.concatenate([other, mine], axis=axis),
        )

    def zl_half(w, axis):
        size = w.shape[axis] // 2
        return lax.dynamic_slice_in_dim(w, zl * size, size, axis)

    rows_in = to_sequence(inputs)
    weights = (
        query_weight, key_weight, value_weight, output_weight, gate_weight, up_weight, down_weight
    )
    whole, (cotangent, weights) = gather(rows_in, (cotangent, weights))
    (
        query_weight, key_weight, value_weight, output_weight, gate_weight, up_weight, down_weight
    ) = weights
    wqkv = jnp.concatenate([zl_half(w, 1) for w in (query_weight, key_weight, value_weight)], 1)
    wo = zl_half(output_weight, 0)
    wg, wu, wd = zl_half(gate_weight, 1), zl_half(up_weight, 1), zl_half(down_weight, 0)
    gq, gk = zl_half(query_gain, 0), zl_half(key_gain, 0)
    heads_width = wo.shape[0]
    heads = heads_width // HEAD

    whole, grad_top = both(whole, to_sequence(cotangent))
    grad_top = grad_top.astype(f32)

    def gathered_order(v):
        v = v.reshape(2, 2, 2, 2, 2, row_count)
        for axis, bit in ((1, zl), (3, y), (4, c)):
            v = jnp.where(bit == 1, jnp.flip(v, axis), v)
        return jnp.transpose(v, (4, 0, 1, 3, 2, 5)).reshape(all_count)

    doc_row = lax.dynamic_index_in_dim(documents, sequence, 0, keepdims=False)
    places = gathered_order(jnp.arange(all_count, dtype=jnp.int32))
    docs = gathered_order(doc_row)
    starts = jnp.sum((doc_row[None, :] < docs[:, None]).astype(jnp.int32), axis=-1)
    cosine, sine_part = rope_tables(places - starts, HEAD)
    signs = jnp.where(jnp.arange(HEAD) < HEAD // 2, -1.0, 1.0).astype(f32)

    def by_half(v):
        return v.reshape(2, 2, half_all // 2, v.shape[-1])

    table = by_half(jnp.concatenate([cosine[:, 0], sine_part[:, 0] * signs], axis=-1))
    row_places = by_half(jnp.stack([places, starts], axis=-1))
    key_places = jnp.transpose(places.reshape(2, 2, half_all // 2), (1, 0, 2))
    key_places = key_places.reshape(2, 1, half_all)
    head_gain = jnp.stack([gq, gk])

    projected = jnp.einsum("rd,dh->rh", whole, wqkv, preferred_element_type=f32)
    queries, keys_proj = projected[:, :heads_width], projected[:, heads_width : 2 * heads_width]
    sums = group_sum(
        jnp.stack([jnp.sum(queries * queries, axis=-1), jnp.sum(keys_proj * keys_proj, axis=-1)])
    )
    inverse = lax.rsqrt(sums / width + EPS).T

    def rows_shape(size, kind):
        return jax.ShapeDtypeStruct((2, 2, half_all // 2, size), kind)

    mixed_low, attended, log_total, query_low, key_low, value_low = pl.pallas_call(
        lambda *refs: attend_kernel(heads, *refs),
        out_shape=[
            rows_shape(heads_width, bf16),
            rows_shape(heads_width, f32),
            rows_shape(heads, f32),
        ]
        + [rows_shape(heads_width, bf16)] * 3,
        compiler_params=pltpu.CompilerParams(vmem_limit_bytes=VMEM_BYTES),
        cost_estimate=pl.CostEstimate(flops=0, bytes_accessed=0, transcendentals=0),
        name="attend",
    )(by_half(projected), by_half(inverse), table, row_places, key_places, head_gain)
    mixed_low = mixed_low.reshape(all_count, heads_width)

    branch = scatter(*times(mixed_low, wo, "rh,hd->rd"))
    attn_inv = rms_scale(branch)
    hidden = rows_in.astype(f32) + branch * attn_inv * attention_gain
    hidden_whole = gather(hidden.astype(bf16))
    gate_value = jnp.einsum("rd,df->rf", hidden_whole, wg, preferred_element_type=f32)
    gate_value = gate_value.astype(bf16)
    up_value = jnp.einsum("rd,df->rf", hidden_whole, wu, preferred_element_type=f32)
    gate_wide = gate_value.astype(f32)
    act_low = (gate_wide * jax.nn.sigmoid(gate_wide) * up_value).astype(bf16)
    up_value = up_value.astype(bf16)
    down_value = scatter(*times(act_low, wd, "rf,fd->rd"))
    feed_inv = rms_scale(down_value)
    down_low = norm_back(down_value, feed_inv, feed_gain, grad_top).astype(bf16)
    down_whole, late_hidden = gather(down_low, hidden)
    layer_out = from_sequence(late_hidden + down_value * feed_inv * feed_gain)
    down_whole, layer_out = both(down_whole, layer_out)

    down_part = grads(down_whole, act_low, ids_all)
    down_whole, down_part = both(down_whole, down_part)
    down_sum = whole_sum(down_part)
    tile = gate_value.shape[1] // 2
    unit_tile = pl.BlockSpec((all_count, tile), lambda j, z: (0, j))
    rows_full = pl.BlockSpec((all_count, width), lambda j, z: (0, 0))
    rows_part = pl.BlockSpec((half_all // 2, width), lambda j, z: (0, 0))
    rows_half = pl.BlockSpec((half_all, width), lambda j, z: (0, 0))
    weight_tile = pl.BlockSpec((width, tile), lambda j, z: (0, 2 * z[0] + j))
    gate_low, up_low, *hidden_part = pl.pallas_call(
        feed_back_kernel,
        grid_spec=pltpu.PrefetchScalarGridSpec(
            num_scalar_prefetch=1,
            grid=(2,),
            in_specs=[
                rows_full,
                weight_tile,
                weight_tile,
                pl.BlockSpec((tile, width), lambda j, z: (2 * z[0] + j, 0)),
                unit_tile,
                unit_tile,
            ],
            out_specs=[unit_tile, unit_tile, rows_half, rows_part, rows_part],
            scratch_shapes=[pltpu.VMEM((all_count, width), f32)],
        ),
        out_shape=[
            jax.ShapeDtypeStruct(gate_value.shape, bf16),
            jax.ShapeDtypeStruct(gate_value.shape, bf16),
            jax.ShapeDtypeStruct((half_all, width), bf16),
        ]
        + [jax.ShapeDtypeStruct((half_all // 2, width), bf16)] * 2,
        compiler_params=pltpu.CompilerParams(vmem_limit_bytes=VMEM_BYTES),
        cost_estimate=pl.CostEstimate(flops=0, bytes_accessed=0, transcendentals=0),
        name="feed_back",
    )(
        zl[None], down_whole, gate_weight, up_weight, down_weight, gate_value,
        up_value,
    )
    gate_part = grads(hidden_whole, gate_low, ids_all)
    hidden_grad = grad_top + scatter_direct(*hidden_part)
    hidden_grad, gate_part = both(hidden_grad, gate_part)
    gate_sum = whole_sum(gate_part)

    branch_low = norm_back(branch, attn_inv, attention_gain, hidden_grad).astype(bf16)
    branch_whole, late_up = gather_direct(branch_low, up_low)
    up_part = grads(hidden_whole, late_up, ids_all)
    branch_whole, up_part = both(branch_whole, up_part)
    up_sum = whole_sum(up_part)
    mixed_grad = pl.pallas_call(
        mixed_back_kernel,
        grid_spec=pltpu.PrefetchScalarGridSpec(
            num_scalar_prefetch=1,
            grid=(2,),
            in_specs=[
                pl.BlockSpec((half_all, width), lambda i, z: (i, 0)),
                pl.BlockSpec((heads_width, width), lambda i, z: (z[0], 0)),
            ],
            out_specs=pl.BlockSpec((half_all, heads_width), lambda i, z: (i, 0)),
        ),
        out_shape=jax.ShapeDtypeStruct((all_count, heads_width), bf16),
        compiler_params=pltpu.CompilerParams(vmem_limit_bytes=VMEM_BYTES),
        cost_estimate=pl.CostEstimate(flops=0, bytes_accessed=0, transcendentals=0),
        name="mixed_back",
    )(zl[None], branch_whole, output_weight)

    yq, yk, value_grad_low = pl.pallas_call(
        lambda *refs: attend_back_kernel(heads, *refs),
        out_shape=[rows_shape(heads_width, f32)] * 2 + [rows_shape(heads_width, bf16)],
        scratch_shapes=[pltpu.VMEM((half_all, HEAD), f32)] * 2,
        compiler_params=pltpu.CompilerParams(vmem_limit_bytes=VMEM_BYTES),
        cost_estimate=pl.CostEstimate(flops=0, bytes_accessed=0, transcendentals=0),
        name="attend_back",
    )(
        query_low, key_low, value_low, attended, log_total, by_half(mixed_grad), table,
        row_places, key_places,
    )
    yq, yk, value_grad_low = (
        v.reshape(all_count, heads_width) for v in (yq, yk, value_grad_low)
    )
    query_inv, key_inv = inverse[:, 0:1], inverse[:, 1:2]
    dots = jnp.stack([jnp.sum(yq * gq * queries, axis=-1), jnp.sum(yk * gk * keys_proj, axis=-1)])
    head_gains = jnp.stack(
        [jnp.sum(yq * queries * query_inv, axis=0), jnp.sum(yk * keys_proj * key_inv, axis=0)]
    )
    head_gains = lax.dynamic_update_slice(
        jnp.zeros((2, width), f32), head_gains, (0, (2 * t + zl) * heads_width)
    )
    row_gains = jnp.stack(
        [
            jnp.sum(hidden_grad * branch * attn_inv, axis=0),
            jnp.sum(grad_top * down_value * feed_inv, axis=0),
        ]
    )
    gains = jnp.concatenate([head_gains, row_gains]).reshape(-1, all_count)
    yq, late_mixed = both(yq, mixed_low)
    out_far = grads(branch_whole, late_mixed, ids_x)
    dots, gains = group_sum(dots, gains)
    dots, out_far, down_sum = both(dots, out_far, down_sum)
    out_far = swap(out_far, "x")
    down_mine, down_other = cross_zl(down_sum)
    dots = dots.T
    gains = gains.reshape(4, width)
    gains = gains + swap(gains, "x")
    query_grad_low = (
        query_inv * gq * yq - queries * query_inv**3 * (dots[:, 0:1] / width)
    ).astype(bf16)
    key_grad_low = (
        key_inv * gk * yk - keys_proj * key_inv**3 * (dots[:, 1:2] / width)
    ).astype(bf16)
    projected_grad = jnp.concatenate([query_grad_low, key_grad_low, value_grad_low], axis=1)
    input_part = times(projected_grad, wqkv, "rh,dh->rd")
    input_own, late_grad, out_far, gains, down_other = both(
        input_part[0], projected_grad, out_far, gains, down_other
    )
    in_far = swap(grads(whole, late_grad, ids_x), "x")
    gains = gains + swap(gains, "zh")
    out_sent = grads(branch_whole, late_mixed, ids_zh, (out_far, 2))
    down_term = joined(down_mine, down_other, True)
    input_sum = scatter_direct(input_own, *input_part[1:])
    input_sum, in_far, out_sent, gate_sum, down_term = both(
        input_sum, in_far, out_sent, gate_sum, down_term
    )
    in_sent = grads(whole, projected_grad, ids_zh, (in_far, 2))
    input_sum, in_sent, out_sent, gate_sum = both(input_sum, in_sent, out_sent, gate_sum)
    in_sent, out_sent = swap(in_sent, "zh"), swap(out_sent, "zh")
    gate_mine, gate_other = cross_zl(gate_sum)
    gate_term = joined(gate_mine, gate_other)
    in_sent, gate_term, input_sum = both(in_sent, gate_term, input_sum)
    in_mine, in_other = finish(whole, projected_grad, in_far, in_sent)
    out_sent, in_mine = both(out_sent, in_mine)
    out_mine, out_other = finish(branch_whole, mixed_low, out_far, out_sent)
    out_term = joined(out_mine, out_other, True)
    up_pair = cross_zl(up_sum)
    input_grad = from_sequence(hidden_grad + input_sum)
    gains = lax.dynamic_slice_in_dim(gains, s * block, block, 1)
    up_term = joined(*up_pair)
    query_term, key_term, value_term = (
        joined(
            in_mine[:, k * heads_width : (k + 1) * heads_width],
            in_other[:, k * heads_width : (k + 1) * heads_width],
        )
        for k in range(3)
    )
    return (
        layer_out,
        input_grad,
        query_term,
        key_term,
        value_term,
        out_term,
        gate_term,
        up_term,
        down_term,
        gains[0],
        gains[1],
        gains[2],
        gains[3],
    )


def solution(mesh):
    rows, columns, inner = ("seq", "tp"), ("tp",), ("seq",)
    step = local
    if mesh.shape["seq"] == 8 and mesh.shape["tp"] == 4:
        mesh = Mesh(mesh.devices.reshape(2, 2, 2, 2, 2), BITS)
        rows, columns, inner = BITS, BITS[3:], BITS[:3]
        step = grouped
    return jax.shard_map(
        step,
        mesh=mesh,
        in_specs=(
            P(rows, None, None),
            P(),
            P(None, columns),
            P(None, columns),
            P(None, columns),
            P(columns, None),
            P(columns),
            P(columns),
            P(),
            P(None, columns),
            P(None, columns),
            P(columns, None),
            P(),
            P(rows, None, None),
        ),
        out_specs=(
            P(rows, None, None),
            P(rows, None, None),
            P(inner, columns),
            P(inner, columns),
            P(inner, columns),
            P(columns, inner),
            P(inner, columns),
            P(inner, columns),
            P(columns, inner),
            P(inner),
            P(inner),
            P(inner),
            P(inner),
        ),
        check_vma=False,
    )
```
